256 devices in a mesh: pass: 32 (over x, z), head: 8 (over y, core).
Axes of the slice: x: 4, y: 4, z: 8, core: 2. Of those that a mesh axis runs over, the one named last changes fastest.
Arguments:
- queries: bfloat16 [12288, 8192], P('pass', 'head'), may hold values from -4.5 to 4.5
- own_kv: bfloat16 [12288, 8, 256], P('pass', 'head'), may hold values from -4.5 to 4.5
- passage_cache: bfloat16 [512, 512, 8, 256], P('pass', None, 'head'), may hold values from -4.5 to 4.5
- out_weight: bfloat16 [8192, 4096], P('head', 'pass'), may hold values from -3.5 to 3.5
- lists: int32 [96, 8], replicated, may hold values from 0 to 511, as said below
- passage_slot: int32 [512], replicated, may hold values from 0 to 511, as said below
- question_slot: int32 [96], replicated, may hold values from 0 to 95, as said below
Outputs:
- attended: bfloat16 [12288, 4096], P('pass', 'head')
The draws below stay inside these ranges and needn't reach their ends.
Inputs may be any that keep to these rules, and one draw needn't show every extreme that they name: Each question lists 8 different passages. The listed passages of the 3 questions at slots d * 3 to d * 3 + 2 are all different, and at most 1 of them have their cache rows in one aligned block of 16 rows; some block holds exactly 1 of them. `passage_slot`: A permutation. `question_slot`: A permutation.
All inputs are finite; a program needn't handle non-finite values.
Results may differ from the reference program's by a relative error of at most 0.014.
Values may be sent and summed in bfloat16 or wider, within the bound.
No kernel may reach another device: no remote copies, remote signals or barrier semaphores. Data moves between devices by JAX's collectives and lax.ppermute only.
A program may use at most 128 MiB of HBM per device.

```python
import jax
import jax.numpy as jnp
from jax import lax

H = 64
KVH = 8
HD = 128
DOUT = 4096
LQ = 128
PLEN = 512
TOPP = 8
Q_DEV = 3
PASS_DEV = 16
NQ = 96
NPASS = 512
TOKENS = 12288
GROUP_ROWS = 1024


def request_layout(key):
    shard_count = NPASS // PASS_DEV
    device_count = NQ // Q_DEV
    entries = Q_DEV * TOPP
    question_slot = jax.random.permutation(jax.random.fold_in(key, 101), NQ).astype(jnp.int32)
    passage_slot = jax.random.permutation(jax.random.fold_in(key, 102), NPASS).astype(jnp.int32)

    def shuffle(subkey):
        return jax.random.permutation(subkey, shard_count).astype(jnp.int32)
    orders = jax.vmap(shuffle)(jax.random.split(jax.random.fold_in(key, 103), device_count))
    first = jax.random.randint(jax.random.fold_in(key, 104), (device_count, shard_count), 0, PASS_DEV)
    second = jax.random.randint(jax.random.fold_in(key, 105), (device_count, shard_count), 0, PASS_DEV)
    base = jnp.minimum(first, second).astype(jnp.int32)
    position = jnp.arange(entries, dtype=jnp.int32) % shard_count
    layer = jnp.arange(entries, dtype=jnp.int32) // shard_count
    shard = orders[:, position]
    local_row = (base[:, position] + layer[None, :]) % PASS_DEV
    cache_row = shard * PASS_DEV + local_row
    passage_of_row = jnp.zeros((NPASS,), jnp.int32).at[passage_slot].set(jnp.arange(NPASS, dtype=jnp.int32))
    by_slot = passage_of_row[cache_row].reshape(NQ, TOPP)
    lists = by_slot[question_slot]
    return (question_slot, passage_slot, lists)


def draw_lists(key, part):
    return request_layout(key)[2]


def draw_passage_slot(key, part):
    return request_layout(key)[1]


def draw_question_slot(key, part):
    return request_layout(key)[0]


def draw_queries(key, part):
    shape = (TOKENS, H, HD)
    values = jnp.clip(jax.random.normal(key, shape, jnp.float32), -4.5, 4.5)
    return values.reshape(TOKENS, H * HD).astype(jnp.bfloat16)


def draw_own_kv(key, part):
    shape = (TOKENS, KVH, 2 * HD)
    values = jnp.clip(jax.random.normal(key, shape, jnp.float32), -4.5, 4.5)
    return values.astype(jnp.bfloat16)


def draw_passage_cache(key, part):
    shape = (NPASS, PLEN, KVH, 2 * HD)
    values = jnp.clip(jax.random.normal(key, shape, jnp.float32), -4.5, 4.5)
    return values.astype(jnp.bfloat16)


def level_of(key, dims, cuts, least, top_value):
    def one(dim, blocks):
        draws = jax.random.uniform(jax.random.fold_in(jax.random.fold_in(key, 6), dim), (blocks,), jnp.float32, least / len(cuts), top_value / len(cuts))
        return jnp.repeat(jnp.exp(draws), dims[dim] // blocks).reshape((-1,) + (1,) * (len(dims) - dim - 1))

    factor_of = one(*cuts[0])
    for cut in cuts[1:]:
        factor_of = factor_of * one(*cut)
    return factor_of


def normal_values(own_key, shape, deviation, limit, pieces=(), kind=jnp.bfloat16):
    level = level_of(own_key, shape, pieces, -0.22, 0.18) if pieces else 1.0
    values = jax.random.normal(own_key, shape, jnp.float32) * deviation * level
    return jnp.minimum(jnp.maximum(values, -limit), limit).astype(kind)


def setup_inputs(seed: int = 0) -> dict:
    streams_of = jax.random.split(jax.random.key(seed), 8)
    queries = draw_queries(jax.random.fold_in(streams_of[7], 71), 0)
    own_kv = draw_own_kv(jax.random.fold_in(streams_of[7], 71), 0)
    passage_cache = draw_passage_cache(jax.random.fold_in(streams_of[7], 71), 0)
    out_weight = normal_values(streams_of[3], (H * HD, DOUT), (20.0 / (H * HD) ** 0.5), 3.5, ((0, 8), (1, 32)))
    lists = draw_lists(jax.random.fold_in(streams_of[7], 71), 0)
    passage_slot = draw_passage_slot(jax.random.fold_in(streams_of[7], 71), 0)
    question_slot = draw_question_slot(jax.random.fold_in(streams_of[7], 71), 0)
    return dict(queries=queries, own_kv=own_kv, passage_cache=passage_cache, out_weight=out_weight, lists=lists, passage_slot=passage_slot, question_slot=question_slot)


def attend(query, keys, values, causal):
    heads = query.shape[1]
    rows = query.shape[0] * heads
    flat = query.reshape(rows, query.shape[2])
    scores = lax.dot_general(flat, keys, (((1,), (1,)), ((), ())), preferred_element_type=jnp.float32)
    scores = scores * (query.shape[2] ** -0.5)
    if causal:
        token = lax.broadcasted_iota(jnp.int32, scores.shape, 0) // heads
        column = lax.broadcasted_iota(jnp.int32, scores.shape, 1)
        scores = jnp.where(column <= token, scores, -1e30)
    row_max = jnp.max(scores, axis=1, keepdims=True)
    weights = jnp.exp(scores - row_max)
    row_total = jnp.sum(weights, axis=1, keepdims=True)
    mixed = jnp.dot(weights.astype(jnp.bfloat16), values, preferred_element_type=jnp.float32) / row_total
    level = row_max + jnp.log(row_total)
    return mixed.astype(jnp.bfloat16).reshape(query.shape[0], heads * query.shape[2]), level.reshape(query.shape[0], heads)


def combine(outputs, levels, heads):
    stacked = jnp.stack(outputs)
    level_stack = jnp.stack(levels)
    peak = jnp.max(level_stack, axis=0, keepdims=True)
    overall = peak + jnp.log(jnp.sum(jnp.exp(level_stack - peak), axis=0, keepdims=True))
    share = jnp.exp(level_stack - overall)
    shaped = stacked.reshape(stacked.shape[0], stacked.shape[1], heads, -1).astype(jnp.float32)
    context = jnp.sum(shaped * share[..., None], axis=0)
    return context.reshape(stacked.shape[1], -1).astype(jnp.bfloat16)


def reference(queries, own_kv, passage_cache, out_weight, lists, passage_slot, question_slot):
    group = H // KVH
    slots = jnp.arange(NQ, dtype=jnp.int32)
    holder = (question_slot[None, :] == slots[:, None]).astype(jnp.int32)
    chosen = jnp.sum(holder[:, :, None] * lists[None, :, :], axis=1).astype(jnp.int32)
    catalog = jnp.arange(NPASS, dtype=jnp.int32)
    picked = (chosen[:, :, None] == catalog[None, None, :]).astype(jnp.int32)
    cache_rows = jnp.sum(picked * passage_slot[None, None, :], axis=2).astype(jnp.int32)
    blocks = queries.reshape(NQ, LQ, KVH, group, HD)
    own_blocks = own_kv.reshape(NQ, LQ, KVH, 2 * HD)

    def per_slot(item):
        query_block, own_block, row_list = item
        head_contexts = []
        for head in range(KVH):
            outputs, levels = [], []
            for index in range(TOPP):
                cache_block = lax.dynamic_index_in_dim(passage_cache, row_list[index], 0, keepdims=False)[:, head]
                mixed, level = attend(query_block[:, head], cache_block[:, :HD], cache_block[:, HD:], False)
                outputs.append(mixed)
                levels.append(level)
            mixed, level = attend(query_block[:, head], own_block[:, head, :HD], own_block[:, head, HD:], True)
            outputs.append(mixed)
            levels.append(level)
            head_contexts.append(combine(outputs, levels, group))
        return jnp.concatenate(head_contexts, axis=1)

    context = lax.map(per_slot, (blocks, own_blocks, cache_rows)).reshape(TOKENS, H * HD)
    result = jnp.zeros((TOKENS, DOUT), jnp.float32)
    for index in range(H * HD // GROUP_ROWS):
        lower = index * GROUP_ROWS
        piece = jnp.dot(context[:, lower:lower + GROUP_ROWS], out_weight[lower:lower + GROUP_ROWS], preferred_element_type=jnp.float32)
        rounded = lax.optimization_barrier(piece.astype(jnp.bfloat16))
        result = result + rounded.astype(jnp.float32)
    return result.astype(jnp.bfloat16)
```

```python
import functools
import math

import jax
import jax.numpy as jnp
from jax import lax
from jax.experimental import pallas as pl
from jax.experimental.pallas import tpu as pltpu
from jax.sharding import Mesh, PartitionSpec as P

HD = 128
GROUP = 8
LQ = 128
PLEN = 512
TOPP = 8
NX, NZ, NY, NC = 4, 8, 4, 2
ROWS = GROUP * LQ
SCALE = math.log2(math.e) / math.sqrt(HD)
NEG = -1e30
WIDTH = 512
VMEM_LIMIT = 50 << 20

FAR_SENT = (3, -3, 4)
FAR_HERE = (2, -2)
NEAR = (0, 1, -1)


def request_tables(lists, passage_slot, question_slot, per_device, pass_dev):
    slot_count = question_slot.shape[0]
    slot_ids = jnp.arange(slot_count, dtype=jnp.int32)
    holder = (question_slot[None, :] == slot_ids[:, None]).astype(jnp.int32)
    chosen = jnp.sum(holder[:, :, None] * lists[None, :, :], axis=1)
    catalog = jnp.arange(passage_slot.shape[0], dtype=jnp.int32)
    picked = (chosen[:, :, None] == catalog[None, None, :]).astype(jnp.int32)
    cache_rows = jnp.sum(picked * passage_slot[None, None, :], axis=2)
    cache_rows = cache_rows.reshape(slot_count // per_device, per_device * TOPP)
    return cache_rows // pass_dev, cache_rows % pass_dev


def row_copy(rows_ref, cache_ref, out_ref):
    out_ref[...] = cache_ref[...]


def take_rows(cache, rows):
    n = rows.shape[0]
    block = (1,) + cache.shape[1:]
    return pl.pallas_call(
        row_copy,
        out_shape=jax.ShapeDtypeStruct((n,) + cache.shape[1:], cache.dtype),
        grid_spec=pltpu.PrefetchScalarGridSpec(
            num_scalar_prefetch=1,
            grid=(n,),
            in_specs=[pl.BlockSpec(block, lambda i, rows_ref: (rows_ref[i], 0, 0))],
            out_specs=pl.BlockSpec(block, lambda i, rows_ref: (i, 0, 0)),
        ),
        name="take_rows",
    )(rows, cache)


def absorb(keys, values_t, query_ref, group, cols, acc, top, total, causal=False):
    which, lane = group
    scores = lax.dot_general(
        keys,
        query_ref[lane, cols, :],
        (((1,), (1,)), ((), ())),
        preferred_element_type=jnp.float32,
    )
    if causal:
        key = lax.broadcasted_iota(jnp.int32, scores.shape, 0)
        token = lax.broadcasted_iota(jnp.int32, scores.shape, 1)
        scores = jnp.where(key <= token, scores, NEG)
    old = top[which, :, cols]
    new = jnp.maximum(old, jnp.max(scores, axis=0, keepdims=True))
    weights = jnp.exp2((scores - new) * SCALE)
    keep = jnp.exp2((old - new) * SCALE)
    top[which, :, cols] = new
    total[which, :, cols] = total[which, :, cols] * keep + jnp.sum(weights, axis=0, keepdims=True)
    acc[which, :, cols] = acc[which, :, cols] * keep + jnp.dot(
        values_t, weights.astype(jnp.bfloat16), preferred_element_type=jnp.float32
    )


def start(acc, top, total):
    acc[...] = jnp.zeros_like(acc)
    top[...] = jnp.full_like(top, NEG)
    total[...] = jnp.zeros_like(total)


def absorb_all(tag_ref, first, kv_ref, count, pick, query_ref, base, acc, top, total):
    def step(i, carry):
        tag = tag_ref[first + i]

        @pl.when(tag >= 0)
        def _():
            index = pick(i)
            keys = kv_ref[(*index, slice(None), slice(0, HD))]
            values_t = kv_ref[(*index, slice(None), slice(HD, 2 * HD))].T
            for part in range(ROWS // WIDTH):
                cols = pl.ds(part * WIDTH, WIDTH)
                absorb(keys, values_t, query_ref, (base + tag, tag), cols, acc, top, total)

        return carry

    lax.fori_loop(0, count, step, 0)


def finish(out_ref, level_ref, base, acc, top, total):
    for j in range(out_ref.shape[0]):
        sums = jnp.maximum(total[base + j], 1e-30)
        out_ref[j] = (acc[base + j] / sums).astype(jnp.bfloat16)
        level_ref[j] = top[base + j] * SCALE + jnp.log2(sums)


def far_kernel(tags, q_up, q_down, here, up3, down3, up4, down4, o_up, l_up, o_down, l_down, *state):
    start(*state)
    n = q_up.shape[0]
    absorb_all(tags, 0, here, 4, lambda i: (i, 0), q_up, 0, *state)
    absorb_all(tags, 4, here, 4, lambda i: (i, 1), q_down, n, *state)
    absorb_all(tags, 8, up3, 4, lambda i: (i,), q_up, 0, *state)
    absorb_all(tags, 12, down3, 4, lambda i: (i,), q_down, n, *state)
    absorb_all(tags, 16, up4, 2, lambda i: (i,), q_up, 0, *state)
    absorb_all(tags, 18, down4, 2, lambda i: (i,), q_down, n, *state)
    finish(o_up, l_up, 0, *state)
    finish(o_down, l_down, n, *state)


def near_kernel(
    tags, q_own, q_up, q_down, here, own, o_own, l_own, o_up, l_up, o_down, l_down, *state
):
    start(*state)
    n = q_own.shape[0]
    for j in range(n):
        rows = slice(j * LQ, (j + 1) * LQ)
        keys = own[rows, 0:HD]
        values_t = own[rows, HD : 2 * HD].T
        for part in range(GROUP):
            cols = pl.ds(part * LQ, LQ)
            absorb(keys, values_t, q_own, (j, j), cols, *state, causal=True)
    absorb_all(tags, 0, here, 4, lambda i: (i, 0), q_own, 0, *state)
    absorb_all(tags, 4, here, 4, lambda i: (i, 1), q_up, n, *state)
    absorb_all(tags, 8, here, 4, lambda i: (i, 2), q_down, 2 * n, *state)
    finish(o_own, l_own, 0, *state)
    finish(o_up, l_up, n, *state)
    finish(o_down, l_down, 2 * n, *state)


def attention(kernel, name, tags, arrays, n, sides, items):
    out = []
    for _ in range(sides):
        out.append(jax.ShapeDtypeStruct((n, HD, ROWS), jnp.bfloat16))
        out.append(jax.ShapeDtypeStruct((n, 1, ROWS), jnp.float32))
    vmem = pl.BlockSpec(memory_space=pltpu.VMEM)
    return pl.pallas_call(
        kernel,
        out_shape=tuple(out),
        in_specs=[pl.BlockSpec(memory_space=pltpu.SMEM)] + [vmem] * len(arrays),
        out_specs=(vmem,) * len(out),
        scratch_shapes=[
            pltpu.VMEM((sides * n, HD, ROWS), jnp.float32),
            pltpu.VMEM((sides * n, 1, ROWS), jnp.float32),
            pltpu.VMEM((sides * n, 1, ROWS), jnp.float32),
        ],
        compiler_params=pltpu.CompilerParams(vmem_limit_bytes=VMEM_LIMIT),
        cost_estimate=pl.CostEstimate(
            flops=items * 4 * ROWS * PLEN * HD * 2,
            bytes_accessed=items * PLEN * 2 * HD * 2,
            transcendentals=items * ROWS * PLEN,
        ),
        name=name,
    )(tags, *arrays)


def merge(pairs):
    level = pairs[0][1]
    for _, other in pairs[1:]:
        level = jnp.maximum(level, other)
    shares = [jnp.exp2(l - level) for _, l in pairs]
    whole = functools.reduce(jnp.add, shares)
    mixed = functools.reduce(
        jnp.add, [o.astype(jnp.float32) * s for (o, _), s in zip(pairs, shares)]
    )
    return mixed / whole, level + jnp.log2(whole)


def hop_kernel(o_a, l_a, o_b, l_b, o_c, l_c, o_d, l_d, o_up, l_up, o_down, l_down):
    for j in range(o_a.shape[0]):
        mixed, level = merge([(o_a[j], l_a[j]), (o_b[j], l_b[j])])
        o_up[j] = mixed.astype(jnp.bfloat16)
        l_up[j] = level
        mixed, level = merge([(o_c[j], l_c[j]), (o_d[j], l_d[j])])
        o_down[j] = mixed.astype(jnp.bfloat16)
        l_down[j] = level


def last_kernel(o_a, l_a, o_b, l_b, o_c, l_c, out_ref):
    for j in range(o_a.shape[0]):
        mixed, _ = merge([(o_a[j], l_a[j]), (o_b[j], l_b[j]), (o_c[j], l_c[j])])
        for part in range(GROUP):
            cols = slice(part * LQ, (part + 1) * LQ)
            out_ref[j * LQ : (j + 1) * LQ, part * HD : (part + 1) * HD] = mixed[:, cols].T.astype(
                jnp.bfloat16
            )


def in_vmem(kernel, name, out, *arrays):
    vmem = pl.BlockSpec(memory_space=pltpu.VMEM)
    return pl.pallas_call(
        kernel,
        out_shape=out,
        in_specs=[vmem] * len(arrays),
        out_specs=jax.tree.map(lambda _: vmem, out),
        compiler_params=pltpu.CompilerParams(vmem_limit_bytes=VMEM_LIMIT),
        name=name,
    )(*arrays)


def project_kernel(context_ref, weight_ref, out_ref):
    weight = jnp.concatenate([weight_ref[0], weight_ref[1]], axis=1)
    out_ref[...] = jnp.dot(
        context_ref[...], weight, preferred_element_type=jnp.float32
    ).astype(jnp.bfloat16)


def project(context, weight):
    blocks, rows, cols = weight.shape
    return pl.pallas_call(
        project_kernel,
        out_shape=jax.ShapeDtypeStruct((context.shape[0], blocks * cols), jnp.bfloat16),
        grid=(blocks // 2,),
        in_specs=[
            pl.BlockSpec(context.shape, lambda i: (0, 0)),
            pl.BlockSpec((2, rows, cols), lambda i: (i, 0, 0)),
        ],
        out_specs=pl.BlockSpec((context.shape[0], 2 * cols), lambda i: (0, i)),
        compiler_params=pltpu.CompilerParams(vmem_limit_bytes=VMEM_LIMIT),
        name="project",
    )(context, weight)


def along(array, axis, size, shift):
    pairs = [(i, (i + shift) % size) for i in range(size)]
    return jax.tree.map(lambda a: lax.ppermute(a, axis, pairs), array)


def over_x(items):
    return lax.all_to_all(items, "x", split_axis=0, concat_axis=0, tiled=True)


def body(queries, own_kv, passage_cache, out_weight, lists, passage_slot, question_slot):
    x, z = lax.axis_index("x"), lax.axis_index("z")
    per_device = queries.shape[0] // LQ
    pass_dev = passage_cache.shape[0]
    cache = passage_cache.reshape(pass_dev, PLEN, 2 * HD)
    own = own_kv.reshape(per_device * LQ, 2 * HD)

    weight = lax.all_gather(out_weight, "z", axis=0)
    weight = lax.all_gather(weight, "x", axis=0)
    weight = weight.reshape(NX * NZ, out_weight.shape[0], out_weight.shape[1])

    q_own = queries.reshape(per_device, LQ, GROUP, HD).transpose(0, 2, 1, 3)
    q_own = q_own.reshape(per_device, ROWS, HD)
    q_up = along(q_own, "z", NZ, -1)
    q_down = along(q_own, "z", NZ, 1)
    q_up2 = along(q_up, "z", NZ, -1)
    q_down2 = along(q_down, "z", NZ, 1)

    owners, local_rows = request_tables(lists, passage_slot, question_slot, per_device, pass_dev)
    mine = jnp.sum(jnp.where(owners == x * NZ + z, local_rows, 0), axis=1).reshape(NX, NZ)
    sent = jnp.array(FAR_SENT + FAR_HERE + NEAR, jnp.int32)
    target_z = (z + sent) % NZ
    rows = jnp.sum(
        jnp.where(target_z[None, :, None] == jnp.arange(NZ)[None, None, :], mine[:, None, :], 0),
        axis=2,
    )

    def items_for(first, count):
        picked = rows[:, first : first + count].reshape(NX * count)
        return over_x(take_rows(cache, picked).reshape(NX, count, PLEN, 2 * HD))

    moved = items_for(0, 3)
    far_here = items_for(3, 2)
    near_here = items_for(5, 3)
    up3 = along(moved[:, 0], "z", NZ, 1)
    down3 = along(moved[:, 1], "z", NZ, -1)
    up4 = along(moved[0:2, 2], "z", NZ, 2)
    down4 = along(moved[2:4, 2], "z", NZ, -2)

    four, low, high = range(NX), (0, 1), (2, 3)
    slots = (
        [(2, i, 0) for i in four]
        + [(-2, i, 0) for i in four]
        + [(2, i, -1) for i in four]
        + [(-2, i, 1) for i in four]
        + [(2, i, -2) for i in low]
        + [(-2, i, 2) for i in high]
        + [(0, i, 0) for i in four]
        + [(1, i, 0) for i in four]
        + [(-1, i, 0) for i in four]
    )
    slot_question = (z + jnp.array([s[0] for s in slots], jnp.int32)) % NZ
    slot_owner = jnp.array([s[1] for s in slots], jnp.int32) * NZ + (
        z + jnp.array([s[2] for s in slots], jnp.int32)
    ) % NZ
    column = lax.dynamic_index_in_dim(owners.reshape(NX, NZ, -1), x, 0, keepdims=False)
    number = jnp.arange(column.shape[1], dtype=jnp.int32) // TOPP + 1
    hit = (slot_question[:, None, None] == jnp.arange(NZ)[None, :, None]) & (
        slot_owner[:, None, None] == column[None, :, :]
    )
    tags = jnp.sum(jnp.where(hit, number[None, None, :], 0), axis=(1, 2)) - 1

    far = attention(
        far_kernel,
        "far",
        tags[:20],
        [q_up2, q_down2, far_here, up3, down3, up4, down4],
        per_device,
        2,
        15,
    )
    o_near = attention(
        near_kernel,
        "near",
        tags[20:],
        [q_own, q_up, q_down, near_here, own],
        per_device,
        3,
        10,
    )
    back_up = along(far[0:2], "z", NZ, 1)
    back_down = along(far[2:4], "z", NZ, -1)
    shapes = tuple(jax.ShapeDtypeStruct(a.shape, a.dtype) for a in far)
    hop = in_vmem(hop_kernel, "hop", shapes, *o_near[2:4], *back_up, *o_near[4:6], *back_down)
    home_up = along(hop[0:2], "z", NZ, 1)
    home_down = along(hop[2:4], "z", NZ, -1)
    context = in_vmem(
        last_kernel,
        "last",
        jax.ShapeDtypeStruct(queries.shape, jnp.bfloat16),
        *o_near[0:2],
        *home_up,
        *home_down,
    )
    partial_value = project(context, weight)
    return lax.psum_scatter(partial_value, ("y", "core"), scatter_dimension=1, tiled=True)


def solution(mesh):
    grid = Mesh(mesh.devices.reshape(NX, NZ, NY, NC), ("x", "z", "y", "core"))
    on_pass, on_head = ("x", "z"), ("y", "core")
    in_specs = (
        P(on_pass, on_head),
        P(on_pass, on_head, None),
        P(on_pass, None, on_head, None),
        P(on_head, on_pass),
        P(),
        P(),
        P(),
    )
    out_specs = P(on_pass, on_head)
    return jax.shard_map(body, mesh=grid, in_specs=in_specs, out_specs=out_specs, check_vma=False)
```

```python
import functools
import math

import jax
import jax.numpy as jnp
from jax import lax
from jax.experimental import pallas as pl
from jax.experimental.pallas import tpu as pltpu
from jax.sharding import Mesh, PartitionSpec as P

HD = 128
GROUP = 8
LQ = 128
PLEN = 512
TOPP = 8
NX, NZ, NY, NC = 4, 8, 4, 2
ROWS = GROUP * LQ
SCALE = math.log2(math.e) / math.sqrt(HD)
NEG = -1e30
WIDTH = 512
VMEM_LIMIT = 50 << 20

FAR_SENT = (3, -3, 4)
FAR_HERE = (2, -2)
NEAR = (0, 1, -1)


def request_tables(lists, passage_slot, question_slot, per_device, pass_dev):
    slot_count = question_slot.shape[0]
    slot_ids = jnp.arange(slot_count, dtype=jnp.int32)
    holder = (question_slot[None, :] == slot_ids[:, None]).astype(jnp.int32)
    chosen = jnp.sum(holder[:, :, None] * lists[None, :, :], axis=1)
    catalog = jnp.arange(passage_slot.shape[0], dtype=jnp.int32)
    picked = (chosen[:, :, None] == catalog[None, None, :]).astype(jnp.int32)
    cache_rows = jnp.sum(picked * passage_slot[None, None, :], axis=2)
    cache_rows = cache_rows.reshape(slot_count // per_device, per_device * TOPP)
    return cache_rows // pass_dev, cache_rows % pass_dev


def row_copy(rows_ref, cache_ref, out_ref):
    out_ref[...] = cache_ref[...]


def take_rows(cache, rows):
    n = rows.shape[0]
    block = (1,) + cache.shape[1:]
    return pl.pallas_call(
        row_copy,
        out_shape=jax.ShapeDtypeStruct((n,) + cache.shape[1:], cache.dtype),
        grid_spec=pltpu.PrefetchScalarGridSpec(
            num_scalar_prefetch=1,
            grid=(n,),
            in_specs=[pl.BlockSpec(block, lambda i, rows_ref: (rows_ref[i], 0, 0))],
            out_specs=pl.BlockSpec(block, lambda i, rows_ref: (i, 0, 0)),
        ),
        name="take_rows",
    )(rows, cache)


def absorb(keys, values_t, query_ref, group, cols, acc, top, total, causal=False):
    which, lane = group
    scores = lax.dot_general(
        keys,
        query_ref[lane, cols, :],
        (((1,), (1,)), ((), ())),
        preferred_element_type=jnp.float32,
    )
    if causal:
        key = lax.broadcasted_iota(jnp.int32, scores.shape, 0)
        token = lax.broadcasted_iota(jnp.int32, scores.shape, 1)
        scores = jnp.where(key <= token, scores, NEG)
    old = top[which, :, cols]
    new = jnp.maximum(old, jnp.max(scores, axis=0, keepdims=True))
    weights = jnp.exp2((scores - new) * SCALE)
    keep = jnp.exp2((old - new) * SCALE)
    top[which, :, cols] = new
    total[which, :, cols] = total[which, :, cols] * keep + jnp.sum(weights, axis=0, keepdims=True)
    acc[which, :, cols] = acc[which, :, cols] * keep + jnp.dot(
        values_t, weights.astype(jnp.bfloat16), preferred_element_type=jnp.float32
    )


def start(acc, top, total):
    acc[...] = jnp.zeros_like(acc)
    top[...] = jnp.full_like(top, NEG)
    total[...] = jnp.zeros_like(total)


def absorb_all(tag_ref, first, kv_ref, count, pick, query_ref, base, acc, top, total):
    def step(i, carry):
        tag = tag_ref[first + i]

        @pl.when(tag >= 0)
        def _():
            index = pick(i)
            keys = kv_ref[(*index, slice(None), slice(0, HD))]
            values_t = kv_ref[(*index, slice(None), slice(HD, 2 * HD))].T
            for part in range(ROWS // WIDTH):
                cols = pl.ds(part * WIDTH, WIDTH)
                absorb(keys, values_t, query_ref, (base + tag, tag), cols, acc, top, total)

        return carry

    lax.fori_loop(0, count, step, 0)


def finish(out_ref, level_ref, base, acc, top, total):
    for j in range(out_ref.shape[0]):
        sums = jnp.maximum(total[base + j], 1e-30)
        out_ref[j] = (acc[base + j] / sums).astype(jnp.bfloat16)
        level_ref[j] = top[base + j] * SCALE + jnp.log2(sums)


def far_kernel(tags, q_up, q_down, here, up3, down3, up4, down4, o_up, l_up, o_down, l_down, *state):
    start(*state)
    n = q_up.shape[0]
    absorb_all(tags, 0, here, 4, lambda i: (i, 0), q_up, 0, *state)
    absorb_all(tags, 4, here, 4, lambda i: (i, 1), q_down, n, *state)
    absorb_all(tags, 8, up3, 4, lambda i: (i,), q_up, 0, *state)
    absorb_all(tags, 12, down3, 4, lambda i: (i,), q_down, n, *state)
    absorb_all(tags, 16, up4, 2, lambda i: (i,), q_up, 0, *state)
    absorb_all(tags, 18, down4, 2, lambda i: (i,), q_down, n, *state)
    finish(o_up, l_up, 0, *state)
    finish(o_down, l_down, n, *state)


def near_kernel(
    tags, q_own, q_up, q_down, here, own, o_own, l_own, o_up, l_up, o_down, l_down, *state
):
    start(*state)
    n = q_own.shape[0]
    for j in range(n):
        rows = slice(j * LQ, (j + 1) * LQ)
        keys = own[rows, 0:HD]
        values_t = own[rows, HD : 2 * HD].T
        for part in range(GROUP):
            cols = pl.ds(part * LQ, LQ)
            absorb(keys, values_t, q_own, (j, j), cols, *state, causal=True)
    absorb_all(tags, 0, here, 4, lambda i: (i, 2), q_own, 0, *state)
    absorb_all(tags, 4, here, 4, lambda i: (i, 3), q_up, n, *state)
    absorb_all(tags, 8, here, 4, lambda i: (i, 4), q_down, 2 * n, *state)
    finish(o_own, l_own, 0, *state)
    finish(o_up, l_up, n, *state)
    finish(o_down, l_down, 2 * n, *state)


def attention(kernel, name, tags, arrays, n, sides, items):
    out = []
    for _ in range(sides):
        out.append(jax.ShapeDtypeStruct((n, HD, ROWS), jnp.bfloat16))
        out.append(jax.ShapeDtypeStruct((n, 1, ROWS), jnp.float32))
    vmem = pl.BlockSpec(memory_space=pltpu.VMEM)
    return pl.pallas_call(
        kernel,
        out_shape=tuple(out),
        in_specs=[pl.BlockSpec(memory_space=pltpu.SMEM)] + [vmem] * len(arrays),
        out_specs=(vmem,) * len(out),
        scratch_shapes=[
            pltpu.VMEM((sides * n, HD, ROWS), jnp.float32),
            pltpu.VMEM((sides * n, 1, ROWS), jnp.float32),
            pltpu.VMEM((sides * n, 1, ROWS), jnp.float32),
        ],
        compiler_params=pltpu.CompilerParams(vmem_limit_bytes=VMEM_LIMIT),
        cost_estimate=pl.CostEstimate(
            flops=items * 4 * ROWS * PLEN * HD * 2,
            bytes_accessed=items * PLEN * 2 * HD * 2,
            transcendentals=items * ROWS * PLEN,
        ),
        name=name,
    )(tags, *arrays)


def merge(pairs):
    level = pairs[0][1]
    for _, other in pairs[1:]:
        level = jnp.maximum(level, other)
    shares = [jnp.exp2(l - level) for _, l in pairs]
    whole = functools.reduce(jnp.add, shares)
    mixed = functools.reduce(
        jnp.add, [o.astype(jnp.float32) * s for (o, _), s in zip(pairs, shares)]
    )
    return mixed / whole, level + jnp.log2(whole)


def hop_kernel(o_a, l_a, o_b, l_b, o_c, l_c, o_d, l_d, o_up, l_up, o_down, l_down):
    for j in range(o_a.shape[0]):
        mixed, level = merge([(o_a[j], l_a[j]), (o_b[j], l_b[j])])
        o_up[j] = mixed.astype(jnp.bfloat16)
        l_up[j] = level
        mixed, level = merge([(o_c[j], l_c[j]), (o_d[j], l_d[j])])
        o_down[j] = mixed.astype(jnp.bfloat16)
        l_down[j] = level


def last_kernel(o_a, l_a, o_b, l_b, o_c, l_c, out_ref):
    for j in range(o_a.shape[0]):
        mixed, _ = merge([(o_a[j], l_a[j]), (o_b[j], l_b[j]), (o_c[j], l_c[j])])
        for part in range(GROUP):
            cols = slice(part * LQ, (part + 1) * LQ)
            out_ref[j * LQ : (j + 1) * LQ, part * HD : (part + 1) * HD] = mixed[:, cols].T.astype(
                jnp.bfloat16
            )


def in_vmem(kernel, name, out, *arrays):
    vmem = pl.BlockSpec(memory_space=pltpu.VMEM)
    return pl.pallas_call(
        kernel,
        out_shape=out,
        in_specs=[vmem] * len(arrays),
        out_specs=jax.tree.map(lambda _: vmem, out),
        compiler_params=pltpu.CompilerParams(vmem_limit_bytes=VMEM_LIMIT),
        name=name,
    )(*arrays)


def along(array, axis, size, shift):
    pairs = [(i, (i + shift) % size) for i in range(size)]
    return jax.tree.map(lambda a: lax.ppermute(a, axis, pairs), array)


def over_x(items):
    return lax.all_to_all(items, "x", split_axis=0, concat_axis=0, tiled=True)


def body(queries, own_kv, passage_cache, out_weight, lists, passage_slot, question_slot):
    x, z = lax.axis_index("x"), lax.axis_index("z")
    per_device = queries.shape[0] // LQ
    pass_dev = passage_cache.shape[0]
    cache = passage_cache.reshape(pass_dev, PLEN, 2 * HD)
    own = own_kv.reshape(per_device * LQ, 2 * HD)

    weight = lax.all_gather(out_weight, ("x", "z"), axis=1, tiled=True)

    q_own = queries.reshape(per_device, LQ, GROUP, HD).transpose(0, 2, 1, 3)
    q_own = q_own.reshape(per_device, ROWS, HD)
    q_up = along(q_own, "z", NZ, -1)
    q_down = along(q_own, "z", NZ, 1)

    owners, local_rows = request_tables(lists, passage_slot, question_slot, per_device, pass_dev)
    mine = jnp.sum(jnp.where(owners == x * NZ + z, local_rows, 0), axis=1).reshape(NX, NZ)
    sent = jnp.array(FAR_SENT + FAR_HERE + NEAR, jnp.int32)
    target_z = (z + sent) % NZ
    rows = jnp.sum(
        jnp.where(target_z[None, :, None] == jnp.arange(NZ)[None, None, :], mine[:, None, :], 0),
        axis=2,
    )

    def items_for(first, count):
        picked = rows[:, first : first + count].reshape(NX * count)
        return take_rows(cache, picked).reshape(NX, count, PLEN, 2 * HD)

    moved = over_x(items_for(0, 3))
    here, moved, q_up, q_down = lax.optimization_barrier((items_for(3, 5), moved, q_up, q_down))
    here = over_x(here)
    q_up2 = along(q_up, "z", NZ, -1)
    q_down2 = along(q_down, "z", NZ, 1)
    up3 = along(moved[:, 0], "z", NZ, 1)
    down3 = along(moved[:, 1], "z", NZ, -1)
    up4 = along(moved[0:2, 2], "z", NZ, 2)
    down4 = along(moved[2:4, 2], "z", NZ, -2)

    four, low, high = range(NX), (0, 1), (2, 3)
    slots = (
        [(2, i, 0) for i in four]
        + [(-2, i, 0) for i in four]
        + [(2, i, -1) for i in four]
        + [(-2, i, 1) for i in four]
        + [(2, i, -2) for i in low]
        + [(-2, i, 2) for i in high]
        + [(0, i, 0) for i in four]
        + [(1, i, 0) for i in four]
        + [(-1, i, 0) for i in four]
    )
    slot_question = (z + jnp.array([s[0] for s in slots], jnp.int32)) % NZ
    slot_owner = jnp.array([s[1] for s in slots], jnp.int32) * NZ + (
        z + jnp.array([s[2] for s in slots], jnp.int32)
    ) % NZ
    column = lax.dynamic_index_in_dim(owners.reshape(NX, NZ, -1), x, 0, keepdims=False)
    number = jnp.arange(column.shape[1], dtype=jnp.int32) // TOPP + 1
    hit = (slot_question[:, None, None] == jnp.arange(NZ)[None, :, None]) & (
        slot_owner[:, None, None] == column[None, :, :]
    )
    tags = jnp.sum(jnp.where(hit, number[None, None, :], 0), axis=(1, 2)) - 1

    far = attention(
        far_kernel,
        "far",
        tags[:20],
        [q_up2, q_down2, here, up3, down3, up4, down4],
        per_device,
        2,
        15,
    )
    o_near = attention(
        near_kernel,
        "near",
        tags[20:],
        [q_own, q_up, q_down, here, own],
        per_device,
        3,
        10,
    )
    back_up = along(far[0:2], "z", NZ, 1)
    back_down = along(far[2:4], "z", NZ, -1)
    shapes = tuple(jax.ShapeDtypeStruct(a.shape, a.dtype) for a in far)
    hop = in_vmem(hop_kernel, "hop", shapes, *o_near[2:4], *back_up, *o_near[4:6], *back_down)
    home_up = along(hop[0:2], "z", NZ, 1)
    home_down = along(hop[2:4], "z", NZ, -1)
    context = in_vmem(
        last_kernel,
        "last",
        jax.ShapeDtypeStruct(queries.shape, jnp.bfloat16),
        *o_near[0:2],
        *home_up,
        *home_down,
    )
    partial_value = jnp.dot(context, weight, preferred_element_type=jnp.float32)
    partial_value = partial_value.astype(jnp.bfloat16)
    return lax.psum_scatter(partial_value, ("y", "core"), scatter_dimension=1, tiled=True)


def solution(mesh):
    grid = Mesh(mesh.devices.reshape(NX, NZ, NY, NC), ("x", "z", "y", "core"))
    on_pass, on_head = ("x", "z"), ("y", "core")
    in_specs = (
        P(on_pass, on_head),
        P(on_pass, on_head, None),
        P(on_pass, None, on_head, None),
        P(on_head, on_pass),
        P(),
        P(),
        P(),
    )
    out_specs = P(on_pass, on_head)
    return jax.shard_map(body, mesh=grid, in_specs=in_specs, out_specs=out_specs, check_vma=False)
```

```python
import functools
import math

import jax
import jax.numpy as jnp
from jax import lax
from jax.experimental import pallas as pl
from jax.experimental.pallas import tpu as pltpu
from jax.sharding import Mesh, PartitionSpec as P

HD = 128
GROUP = 8
LQ = 128
PLEN = 512
TOPP = 8
NX, NZ, NY, NC = 4, 8, 4, 2
ROWS = GROUP * LQ
SCALE = math.log2(math.e) / math.sqrt(HD)
NEG = -1e30
WIDTH = 512
PACK = 16
VMEM_LIMIT = 50 << 20

STAY = (0, 1, -1, 2, -2)
MOVE = (3, -3, 4)


def request_tables(lists, passage_slot, question_slot, per_device, pass_dev):
    slot_count = question_slot.shape[0]
    slot_ids = jnp.arange(slot_count, dtype=jnp.int32)
    holder = (question_slot[None, :] == slot_ids[:, None]).astype(jnp.int32)
    chosen = jnp.sum(holder[:, :, None] * lists[None, :, :], axis=1)
    catalog = jnp.arange(passage_slot.shape[0], dtype=jnp.int32)
    picked = (chosen[:, :, None] == catalog[None, None, :]).astype(jnp.int32)
    cache_rows = jnp.sum(picked * passage_slot[None, None, :], axis=2)
    cache_rows = cache_rows.reshape(slot_count // per_device, per_device * TOPP)
    return cache_rows // pass_dev, cache_rows % pass_dev


def row_copies(rows_ref, cache_ref, *refs):
    outs, sems = refs[:-1], refs[-1]
    copies = []
    for out_ref in outs:
        for i in range(out_ref.shape[0]):
            n = len(copies)
            copies.append(
                pltpu.make_async_copy(cache_ref.at[rows_ref[n]], out_ref.at[i], sems.at[n])
            )
    for copy in copies:
        copy.start()
    for copy in copies:
        copy.wait()


def take_rows(cache, rows, counts):
    anywhere = pl.BlockSpec(memory_space=pl.ANY)
    return pl.pallas_call(
        row_copies,
        out_shape=tuple(jax.ShapeDtypeStruct((n,) + cache.shape[1:], cache.dtype) for n in counts),
        in_specs=[pl.BlockSpec(memory_space=pltpu.SMEM), anywhere],
        out_specs=(anywhere,) * len(counts),
        scratch_shapes=[pltpu.SemaphoreType.DMA((sum(counts),))],
        name="take_rows",
    )(rows, cache)


def absorb(keys, values_t, query_ref, group, cols, acc, top, total, causal=False):
    which, lane = group
    scores = lax.dot_general(
        keys,
        query_ref[lane, cols, :],
        (((1,), (1,)), ((), ())),
        preferred_element_type=jnp.float32,
    )
    if causal:
        key = lax.broadcasted_iota(jnp.int32, scores.shape, 0)
        token = lax.broadcasted_iota(jnp.int32, scores.shape, 1)
        scores = jnp.where(key <= token, scores, NEG)
    old = top[which, :, cols]
    new = jnp.maximum(old, jnp.max(scores, axis=0, keepdims=True))
    weights = jnp.exp2((scores - new) * SCALE)
    keep = jnp.exp2((old - new) * SCALE)
    top[which, :, cols] = new
    total[which, :, cols] = total[which, :, cols] * keep + jnp.sum(weights, axis=0, keepdims=True)
    acc[which, :, cols] = acc[which, :, cols] * keep + jnp.dot(
        values_t, weights.astype(jnp.bfloat16), preferred_element_type=jnp.float32
    )


def start(acc, top, total):
    acc[...] = jnp.zeros_like(acc)
    top[...] = jnp.full_like(top, NEG)
    total[...] = jnp.zeros_like(total)


def absorb_all(tag_ref, first, kv_ref, count, pick, query_ref, base, acc, top, total):
    def step(i, carry):
        tag = tag_ref[first + i]

        @pl.when(tag >= 0)
        def _():
            index = pick(i)
            keys = kv_ref[(*index, slice(None), slice(0, HD))]
            values_t = kv_ref[(*index, slice(None), slice(HD, 2 * HD))].T
            for part in range(ROWS // WIDTH):
                cols = pl.ds(part * WIDTH, WIDTH)
                absorb(keys, values_t, query_ref, (base + tag, tag), cols, acc, top, total)

        return carry

    lax.fori_loop(0, count, step, 0)


def pack(level):
    parts = []
    for _ in range(3):
        part = level.astype(jnp.bfloat16).astype(jnp.float32)
        parts.append(part)
        level = level - part
    parts.append(jnp.zeros((PACK - 3, level.shape[1]), jnp.float32))
    return jnp.concatenate(parts, axis=0).astype(jnp.bfloat16)


def store(out_ref, j, mixed, level):
    out_ref[j, 0:HD, :] = mixed.astype(jnp.bfloat16)
    out_ref[j, HD : HD + PACK, :] = pack(level)


def load(ref, j):
    parts = ref[j, HD : HD + PACK, :].astype(jnp.float32)
    level = parts[0:1] + parts[1:2] + parts[2:3]
    return ref[j, 0:HD, :].astype(jnp.float32), level


def state_of(group, acc, top, total):
    sums = jnp.maximum(total[group], 1e-30)
    return acc[group] / sums, top[group] * SCALE + jnp.log2(sums)


def merge(pairs):
    level = pairs[0][1]
    for _, other in pairs[1:]:
        level = jnp.maximum(level, other)
    shares = [jnp.exp2(l - level) for _, l in pairs]
    whole = functools.reduce(jnp.add, shares)
    mixed = functools.reduce(jnp.add, [o * s for (o, _), s in zip(pairs, shares)])
    return mixed / whole, level + jnp.log2(whole)


def stay_kernel(tags, here, own, q0, q1, q2, q3, q4, o0, o1, o2, o3, o4, *state):
    start(*state)
    n = q0.shape[0]
    for j in range(n):
        rows = slice(j * LQ, (j + 1) * LQ)
        keys = own[rows, 0:HD]
        values_t = own[rows, HD : 2 * HD].T
        for part in range(GROUP):
            cols = pl.ds(part * LQ, LQ)
            absorb(keys, values_t, q0, (j, j), cols, *state, causal=True)
    for k, query in enumerate((q0, q1, q2, q3, q4)):
        absorb_all(tags, k * NX, here, NX, lambda i, k=k: (i, k), query, k * n, *state)
    for k, out_ref in enumerate((o0, o1, o2, o3, o4)):
        for j in range(n):
            store(out_ref, j, *state_of(k * n + j, *state))


def move_kernel(tags, moved, q_up, q_down, so_far_up, so_far_down, o_up, o_down, *state):
    start(*state)
    n = q_up.shape[0]
    absorb_all(tags, 0, moved, NX, lambda i: (i, 0), q_up, 0, *state)
    absorb_all(tags, 4, moved, NX, lambda i: (i, 1), q_down, n, *state)
    absorb_all(tags, 8, moved, NX, lambda i: (i, 2), q_up, 0, *state)
    absorb_all(tags, 12, moved, NX, lambda i: (i, 2), q_down, n, *state)
    for j in range(n):
        store(o_up, j, *merge([state_of(j, *state), load(so_far_up, j)]))
        store(o_down, j, *merge([state_of(n + j, *state), load(so_far_down, j)]))


def attention(kernel, name, tags, arrays, n, groups, outs, items):
    vmem = pl.BlockSpec(memory_space=pltpu.VMEM)
    return pl.pallas_call(
        kernel,
        out_shape=(jax.ShapeDtypeStruct((n, HD + PACK, ROWS), jnp.bfloat16),) * outs,
        in_specs=[pl.BlockSpec(memory_space=pltpu.SMEM)] + [vmem] * len(arrays),
        out_specs=(vmem,) * outs,
        scratch_shapes=[
            pltpu.VMEM((groups * n, HD, ROWS), jnp.float32),
            pltpu.VMEM((groups * n, 1, ROWS), jnp.float32),
            pltpu.VMEM((groups * n, 1, ROWS), jnp.float32),
        ],
        compiler_params=pltpu.CompilerParams(vmem_limit_bytes=VMEM_LIMIT),
        cost_estimate=pl.CostEstimate(
            flops=items * 4 * ROWS * PLEN * HD * 2,
            bytes_accessed=items * PLEN * 2 * HD * 2,
            transcendentals=items * ROWS * PLEN,
        ),
        name=name,
    )(tags, *arrays)


def hop_kernel(near_up, back_up, near_down, back_down, o_up, o_down):
    for j in range(near_up.shape[0]):
        store(o_up, j, *merge([load(near_up, j), load(back_up, j)]))
        store(o_down, j, *merge([load(near_down, j), load(back_down, j)]))


def last_kernel(own, home_up, home_down, out_ref):
    for j in range(own.shape[0]):
        mixed, _ = merge([load(own, j), load(home_up, j), load(home_down, j)])
        for part in range(GROUP):
            cols = slice(part * LQ, (part + 1) * LQ)
            out_ref[j * LQ : (j + 1) * LQ, part * HD : (part + 1) * HD] = mixed[:, cols].T.astype(
                jnp.bfloat16
            )


def in_vmem(kernel, name, out, *arrays):
    vmem = pl.BlockSpec(memory_space=pltpu.VMEM)
    return pl.pallas_call(
        kernel,
        out_shape=out,
        in_specs=[vmem] * len(arrays),
        out_specs=jax.tree.map(lambda _: vmem, out),
        compiler_params=pltpu.CompilerParams(vmem_limit_bytes=VMEM_LIMIT),
        name=name,
    )(*arrays)


def along_z(array, shift):
    return lax.ppermute(array, "z", [(i, (i + shift) % NZ) for i in range(NZ)])


def over_x(items):
    return lax.all_to_all(items, "x", split_axis=0, concat_axis=0, tiled=True)


def body(queries, own_kv, passage_cache, out_weight, lists, passage_slot, question_slot):
    x, z = lax.axis_index("x"), lax.axis_index("z")
    per_device = queries.shape[0] // LQ
    pass_dev = passage_cache.shape[0]
    cache = passage_cache.reshape(pass_dev, PLEN, 2 * HD)
    own = own_kv.reshape(per_device * LQ, 2 * HD)

    q_own = queries.reshape(per_device, LQ, GROUP, HD).transpose(0, 2, 1, 3)
    q_own = q_own.reshape(per_device, ROWS, HD)
    q_up = along_z(q_own, -1)
    q_down = along_z(q_own, 1)
    owners, local_rows = request_tables(lists, passage_slot, question_slot, per_device, pass_dev)
    mine = jnp.sum(jnp.where(owners == x * NZ + z, local_rows, 0), axis=1).reshape(NX, NZ)
    target_z = (z + jnp.array(STAY + MOVE, jnp.int32)) % NZ
    rows = jnp.sum(
        jnp.where(target_z[None, :, None] == jnp.arange(NZ)[None, None, :], mine[:, None, :], 0),
        axis=2,
    )
    stay = len(STAY)
    (here,) = take_rows(cache, rows[:, :stay].reshape(-1), (NX * stay,))
    here = over_x(here.reshape(NX, stay, PLEN, 2 * HD))
    moving = take_rows(cache, rows[:, stay:].T.reshape(-1), (4, 4, 2, 2))
    (up3, down3, up4, down4), q_up, q_down = lax.optimization_barrier((moving, q_up, q_down))
    up3 = along_z(up3, 1)
    down3 = along_z(down3, -1)
    up4 = along_z(up4, 2)
    down4 = along_z(down4, -2)
    moved = jnp.stack([up3, down3, jnp.concatenate([up4, down4], axis=0)], axis=1)
    moved, here, out_weight = lax.optimization_barrier((moved, here, out_weight))
    moved = over_x(moved)
    weight = lax.all_gather(out_weight, "z", axis=1, tiled=True)
    q_up2 = along_z(q_up, -1)
    q_down2 = along_z(q_down, 1)

    four = range(NX)
    slots = (
        [(d, i, 0) for d in STAY for i in four]
        + [(2, i, -1) for i in four]
        + [(-2, i, 1) for i in four]
        + [(2, i, -2) for i in four]
        + [(-2, i, 2) for i in four]
    )
    count = len(slots)
    slot_question = (z + jnp.array([s[0] for s in slots], jnp.int32)) % NZ
    slot_owner = jnp.array([s[1] for s in slots], jnp.int32) * NZ + (
        z + jnp.array([s[2] for s in slots], jnp.int32)
    ) % NZ
    index = jnp.arange(count)
    absent = jnp.where(x < 2, index >= count - NX, (index >= count - 2 * NX) & (index < count - NX))
    column = lax.dynamic_index_in_dim(owners.reshape(NX, NZ, -1), x, 0, keepdims=False)
    number = jnp.arange(column.shape[1], dtype=jnp.int32) // TOPP + 1
    hit = (slot_question[:, None, None] == jnp.arange(NZ)[None, :, None]) & (
        slot_owner[:, None, None] == column[None, :, :]
    )
    tags = jnp.sum(jnp.where(hit, number[None, None, :], 0), axis=(1, 2)) - 1
    tags = jnp.where(absent, -1, tags)

    split = NX * stay
    own_part, near_up, near_down, far_up, far_down = attention(
        stay_kernel,
        "stay",
        tags[:split],
        [here, own, q_own, q_up, q_down, q_up2, q_down2],
        per_device,
        stay,
        stay,
        17,
    )
    weight, moved, far_up, far_down = lax.optimization_barrier((weight, moved, far_up, far_down))
    weight = lax.all_gather(weight, "x", axis=1, tiled=True)
    far_up, far_down = attention(
        move_kernel,
        "move",
        tags[split:],
        [moved, q_up2, q_down2, far_up, far_down],
        per_device,
        2,
        2,
        9,
    )
    shape = jax.ShapeDtypeStruct(own_part.shape, own_part.dtype)
    hop_up, hop_down = in_vmem(
        hop_kernel,
        "hop",
        (shape, shape),
        near_up,
        along_z(far_up, 1),
        near_down,
        along_z(far_down, -1),
    )
    context = in_vmem(
        last_kernel,
        "last",
        jax.ShapeDtypeStruct(queries.shape, jnp.bfloat16),
        own_part,
        along_z(hop_up, 1),
        along_z(hop_down, -1),
    )
    partial_value = jnp.dot(context, weight, preferred_element_type=jnp.float32)
    partial_value = partial_value.astype(jnp.bfloat16)
    return lax.psum_scatter(partial_value, ("y", "core"), scatter_dimension=1, tiled=True)


def solution(mesh):
    grid = Mesh(mesh.devices.reshape(NX, NZ, NY, NC), ("x", "z", "y", "core"))
    on_pass, on_head = ("x", "z"), ("y", "core")
    in_specs = (
        P(on_pass, on_head),
        P(on_pass, on_head, None),
        P(on_pass, None, on_head, None),
        P(on_head, on_pass),
        P(),
        P(),
        P(),
    )
    out_specs = P(on_pass, on_head)
    return jax.shard_map(body, mesh=grid, in_specs=in_specs, out_specs=out_specs, check_vma=False)
```

```python
import functools
import math

import jax
import jax.numpy as jnp
from jax import lax
from jax.experimental import pallas as pl
from jax.experimental.pallas import tpu as pltpu
from jax.sharding import Mesh, PartitionSpec as P

HD = 128
GROUP = 8
LQ = 128
PLEN = 512
TOPP = 8
NX, NZ, NY, NC = 4, 8, 4, 2
ROWS = GROUP * LQ
SCALE = math.log2(math.e) / math.sqrt(HD)
NEG = -1e30
WIDTH = 512
PACK = 16
VMEM_LIMIT = 50 << 20

STAY = (0, 1, -1, 2, -2)
MOVE = (3, -3, 4)


def request_tables(lists, passage_slot, question_slot, per_device, pass_dev):
    slot_count = question_slot.shape[0]
    slot_ids = jnp.arange(slot_count, dtype=jnp.int32)
    holder = (question_slot[None, :] == slot_ids[:, None]).astype(jnp.int32)
    chosen = jnp.sum(holder[:, :, None] * lists[None, :, :], axis=1)
    catalog = jnp.arange(passage_slot.shape[0], dtype=jnp.int32)
    picked = (chosen[:, :, None] == catalog[None, None, :]).astype(jnp.int32)
    cache_rows = jnp.sum(picked * passage_slot[None, None, :], axis=2)
    cache_rows = cache_rows.reshape(slot_count // per_device, per_device * TOPP)
    return cache_rows // pass_dev, cache_rows % pass_dev


def row_copies(rows_ref, cache_ref, *refs):
    outs, (buffer, read_sems, write_sems) = refs[:-3], refs[-3:]
    places = [out_ref.at[i] for out_ref in outs for i in range(out_ref.shape[0])]
    reads, writes = [], []
    for n, place in enumerate(places):
        reads.append(
            pltpu.make_async_copy(cache_ref.at[rows_ref[n]], buffer.at[n], read_sems.at[n])
        )
        writes.append(pltpu.make_async_copy(buffer.at[n], place, write_sems.at[n]))
    for read in reads:
        read.start()
    for read, write in zip(reads, writes):
        read.wait()
        write.start()
    for write in writes:
        write.wait()


def take_rows(cache, rows, counts):
    anywhere = pl.BlockSpec(memory_space=pl.ANY)
    total = sum(counts)
    return pl.pallas_call(
        row_copies,
        out_shape=tuple(jax.ShapeDtypeStruct((n,) + cache.shape[1:], cache.dtype) for n in counts),
        in_specs=[pl.BlockSpec(memory_space=pltpu.SMEM), anywhere],
        out_specs=(anywhere,) * len(counts),
        scratch_shapes=[
            pltpu.VMEM((total,) + cache.shape[1:], cache.dtype),
            pltpu.SemaphoreType.DMA((total,)),
            pltpu.SemaphoreType.DMA((total,)),
        ],
        compiler_params=pltpu.CompilerParams(vmem_limit_bytes=VMEM_LIMIT),
        name="take_rows",
    )(rows, cache)


def absorb(keys, values_t, query_ref, group, cols, acc, top, total, causal=False):
    which, lane = group
    scores = lax.dot_general(
        keys,
        query_ref[lane, cols, :],
        (((1,), (1,)), ((), ())),
        preferred_element_type=jnp.float32,
    )
    if causal:
        key = lax.broadcasted_iota(jnp.int32, scores.shape, 0)
        token = lax.broadcasted_iota(jnp.int32, scores.shape, 1)
        scores = jnp.where(key <= token, scores, NEG)
    old = top[which, :, cols]
    new = jnp.maximum(old, jnp.max(scores, axis=0, keepdims=True))
    weights = jnp.exp2((scores - new) * SCALE)
    keep = jnp.exp2((old - new) * SCALE)
    top[which, :, cols] = new
    total[which, :, cols] = total[which, :, cols] * keep + jnp.sum(weights, axis=0, keepdims=True)
    acc[which, :, cols] = acc[which, :, cols] * keep + jnp.dot(
        values_t, weights.astype(jnp.bfloat16), preferred_element_type=jnp.float32
    )


def start(acc, top, total):
    acc[...] = jnp.zeros_like(acc)
    top[...] = jnp.full_like(top, NEG)
    total[...] = jnp.zeros_like(total)


def fetches(items_ref, picks, buffer, sems):
    return [
        pltpu.make_async_copy(items_ref.at[i, k], buffer.at[n], sems.at[n])
        for n, (i, k) in enumerate(picks)
    ]


def absorb_all(tag_ref, first, copies, slot, buffer, query_ref, base, acc, top, total):
    for copy in copies:
        copy.wait()

    def step(i, carry):
        tag = tag_ref[first + i]

        @pl.when(tag >= 0)
        def _():
            keys = buffer[slot + i, :, 0:HD]
            values_t = buffer[slot + i, :, HD : 2 * HD].T
            for part in range(ROWS // WIDTH):
                cols = pl.ds(part * WIDTH, WIDTH)
                absorb(keys, values_t, query_ref, (base + tag, tag), cols, acc, top, total)

        return carry

    lax.fori_loop(0, NX, step, 0)


def pack(level):
    parts = []
    for _ in range(3):
        part = level.astype(jnp.bfloat16).astype(jnp.float32)
        parts.append(part)
        level = level - part
    parts.append(jnp.zeros((PACK - 3, level.shape[1]), jnp.float32))
    return jnp.concatenate(parts, axis=0).astype(jnp.bfloat16)


def store(out_ref, j, mixed, level):
    out_ref[j, 0:HD, :] = mixed.astype(jnp.bfloat16)
    out_ref[j, HD : HD + PACK, :] = pack(level)


def load(ref, j):
    parts = ref[j, HD : HD + PACK, :].astype(jnp.float32)
    level = parts[0:1] + parts[1:2] + parts[2:3]
    return ref[j, 0:HD, :].astype(jnp.float32), level


def state_of(group, acc, top, total):
    sums = jnp.maximum(total[group], 1e-30)
    return acc[group] / sums, top[group] * SCALE + jnp.log2(sums)


def merge(pairs):
    level = pairs[0][1]
    for _, other in pairs[1:]:
        level = jnp.maximum(level, other)
    shares = [jnp.exp2(l - level) for _, l in pairs]
    whole = functools.reduce(jnp.add, shares)
    mixed = functools.reduce(jnp.add, [o * s for (o, _), s in zip(pairs, shares)])
    return mixed / whole, level + jnp.log2(whole)


def near_kernel(tags, here, own, q0, q1, q2, o0, o1, o2, buffer, sems, *state):
    copies = fetches(here, [(i, k) for k in range(3) for i in range(NX)], buffer, sems)
    for copy in copies:
        copy.start()
    start(*state)
    n = q0.shape[0]
    for j in range(n):
        rows = slice(j * LQ, (j + 1) * LQ)
        keys = own[rows, 0:HD]
        values_t = own[rows, HD : 2 * HD].T

        def head(part, carry, j=j, keys=keys, values_t=values_t):
            cols = pl.ds(pl.multiple_of(part * LQ, LQ), LQ)
            absorb(keys, values_t, q0, (j, j), cols, *state, causal=True)
            return carry

        lax.fori_loop(0, GROUP, head, 0)
    for k, query in enumerate((q0, q1, q2)):
        slot = k * NX
        absorb_all(tags, slot, copies[slot : slot + NX], slot, buffer, query, k * n, *state)
    for k, out_ref in enumerate((o0, o1, o2)):
        for j in range(n):
            store(out_ref, j, *state_of(k * n + j, *state))


def far_kernel(tags, here, q_up, q_down, o_up, o_down, buffer, sems, *state):
    copies = fetches(here, [(i, k) for k in (3, 4) for i in range(NX)], buffer, sems)
    for copy in copies:
        copy.start()
    start(*state)
    n = q_up.shape[0]
    absorb_all(tags, 0, copies[0:4], 0, buffer, q_up, 0, *state)
    absorb_all(tags, 4, copies[4:8], 4, buffer, q_down, n, *state)
    for j in range(n):
        store(o_up, j, *state_of(j, *state))
        store(o_down, j, *state_of(n + j, *state))


def move_kernel(
    tags, moved, q_up, q_down, so_far_up, so_far_down, o_up, o_down, buffer, sems, *state
):
    copies = fetches(moved, [(i, k) for k in range(3) for i in range(NX)], buffer, sems)
    for copy in copies:
        copy.start()
    start(*state)
    n = q_up.shape[0]
    absorb_all(tags, 0, copies[0:4], 0, buffer, q_up, 0, *state)
    absorb_all(tags, 4, copies[4:8], 4, buffer, q_down, n, *state)
    absorb_all(tags, 8, copies[8:12], 8, buffer, q_up, 0, *state)
    absorb_all(tags, 12, [], 8, buffer, q_down, n, *state)
    for j in range(n):
        store(o_up, j, *merge([state_of(j, *state), load(so_far_up, j)]))
        store(o_down, j, *merge([state_of(n + j, *state), load(so_far_down, j)]))


def attention(kernel, name, tags, items, arrays, n, groups, slots, work):
    vmem = pl.BlockSpec(memory_space=pltpu.VMEM)
    return pl.pallas_call(
        kernel,
        out_shape=(jax.ShapeDtypeStruct((n, HD + PACK, ROWS), jnp.bfloat16),) * groups,
        in_specs=[pl.BlockSpec(memory_space=pltpu.SMEM), pl.BlockSpec(memory_space=pl.ANY)]
        + [vmem] * len(arrays),
        out_specs=(vmem,) * groups,
        scratch_shapes=[
            pltpu.VMEM((slots, PLEN, 2 * HD), jnp.bfloat16),
            pltpu.SemaphoreType.DMA((slots,)),
            pltpu.VMEM((groups * n, HD, ROWS), jnp.float32),
            pltpu.VMEM((groups * n, 1, ROWS), jnp.float32),
            pltpu.VMEM((groups * n, 1, ROWS), jnp.float32),
        ],
        compiler_params=pltpu.CompilerParams(vmem_limit_bytes=VMEM_LIMIT),
        cost_estimate=pl.CostEstimate(
            flops=work * ROWS * PLEN,
            bytes_accessed=work * PLEN,
            transcendentals=0,
        ),
        name=name,
    )(tags, items, *arrays)


def last_kernel(*refs):
    parts, out_ref = refs[:-1], refs[-1]
    for j in range(parts[0].shape[0]):
        mixed, _ = merge([load(part, j) for part in parts])
        for head in range(GROUP):
            cols = slice(head * LQ, (head + 1) * LQ)
            out_ref[j * LQ : (j + 1) * LQ, head * HD : (head + 1) * HD] = mixed[:, cols].T.astype(
                jnp.bfloat16
            )


def project_kernel(core_ref, context_ref, weight_ref, out_ref):
    out_ref[0] = jnp.dot(
        context_ref[...], weight_ref[...], preferred_element_type=jnp.float32
    ).astype(jnp.bfloat16)


def project(context, weight, core, name):
    width = weight.shape[1] // (NY * NC)
    return pl.pallas_call(
        project_kernel,
        out_shape=jax.ShapeDtypeStruct((NY, context.shape[0], width), jnp.bfloat16),
        grid_spec=pltpu.PrefetchScalarGridSpec(
            num_scalar_prefetch=1,
            grid=(NY,),
            in_specs=[
                pl.BlockSpec(context.shape, lambda i, core_ref: (0, 0)),
                pl.BlockSpec(
                    (weight.shape[0], width), lambda i, core_ref: (0, NC * i + core_ref[0])
                ),
            ],
            out_specs=pl.BlockSpec((1, context.shape[0], width), lambda i, core_ref: (i, 0, 0)),
        ),
        compiler_params=pltpu.CompilerParams(vmem_limit_bytes=VMEM_LIMIT),
        cost_estimate=pl.CostEstimate(
            flops=2 * context.shape[0] * weight.shape[0] * width * NY,
            bytes_accessed=weight.shape[0] * width * NY * 2,
            transcendentals=0,
        ),
        name=name,
    )(core.reshape(1), context, weight)


def in_vmem(kernel, name, out, *arrays):
    vmem = pl.BlockSpec(memory_space=pltpu.VMEM)
    return pl.pallas_call(
        kernel,
        out_shape=out,
        in_specs=[vmem] * len(arrays),
        out_specs=jax.tree.map(lambda _: vmem, out),
        compiler_params=pltpu.CompilerParams(vmem_limit_bytes=VMEM_LIMIT),
        name=name,
    )(*arrays)


def along_z(array, shift):
    return lax.ppermute(array, "z", [(i, (i + shift) % NZ) for i in range(NZ)])


def over_x(items):
    return lax.all_to_all(items, "x", split_axis=0, concat_axis=0, tiled=True)


def body(queries, own_kv, passage_cache, out_weight, lists, passage_slot, question_slot):
    x, z = lax.axis_index("x"), lax.axis_index("z")
    per_device = queries.shape[0] // LQ
    pass_dev = passage_cache.shape[0]
    cache = passage_cache.reshape(pass_dev, PLEN, 2 * HD)
    own = own_kv.reshape(per_device * LQ, 2 * HD)

    q_own = queries.reshape(per_device, LQ, GROUP, HD).transpose(0, 2, 1, 3)
    q_own = q_own.reshape(per_device, ROWS, HD)
    q_up = along_z(q_own, -1)
    q_down = along_z(q_own, 1)
    owners, local_rows = request_tables(lists, passage_slot, question_slot, per_device, pass_dev)
    mine = jnp.sum(jnp.where(owners == x * NZ + z, local_rows, 0), axis=1).reshape(NX, NZ)
    target_z = (z + jnp.array(STAY + MOVE, jnp.int32)) % NZ
    rows = jnp.sum(
        jnp.where(target_z[None, :, None] == jnp.arange(NZ)[None, None, :], mine[:, None, :], 0),
        axis=2,
    )
    stay = len(STAY)
    (here,) = take_rows(cache, rows[:, :stay].reshape(-1), (NX * stay,))
    here = over_x(here.reshape(NX, stay, PLEN, 2 * HD))
    moving = take_rows(cache, rows[:, stay:].T.reshape(-1), (4, 4, 2, 2))
    (up3, down3, up4, down4), q_up, q_down = lax.optimization_barrier((moving, q_up, q_down))
    up3 = along_z(up3, 1)
    down3 = along_z(down3, -1)
    up4 = along_z(up4, 2)
    down4 = along_z(down4, -2)
    moved = jnp.stack([up3, down3, jnp.concatenate([up4, down4], axis=0)], axis=1)
    weight = lax.all_gather(out_weight, "z", axis=1, tiled=True)
    moved, here, q_up, q_down = lax.optimization_barrier((moved, here, q_up, q_down))
    moved = over_x(moved)
    q_up2 = along_z(q_up, -1)
    q_down2 = along_z(q_down, 1)

    four = range(NX)
    slots = (
        [(d, i, 0) for d in STAY for i in four]
        + [(2, i, -1) for i in four]
        + [(-2, i, 1) for i in four]
        + [(2, i, -2) for i in four]
        + [(-2, i, 2) for i in four]
    )
    count = len(slots)
    slot_question = (z + jnp.array([s[0] for s in slots], jnp.int32)) % NZ
    slot_owner = jnp.array([s[1] for s in slots], jnp.int32) * NZ + (
        z + jnp.array([s[2] for s in slots], jnp.int32)
    ) % NZ
    index = jnp.arange(count)
    absent = jnp.where(x < 2, index >= count - NX, (index >= count - 2 * NX) & (index < count - NX))
    column = lax.dynamic_index_in_dim(owners.reshape(NX, NZ, -1), x, 0, keepdims=False)
    number = jnp.arange(column.shape[1], dtype=jnp.int32) // TOPP + 1
    hit = (slot_question[:, None, None] == jnp.arange(NZ)[None, :, None]) & (
        slot_owner[:, None, None] == column[None, :, :]
    )
    tags = jnp.sum(jnp.where(hit, number[None, None, :], 0), axis=(1, 2)) - 1
    tags = jnp.where(absent, -1, tags)

    split = NX * stay
    near = attention(
        near_kernel,
        "near",
        tags[: 3 * NX],
        here,
        [own, q_own, q_up, q_down],
        per_device,
        3,
        3 * NX,
        10,
    )
    near, q_up2, q_down2 = lax.optimization_barrier((near, q_up2, q_down2))
    own_part, near_up, near_down = near
    home_up = along_z(near_up, 1)
    home_down = along_z(near_down, -1)
    far = attention(
        far_kernel,
        "far",
        tags[3 * NX : split],
        here,
        [q_up2, q_down2],
        per_device,
        2,
        2 * NX,
        6,
    )
    weight, moved, far, home_up, home_down = lax.optimization_barrier(
        (weight, moved, far, home_up, home_down)
    )
    weight = lax.all_gather(weight, "x", axis=1, tiled=True)
    far_up, far_down = attention(
        move_kernel,
        "move",
        tags[split:],
        moved,
        [q_up2, q_down2, *far],
        per_device,
        2,
        3 * NX,
        9,
    )
    context = in_vmem(
        last_kernel,
        "last",
        jax.ShapeDtypeStruct(queries.shape, jnp.bfloat16),
        own_part,
        home_up,
        home_down,
        along_z(far_up, 2),
        along_z(far_down, -2),
    )
    core = lax.axis_index("core")
    theirs = project(context, weight, 1 - core, "theirs")
    theirs = lax.ppermute(theirs, "core", [(0, 1), (1, 0)])
    ours = project(context, weight, core, "ours")
    chip = (ours.astype(jnp.float32) + theirs.astype(jnp.float32)).astype(jnp.bfloat16)
    chips = lax.all_to_all(chip, "y", split_axis=0, concat_axis=0, tiled=True)
    return jnp.sum(chips.astype(jnp.float32), axis=0).astype(jnp.bfloat16)


def solution(mesh):
    grid = Mesh(mesh.devices.reshape(NX, NZ, NY, NC), ("x", "z", "y", "core"))
    on_pass, on_head = ("x", "z"), ("y", "core")
    in_specs = (
        P(on_pass, on_head),
        P(on_pass, on_head, None),
        P(on_pass, None, on_head, None),
        P(on_head, on_pass),
        P(),
        P(),
        P(),
    )
    out_specs = P(on_pass, on_head)
    return jax.shard_map(body, mesh=grid, in_specs=in_specs, out_specs=out_specs, check_vma=False)
```

```python
import functools
import math

import jax
import jax.numpy as jnp
from jax import lax
from jax.experimental import pallas as pl
from jax.experimental.pallas import tpu as pltpu
from jax.sharding import Mesh, PartitionSpec as P

HD = 128
GROUP = 8
LQ = 128
PLEN = 512
TOPP = 8
NX, NZ, NY, NC = 4, 8, 4, 2
ROWS = GROUP * LQ
SCALE = math.log2(math.e) / math.sqrt(HD)
NEG = -1e30
WIDTH = 512
PACK = 16
VMEM_LIMIT = 50 << 20

STAY = (0, 1, -1, 2, -2)
MOVE = (3, -3, 4)


def request_tables(lists, passage_slot, question_slot, per_device, pass_dev):
    slot_count = question_slot.shape[0]
    slot_ids = jnp.arange(slot_count, dtype=jnp.int32)
    holder = (question_slot[None, :] == slot_ids[:, None]).astype(jnp.int32)
    chosen = jnp.sum(holder[:, :, None] * lists[None, :, :], axis=1)
    catalog = jnp.arange(passage_slot.shape[0], dtype=jnp.int32)
    picked = (chosen[:, :, None] == catalog[None, None, :]).astype(jnp.int32)
    cache_rows = jnp.sum(picked * passage_slot[None, None, :], axis=2)
    cache_rows = cache_rows.reshape(slot_count // per_device, per_device * TOPP)
    return cache_rows // pass_dev, cache_rows % pass_dev


def row_copies(rows_ref, cache_ref, *refs):
    outs, (buffer, read_sems, write_sems) = refs[:-3], refs[-3:]
    places = [out_ref.at[i] for out_ref in outs for i in range(out_ref.shape[0])]
    reads, writes = [], []
    for n, place in enumerate(places):
        reads.append(
            pltpu.make_async_copy(cache_ref.at[rows_ref[n]], buffer.at[n], read_sems.at[n])
        )
        writes.append(pltpu.make_async_copy(buffer.at[n], place, write_sems.at[n]))
    for read in reads:
        read.start()
    for read, write in zip(reads, writes):
        read.wait()
        write.start()
    for write in writes:
        write.wait()


def take_rows(cache, rows, counts):
    anywhere = pl.BlockSpec(memory_space=pl.ANY)
    total = sum(counts)
    return pl.pallas_call(
        row_copies,
        out_shape=tuple(jax.ShapeDtypeStruct((n,) + cache.shape[1:], cache.dtype) for n in counts),
        in_specs=[pl.BlockSpec(memory_space=pltpu.SMEM), anywhere],
        out_specs=(anywhere,) * len(counts),
        scratch_shapes=[
            pltpu.VMEM((total,) + cache.shape[1:], cache.dtype),
            pltpu.SemaphoreType.DMA((total,)),
            pltpu.SemaphoreType.DMA((total,)),
        ],
        compiler_params=pltpu.CompilerParams(vmem_limit_bytes=VMEM_LIMIT),
        name="take_rows",
    )(rows, cache)


def absorb(keys, values_t, query_ref, group, cols, acc, top, total, causal=False):
    scores = lax.dot_general(
        keys,
        query_ref[group, cols, :],
        (((1,), (1,)), ((), ())),
        preferred_element_type=jnp.float32,
    )
    if causal:
        key = lax.broadcasted_iota(jnp.int32, scores.shape, 0)
        token = lax.broadcasted_iota(jnp.int32, scores.shape, 1)
        scores = jnp.where(key <= token, scores, NEG)
    old = top[group, :, cols]
    new = jnp.maximum(old, jnp.max(scores, axis=0, keepdims=True))
    weights = jnp.exp2((scores - new) * SCALE)
    keep = jnp.exp2((old - new) * SCALE)
    top[group, :, cols] = new
    total[group, :, cols] = total[group, :, cols] * keep + jnp.sum(weights, axis=0, keepdims=True)
    acc[group, :, cols] = acc[group, :, cols] * keep + jnp.dot(
        values_t, weights.astype(jnp.bfloat16), preferred_element_type=jnp.float32
    )


def start(acc, top, total):
    acc[...] = jnp.zeros_like(acc)
    top[...] = jnp.full_like(top, NEG)
    total[...] = jnp.zeros_like(total)


def fetches(items_ref, picks, buffer, sems):
    return [
        pltpu.make_async_copy(items_ref.at[i, k], buffer.at[n], sems.at[n])
        for n, (i, k) in enumerate(picks)
    ]


def absorb_all(tag_ref, copies, buffer, query_ref, acc, top, total):
    for copy in copies:
        copy.wait()

    def step(i, carry):
        tag = tag_ref[i]

        @pl.when(tag >= 0)
        def _():
            keys = buffer[i, :, 0:HD]
            values_t = buffer[i, :, HD : 2 * HD].T
            for part in range(ROWS // WIDTH):
                cols = pl.ds(part * WIDTH, WIDTH)
                absorb(keys, values_t, query_ref, tag, cols, acc, top, total)

        return carry

    lax.fori_loop(0, len(copies), step, 0)


def pack(level):
    parts = []
    for _ in range(3):
        part = level.astype(jnp.bfloat16).astype(jnp.float32)
        parts.append(part)
        level = level - part
    parts.append(jnp.zeros((PACK - 3, level.shape[1]), jnp.float32))
    return jnp.concatenate(parts, axis=0).astype(jnp.bfloat16)


def store(out_ref, j, mixed, level):
    out_ref[j, 0:HD, :] = mixed.astype(jnp.bfloat16)
    out_ref[j, HD : HD + PACK, :] = pack(level)


def load(ref, j):
    parts = ref[j, HD : HD + PACK, :].astype(jnp.float32)
    level = parts[0:1] + parts[1:2] + parts[2:3]
    return ref[j, 0:HD, :].astype(jnp.float32), level


def state_of(group, acc, top, total):
    sums = jnp.maximum(total[group], 1e-30)
    return acc[group] / sums, top[group] * SCALE + jnp.log2(sums)


def merge(pairs):
    level = pairs[0][1]
    for _, other in pairs[1:]:
        level = jnp.maximum(level, other)
    shares = [jnp.exp2(l - level) for _, l in pairs]
    whole = functools.reduce(jnp.add, shares)
    mixed = functools.reduce(jnp.add, [o * s for (o, _), s in zip(pairs, shares)])
    return mixed / whole, level + jnp.log2(whole)


def near_kernel(tags, here, own, query, o0, o1, o2, buffer, sems, *state):
    copies = fetches(here, [(i, k) for k in range(3) for i in range(NX)], buffer, sems)
    for copy in copies:
        copy.start()
    start(*state)
    n = o0.shape[0]
    for j in range(n):
        rows = slice(j * LQ, (j + 1) * LQ)
        keys = own[rows, 0:HD]
        values_t = own[rows, HD : 2 * HD].T

        def head(part, carry, j=j, keys=keys, values_t=values_t):
            cols = pl.ds(pl.multiple_of(part * LQ, LQ), LQ)
            absorb(keys, values_t, query, j, cols, *state, causal=True)
            return carry

        lax.fori_loop(0, GROUP, head, 0)
    absorb_all(tags, copies, buffer, query, *state)
    for k, out_ref in enumerate((o0, o1, o2)):
        for j in range(n):
            store(out_ref, j, *state_of(k * n + j, *state))


def far_kernel(tags, here, query, o_up, o_down, buffer, sems, *state):
    copies = fetches(here, [(i, k) for k in (3, 4) for i in range(NX)], buffer, sems)
    for copy in copies:
        copy.start()
    start(*state)
    absorb_all(tags, copies, buffer, query, *state)
    n = o_up.shape[0]
    for j in range(n):
        store(o_up, j, *state_of(j, *state))
        store(o_down, j, *state_of(n + j, *state))


def move_kernel(tags, moved, query, so_far_up, so_far_down, o_up, o_down, buffer, sems, *state):
    copies = fetches(moved, [(i, k) for k in range(3) for i in range(NX)], buffer, sems)
    for copy in copies:
        copy.start()
    start(*state)
    absorb_all(tags, copies, buffer, query, *state)
    n = o_up.shape[0]
    for j in range(n):
        store(o_up, j, *merge([state_of(j, *state), load(so_far_up, j)]))
        store(o_down, j, *merge([state_of(n + j, *state), load(so_far_down, j)]))


def attention(kernel, name, tags, items, arrays, n, groups, slots, work):
    vmem = pl.BlockSpec(memory_space=pltpu.VMEM)
    return pl.pallas_call(
        kernel,
        out_shape=(jax.ShapeDtypeStruct((n, HD + PACK, ROWS), jnp.bfloat16),) * groups,
        in_specs=[pl.BlockSpec(memory_space=pltpu.SMEM), pl.BlockSpec(memory_space=pl.ANY)]
        + [vmem] * len(arrays),
        out_specs=(vmem,) * groups,
        scratch_shapes=[
            pltpu.VMEM((slots, PLEN, 2 * HD), jnp.bfloat16),
            pltpu.SemaphoreType.DMA((slots,)),
            pltpu.VMEM((groups * n, HD, ROWS), jnp.float32),
            pltpu.VMEM((groups * n, 1, ROWS), jnp.float32),
            pltpu.VMEM((groups * n, 1, ROWS), jnp.float32),
        ],
        compiler_params=pltpu.CompilerParams(vmem_limit_bytes=VMEM_LIMIT),
        cost_estimate=pl.CostEstimate(
            flops=work * ROWS * PLEN,
            bytes_accessed=work * PLEN,
            transcendentals=0,
        ),
        name=name,
    )(tags, items, *arrays)


def last_kernel(*refs):
    parts, out_ref = refs[:-1], refs[-1]
    for j in range(parts[0].shape[0]):
        mixed, _ = merge([load(part, j) for part in parts])
        for head in range(GROUP):
            cols = slice(head * LQ, (head + 1) * LQ)
            out_ref[j * LQ : (j + 1) * LQ, head * HD : (head + 1) * HD] = mixed[:, cols].T.astype(
                jnp.bfloat16
            )


def project_kernel(place, context_ref, own_ref, before_ref, after_ref, top_ref, bottom_ref, out_ref):
    x = place[1]

    def put(index, products):
        out_ref[lax.rem(index, NX)] = functools.reduce(jnp.add, products).astype(jnp.bfloat16)

    def times(cols, weight_ref):
        return jnp.dot(
            context_ref[:, cols], weight_ref[...], preferred_element_type=jnp.float32
        )

    half = top_ref.shape[0]
    everything = slice(None)
    put(x, [times(everything, own_ref)])
    put(x + NX - 1, [times(everything, before_ref)])
    put(x + 1, [times(everything, after_ref)])
    put(x + 2, [times(slice(0, half), top_ref), times(slice(half, None), bottom_ref)])


def project(context, weights, core, x, name):
    tile = 256
    width = weights[0].shape[1] // NC
    steps = width // tile

    def tiles(weight):
        return pl.BlockSpec((weight.shape[0], tile), lambda i, place: (0, steps * place[0] + i))

    return pl.pallas_call(
        project_kernel,
        out_shape=jax.ShapeDtypeStruct((NX, context.shape[0], width), jnp.bfloat16),
        grid_spec=pltpu.PrefetchScalarGridSpec(
            num_scalar_prefetch=1,
            grid=(steps,),
            in_specs=[pl.BlockSpec(context.shape, lambda i, place: (0, 0))]
            + [tiles(weight) for weight in weights],
            out_specs=pl.BlockSpec((NX, context.shape[0], tile), lambda i, place: (0, 0, i)),
        ),
        compiler_params=pltpu.CompilerParams(vmem_limit_bytes=VMEM_LIMIT),
        cost_estimate=pl.CostEstimate(
            flops=2 * context.shape[0] * context.shape[1] * width * NX,
            bytes_accessed=context.shape[1] * width * NX * 2,
            transcendentals=0,
        ),
        name=name,
    )(jnp.stack([core, x]), context, *weights)


def in_vmem(kernel, name, out, *arrays):
    vmem = pl.BlockSpec(memory_space=pltpu.VMEM)
    return pl.pallas_call(
        kernel,
        out_shape=out,
        in_specs=[vmem] * len(arrays),
        out_specs=jax.tree.map(lambda _: vmem, out),
        compiler_params=pltpu.CompilerParams(vmem_limit_bytes=VMEM_LIMIT),
        name=name,
    )(*arrays)


def along_z(array, shift):
    return lax.ppermute(array, "z", [(i, (i + shift) % NZ) for i in range(NZ)])


def along_x(array, shift):
    return lax.ppermute(array, "x", [(i, (i + shift) % NX) for i in range(NX)])


def over_x(items):
    return lax.all_to_all(items, "x", split_axis=0, concat_axis=0, tiled=True)


def body(queries, own_kv, passage_cache, out_weight, lists, passage_slot, question_slot):
    x, z = lax.axis_index("x"), lax.axis_index("z")
    per_device = queries.shape[0] // LQ
    pass_dev = passage_cache.shape[0]
    cache = passage_cache.reshape(pass_dev, PLEN, 2 * HD)
    own = own_kv.reshape(per_device * LQ, 2 * HD)

    q_own = queries.reshape(per_device, LQ, GROUP, HD).transpose(0, 2, 1, 3)
    q_own = q_own.reshape(per_device, ROWS, HD)
    owners, local_rows = request_tables(lists, passage_slot, question_slot, per_device, pass_dev)
    mine = jnp.sum(jnp.where(owners == x * NZ + z, local_rows, 0), axis=1).reshape(NX, NZ)
    target_z = (z + jnp.array(STAY + MOVE, jnp.int32)) % NZ
    rows = jnp.sum(
        jnp.where(target_z[None, :, None] == jnp.arange(NZ)[None, None, :], mine[:, None, :], 0),
        axis=2,
    )
    stay = len(STAY)
    moving = take_rows(cache, rows[:, stay:].T.reshape(-1), (4, 4, 2, 2))
    moving, staying = lax.optimization_barrier((moving, rows[:, :stay].reshape(-1)))
    (here,) = take_rows(cache, staying, (NX * stay,))
    here = over_x(here.reshape(NX, stay, PLEN, 2 * HD))
    up3, down3, up4, down4 = moving
    up3 = along_z(up3, 1)
    down3 = along_z(down3, -1)
    up4 = along_z(up4, 2)
    down4 = along_z(down4, -2)
    up3, down3, up4, down4, q_own, out_weight = lax.optimization_barrier(
        (up3, down3, up4, down4, q_own, out_weight)
    )
    q_up = along_z(q_own, -1)
    q_down = along_z(q_own, 1)
    q_up2 = along_z(q_up, -1)
    q_down2 = along_z(q_down, 1)
    weight = lax.all_gather(out_weight, "z", axis=1, tiled=True)
    moved = jnp.stack([up3, down3, jnp.concatenate([up4, down4], axis=0)], axis=1)
    moved, here = lax.optimization_barrier((moved, here))
    moved = over_x(moved)

    slots = [(d, i, 0, k) for k, d in enumerate(STAY[:3]) for i in range(NX)]
    slots += [(d, i, 0, k) for k, d in enumerate(STAY[3:]) for i in range(NX)]
    slots += [(2, i, -1, 0) for i in range(NX)]
    slots += [(-2, i, 1, 1) for i in range(NX)]
    slots += [(2, i, -2, 0) for i in range(NX)]
    slots = jnp.array(slots, jnp.int32)
    last = jnp.arange(slots.shape[0]) >= slots.shape[0] - NX
    turn = jnp.where(last & (x >= 2), -1, 1)
    slot_question = (z + slots[:, 0] * turn) % NZ
    slot_owner = slots[:, 1] * NZ + (z + slots[:, 2] * turn) % NZ
    base = per_device * jnp.where(turn < 0, 1, slots[:, 3])
    column = lax.dynamic_index_in_dim(owners.reshape(NX, NZ, -1), x, 0, keepdims=False)
    number = jnp.arange(column.shape[1], dtype=jnp.int32) // TOPP + 1
    hit = (slot_question[:, None, None] == jnp.arange(NZ)[None, :, None]) & (
        slot_owner[:, None, None] == column[None, :, :]
    )
    tags = jnp.sum(jnp.where(hit, number[None, None, :], 0), axis=(1, 2)) - 1
    tags = jnp.where(tags < 0, -1, tags + base)

    split = NX * stay
    near = attention(
        near_kernel,
        "near",
        tags[: 3 * NX],
        here,
        [own, jnp.concatenate([q_own, q_up, q_down])],
        per_device,
        3,
        3 * NX,
        10,
    )
    near, q_up2, q_down2 = lax.optimization_barrier((near, q_up2, q_down2))
    own_part, near_up, near_down = near
    home_up = along_z(near_up, 1)
    home_down = along_z(near_down, -1)
    q_far = jnp.concatenate([q_up2, q_down2])
    far = attention(
        far_kernel,
        "far",
        tags[3 * NX : split],
        here,
        [q_far],
        per_device,
        2,
        2 * NX,
        6,
    )
    weight, moved, far, home_up, home_down = lax.optimization_barrier(
        (weight, moved, far, home_up, home_down)
    )
    before = along_x(weight, 1)
    after = along_x(weight, -1)
    far_up, far_down = attention(
        move_kernel,
        "move",
        tags[split:],
        moved,
        [q_far, *far],
        per_device,
        2,
        3 * NX,
        9,
    )
    far_up = along_z(far_up, 2)
    far_down = along_z(far_down, -2)
    before, after, far_up, far_down = lax.optimization_barrier((before, after, far_up, far_down))
    context = in_vmem(
        last_kernel,
        "last",
        jax.ShapeDtypeStruct(queries.shape, jnp.bfloat16),
        own_part,
        home_up,
        home_down,
        far_up,
        far_down,
    )
    core = lax.axis_index("core")
    half = weight.shape[0] // 2
    weights = (weight, before, after, along_x(before[:half], 1), along_x(after[half:], -1))
    theirs = project(context, weights, 1 - core, x, "theirs")
    theirs = lax.ppermute(theirs, "core", [(0, 1), (1, 0)])
    ours = project(context, weights, core, x, "ours")
    chip = (ours.astype(jnp.float32) + theirs.astype(jnp.float32)).astype(jnp.bfloat16)
    chips = lax.all_to_all(chip, "y", split_axis=0, concat_axis=0, tiled=True)
    return jnp.sum(chips.astype(jnp.float32), axis=0).astype(jnp.bfloat16)


def solution(mesh):
    grid = Mesh(mesh.devices.reshape(NX, NZ, NY, NC), ("x", "z", "y", "core"))
    on_pass, on_head = ("x", "z"), ("y", "core")
    in_specs = (
        P(on_pass, on_head),
        P(on_pass, on_head, None),
        P(on_pass, None, on_head, None),
        P(on_head, on_pass),
        P(),
        P(),
        P(),
    )
    out_specs = P(on_pass, on_head)
    return jax.shard_map(body, mesh=grid, in_specs=in_specs, out_specs=out_specs, check_vma=False)
```

```python
import functools
import math

import jax
import jax.numpy as jnp
from jax import lax
from jax.experimental import pallas as pl
from jax.experimental.pallas import tpu as pltpu
from jax.sharding import Mesh, PartitionSpec as P

HD = 128
GROUP = 8
LQ = 128
PLEN = 512
TOPP = 8
NX, NZ, NY, NC = 4, 8, 4, 2
ROWS = GROUP * LQ
SCALE = math.log2(math.e) / math.sqrt(HD)
NEG = -1e30
WIDTH = 512
PACK = 16
VMEM_LIMIT = 50 << 20

STAY = (0, 1, -1, 2, -2)
MOVE = (3, -3, 4)


def request_tables(lists, passage_slot, question_slot, per_device, pass_dev):
    slot_count = question_slot.shape[0]
    slot_ids = jnp.arange(slot_count, dtype=jnp.int32)
    holder = (question_slot[None, :] == slot_ids[:, None]).astype(jnp.int32)
    chosen = jnp.sum(holder[:, :, None] * lists[None, :, :], axis=1)
    catalog = jnp.arange(passage_slot.shape[0], dtype=jnp.int32)
    picked = (chosen[:, :, None] == catalog[None, None, :]).astype(jnp.int32)
    cache_rows = jnp.sum(picked * passage_slot[None, None, :], axis=2)
    cache_rows = cache_rows.reshape(slot_count // per_device, per_device * TOPP)
    return cache_rows // pass_dev, cache_rows % pass_dev


def row_copies(rows_ref, cache_ref, *refs):
    outs, (buffer, read_sems, write_sems) = refs[:-3], refs[-3:]
    places = [out_ref.at[i] for out_ref in outs for i in range(out_ref.shape[0])]
    reads, writes = [], []
    for n, place in enumerate(places):
        reads.append(
            pltpu.make_async_copy(cache_ref.at[rows_ref[n]], buffer.at[n], read_sems.at[n])
        )
        writes.append(pltpu.make_async_copy(buffer.at[n], place, write_sems.at[n]))
    for read in reads:
        read.start()
    for read, write in zip(reads, writes):
        read.wait()
        write.start()
    for write in writes:
        write.wait()


def take_rows(cache, rows, counts):
    anywhere = pl.BlockSpec(memory_space=pl.ANY)
    total = sum(counts)
    return pl.pallas_call(
        row_copies,
        out_shape=tuple(jax.ShapeDtypeStruct((n,) + cache.shape[1:], cache.dtype) for n in counts),
        in_specs=[pl.BlockSpec(memory_space=pltpu.SMEM), anywhere],
        out_specs=(anywhere,) * len(counts),
        scratch_shapes=[
            pltpu.VMEM((total,) + cache.shape[1:], cache.dtype),
            pltpu.SemaphoreType.DMA((total,)),
            pltpu.SemaphoreType.DMA((total,)),
        ],
        compiler_params=pltpu.CompilerParams(vmem_limit_bytes=VMEM_LIMIT),
        name="take_rows",
    )(rows, cache)


def absorb(keys, values_t, query_ref, group, cols, acc, top, total, causal=False):
    scores = lax.dot_general(
        keys,
        query_ref[group, cols, :],
        (((1,), (1,)), ((), ())),
        preferred_element_type=jnp.float32,
    )
    if causal:
        key = lax.broadcasted_iota(jnp.int32, scores.shape, 0)
        token = lax.broadcasted_iota(jnp.int32, scores.shape, 1)
        scores = jnp.where(key <= token, scores, NEG)
    old = top[group, :, cols]
    new = jnp.maximum(old, jnp.max(scores, axis=0, keepdims=True))
    weights = jnp.exp2((scores - new) * SCALE)
    keep = jnp.exp2((old - new) * SCALE)
    top[group, :, cols] = new
    total[group, :, cols] = total[group, :, cols] * keep + jnp.sum(weights, axis=0, keepdims=True)
    acc[group, :, cols] = acc[group, :, cols] * keep + jnp.dot(
        values_t, weights.astype(jnp.bfloat16), preferred_element_type=jnp.float32
    )


def start(acc, top, total):
    acc[...] = jnp.zeros_like(acc)
    top[...] = jnp.full_like(top, NEG)
    total[...] = jnp.zeros_like(total)


def fetches(items_ref, picks, buffer, sems):
    return [
        pltpu.make_async_copy(items_ref.at[i, k], buffer.at[n], sems.at[n])
        for n, (i, k) in enumerate(picks)
    ]


def absorb_all(tag_ref, copies, buffer, query_ref, acc, top, total):
    for copy in copies:
        copy.wait()

    def step(i, carry):
        tag = tag_ref[i]

        @pl.when(tag >= 0)
        def _():
            keys = buffer[i, :, 0:HD]
            values_t = buffer[i, :, HD : 2 * HD].T
            for part in range(ROWS // WIDTH):
                cols = pl.ds(part * WIDTH, WIDTH)
                absorb(keys, values_t, query_ref, tag, cols, acc, top, total)

        return carry

    lax.fori_loop(0, len(copies), step, 0)


def pack(level):
    parts = []
    for _ in range(3):
        part = level.astype(jnp.bfloat16).astype(jnp.float32)
        parts.append(part)
        level = level - part
    parts.append(jnp.zeros((PACK - 3, level.shape[1]), jnp.float32))
    return jnp.concatenate(parts, axis=0).astype(jnp.bfloat16)


def store(out_ref, j, mixed, level):
    out_ref[j, 0:HD, :] = mixed.astype(jnp.bfloat16)
    out_ref[j, HD : HD + PACK, :] = pack(level)


def load(ref, j):
    parts = ref[j, HD : HD + PACK, :].astype(jnp.float32)
    level = parts[0:1] + parts[1:2] + parts[2:3]
    return ref[j, 0:HD, :].astype(jnp.float32), level


def state_of(group, acc, top, total):
    sums = jnp.maximum(total[group], 1e-30)
    return acc[group] / sums, top[group] * SCALE + jnp.log2(sums)


def merge(pairs):
    level = pairs[0][1]
    for _, other in pairs[1:]:
        level = jnp.maximum(level, other)
    shares = [jnp.exp2(l - level) for _, l in pairs]
    whole = functools.reduce(jnp.add, shares)
    mixed = functools.reduce(jnp.add, [o * s for (o, _), s in zip(pairs, shares)])
    return mixed / whole, level + jnp.log2(whole)


def near_kernel(tags, here, own, query, o0, o1, o2, buffer, sems, *state):
    copies = fetches(here, [(i, k) for k in range(3) for i in range(NX)], buffer, sems)
    for copy in copies:
        copy.start()
    start(*state)
    n = o0.shape[0]
    for j in range(n):
        rows = slice(j * LQ, (j + 1) * LQ)
        keys = own[rows, 0:HD]
        values_t = own[rows, HD : 2 * HD].T

        def head(part, carry, j=j, keys=keys, values_t=values_t):
            cols = pl.ds(pl.multiple_of(part * LQ, LQ), LQ)
            absorb(keys, values_t, query, j, cols, *state, causal=True)
            return carry

        lax.fori_loop(0, GROUP, head, 0)
    absorb_all(tags, copies, buffer, query, *state)
    for k, out_ref in enumerate((o0, o1, o2)):
        for j in range(n):
            store(out_ref, j, *state_of(k * n + j, *state))


def far_kernel(tags, here, query, o_up, o_down, buffer, sems, *state):
    copies = fetches(here, [(i, k) for k in (3, 4) for i in range(NX)], buffer, sems)
    for copy in copies:
        copy.start()
    start(*state)
    absorb_all(tags, copies, buffer, query, *state)
    n = o_up.shape[0]
    for j in range(n):
        store(o_up, j, *state_of(j, *state))
        store(o_down, j, *state_of(n + j, *state))


def move_kernel(tags, moved, query, so_far_up, so_far_down, o_up, o_down, buffer, sems, *state):
    copies = fetches(moved, [(i, k) for k in range(3) for i in range(NX)], buffer, sems)
    for copy in copies:
        copy.start()
    start(*state)
    absorb_all(tags, copies, buffer, query, *state)
    n = o_up.shape[0]
    for j in range(n):
        store(o_up, j, *merge([state_of(j, *state), load(so_far_up, j)]))
        store(o_down, j, *merge([state_of(n + j, *state), load(so_far_down, j)]))


def attention(kernel, name, tags, items, arrays, n, groups, slots, work):
    vmem = pl.BlockSpec(memory_space=pltpu.VMEM)
    return pl.pallas_call(
        kernel,
        out_shape=(jax.ShapeDtypeStruct((n, HD + PACK, ROWS), jnp.bfloat16),) * groups,
        in_specs=[pl.BlockSpec(memory_space=pltpu.SMEM), pl.BlockSpec(memory_space=pl.ANY)]
        + [vmem] * len(arrays),
        out_specs=(vmem,) * groups,
        scratch_shapes=[
            pltpu.VMEM((slots, PLEN, 2 * HD), jnp.bfloat16),
            pltpu.SemaphoreType.DMA((slots,)),
            pltpu.VMEM((groups * n, HD, ROWS), jnp.float32),
            pltpu.VMEM((groups * n, 1, ROWS), jnp.float32),
            pltpu.VMEM((groups * n, 1, ROWS), jnp.float32),
        ],
        compiler_params=pltpu.CompilerParams(vmem_limit_bytes=VMEM_LIMIT),
        cost_estimate=pl.CostEstimate(
            flops=work * ROWS * PLEN,
            bytes_accessed=work * PLEN,
            transcendentals=0,
        ),
        name=name,
    )(tags, items, *arrays)


def last_kernel(*refs):
    parts, out_ref = refs[:-1], refs[-1]
    for j in range(parts[0].shape[0]):
        mixed, _ = merge([load(part, j) for part in parts])
        for head in range(GROUP):
            cols = slice(head * LQ, (head + 1) * LQ)
            out_ref[j * LQ : (j + 1) * LQ, head * HD : (head + 1) * HD] = mixed[:, cols].T.astype(
                jnp.bfloat16
            )


def project_kernel(place, context_ref, own_ref, before_ref, after_ref, top_ref, bottom_ref, out_ref):
    x = place[1]

    def put(index, products):
        out_ref[lax.rem(index, NX)] = functools.reduce(jnp.add, products).astype(jnp.bfloat16)

    def times(cols, weight_ref):
        return jnp.dot(
            context_ref[:, cols], weight_ref[...], preferred_element_type=jnp.float32
        )

    half = top_ref.shape[0]
    everything = slice(None)
    put(x, [times(everything, own_ref)])
    put(x + NX - 1, [times(everything, before_ref)])
    put(x + 1, [times(everything, after_ref)])
    put(x + 2, [times(slice(0, half), top_ref), times(slice(half, None), bottom_ref)])


def project(context, weights, core, x, name):
    tile = 256
    width = weights[0].shape[1] // NC
    steps = width // tile

    def tiles(weight):
        return pl.BlockSpec((weight.shape[0], tile), lambda i, place: (0, steps * place[0] + i))

    return pl.pallas_call(
        project_kernel,
        out_shape=jax.ShapeDtypeStruct((NX, context.shape[0], width), jnp.bfloat16),
        grid_spec=pltpu.PrefetchScalarGridSpec(
            num_scalar_prefetch=1,
            grid=(steps,),
            in_specs=[pl.BlockSpec(context.shape, lambda i, place: (0, 0))]
            + [tiles(weight) for weight in weights],
            out_specs=pl.BlockSpec((NX, context.shape[0], tile), lambda i, place: (0, 0, i)),
        ),
        compiler_params=pltpu.CompilerParams(vmem_limit_bytes=VMEM_LIMIT),
        cost_estimate=pl.CostEstimate(
            flops=2 * context.shape[0] * context.shape[1] * width * NX,
            bytes_accessed=context.shape[1] * width * NX * 2,
            transcendentals=0,
        ),
        name=name,
    )(jnp.stack([core, x]), context, *weights)


def in_vmem(kernel, name, out, *arrays):
    vmem = pl.BlockSpec(memory_space=pltpu.VMEM)
    return pl.pallas_call(
        kernel,
        out_shape=out,
        in_specs=[vmem] * len(arrays),
        out_specs=jax.tree.map(lambda _: vmem, out),
        compiler_params=pltpu.CompilerParams(vmem_limit_bytes=VMEM_LIMIT),
        name=name,
    )(*arrays)


def along_z(array, shift):
    return lax.ppermute(array, "z", [(i, (i + shift) % NZ) for i in range(NZ)])


def along_x(array, shift):
    return lax.ppermute(array, "x", [(i, (i + shift) % NX) for i in range(NX)])


def over_x(items):
    return lax.all_to_all(items, "x", split_axis=0, concat_axis=0, tiled=True)


def body(queries, own_kv, passage_cache, out_weight, lists, passage_slot, question_slot):
    x, z = lax.axis_index("x"), lax.axis_index("z")
    per_device = queries.shape[0] // LQ
    pass_dev = passage_cache.shape[0]
    cache = passage_cache.reshape(pass_dev, PLEN, 2 * HD)
    own = own_kv.reshape(per_device * LQ, 2 * HD)

    q_own = queries.reshape(per_device, LQ, GROUP, HD).transpose(0, 2, 1, 3)
    q_own = q_own.reshape(per_device, ROWS, HD)
    owners, local_rows = request_tables(lists, passage_slot, question_slot, per_device, pass_dev)
    mine = jnp.sum(jnp.where(owners == x * NZ + z, local_rows, 0), axis=1).reshape(NX, NZ)
    target_z = (z + jnp.array(STAY + MOVE, jnp.int32)) % NZ
    rows = jnp.sum(
        jnp.where(target_z[None, :, None] == jnp.arange(NZ)[None, None, :], mine[:, None, :], 0),
        axis=2,
    )
    stay = len(STAY)
    moving = take_rows(cache, rows[:, stay:].T.reshape(-1), (4, 4, 2, 2))
    moving, staying = lax.optimization_barrier((moving, rows[:, :stay].reshape(-1)))
    (here,) = take_rows(cache, staying, (NX * stay,))
    q_up = along_z(q_own, -1)
    q_down = along_z(q_own, 1)
    here, q_up, q_down = lax.optimization_barrier((here, q_up, q_down))
    here = over_x(here.reshape(NX, stay, PLEN, 2 * HD))
    up3, down3, up4, down4 = moving
    up3 = along_z(up3, 1)
    down3 = along_z(down3, -1)
    up4 = along_z(up4, 2)
    down4 = along_z(down4, -2)
    up3, down3, up4, down4, q_up, q_down = lax.optimization_barrier(
        (up3, down3, up4, down4, q_up, q_down)
    )
    q_up2 = along_z(q_up, -1)
    q_down2 = along_z(q_down, 1)
    weight = lax.all_gather(out_weight, "z", axis=1, tiled=True)
    moved = jnp.stack([up3, down3, jnp.concatenate([up4, down4], axis=0)], axis=1)
    moved, here = lax.optimization_barrier((moved, here))
    moved = over_x(moved)

    slots = [(d, i, 0, k) for k, d in enumerate(STAY[:3]) for i in range(NX)]
    slots += [(d, i, 0, k) for k, d in enumerate(STAY[3:]) for i in range(NX)]
    slots += [(2, i, -1, 0) for i in range(NX)]
    slots += [(-2, i, 1, 1) for i in range(NX)]
    slots += [(2, i, -2, 0) for i in range(NX)]
    slots = jnp.array(slots, jnp.int32)
    last = jnp.arange(slots.shape[0]) >= slots.shape[0] - NX
    turn = jnp.where(last & (x >= 2), -1, 1)
    slot_question = (z + slots[:, 0] * turn) % NZ
    slot_owner = slots[:, 1] * NZ + (z + slots[:, 2] * turn) % NZ
    base = per_device * jnp.where(turn < 0, 1, slots[:, 3])
    column = lax.dynamic_index_in_dim(owners.reshape(NX, NZ, -1), x, 0, keepdims=False)
    number = jnp.arange(column.shape[1], dtype=jnp.int32) // TOPP + 1
    hit = (slot_question[:, None, None] == jnp.arange(NZ)[None, :, None]) & (
        slot_owner[:, None, None] == column[None, :, :]
    )
    tags = jnp.sum(jnp.where(hit, number[None, None, :], 0), axis=(1, 2)) - 1
    tags = jnp.where(tags < 0, -1, tags + base)

    split = NX * stay
    near = attention(
        near_kernel,
        "near",
        tags[: 3 * NX],
        here,
        [own, jnp.concatenate([q_own, q_up, q_down])],
        per_device,
        3,
        3 * NX,
        10,
    )
    near, q_up2, q_down2 = lax.optimization_barrier((near, q_up2, q_down2))
    own_part, near_up, near_down = near
    home_up = along_z(near_up, 1)
    home_down = along_z(near_down, -1)
    q_far = jnp.concatenate([q_up2, q_down2])
    far = attention(
        far_kernel,
        "far",
        tags[3 * NX : split],
        here,
        [q_far],
        per_device,
        2,
        2 * NX,
        6,
    )
    weight, moved, far, home_up, home_down = lax.optimization_barrier(
        (weight, moved, far, home_up, home_down)
    )
    before = along_x(weight, 1)
    after = along_x(weight, -1)
    far_up, far_down = attention(
        move_kernel,
        "move",
        tags[split:],
        moved,
        [q_far, *far],
        per_device,
        2,
        3 * NX,
        9,
    )
    far_up = along_z(far_up, 2)
    far_down = along_z(far_down, -2)
    before, after, far_up, far_down = lax.optimization_barrier((before, after, far_up, far_down))
    context = in_vmem(
        last_kernel,
        "last",
        jax.ShapeDtypeStruct(queries.shape, jnp.bfloat16),
        own_part,
        home_up,
        home_down,
        far_up,
        far_down,
    )
    core = lax.axis_index("core")
    half = weight.shape[0] // 2
    weights = (weight, before, after, along_x(before[:half], 1), along_x(after[half:], -1))
    theirs = project(context, weights, 1 - core, x, "theirs")
    theirs = lax.ppermute(theirs, "core", [(0, 1), (1, 0)])
    ours = project(context, weights, core, x, "ours")
    chip = (ours.astype(jnp.float32) + theirs.astype(jnp.float32)).astype(jnp.bfloat16)
    chips = lax.all_to_all(chip, "y", split_axis=0, concat_axis=0, tiled=True)
    return jnp.sum(chips.astype(jnp.float32), axis=0).astype(jnp.bfloat16)


def solution(mesh):
    grid = Mesh(mesh.devices.reshape(NX, NZ, NY, NC), ("x", "z", "y", "core"))
    on_pass, on_head = ("x", "z"), ("y", "core")
    in_specs = (
        P(on_pass, on_head),
        P(on_pass, on_head, None),
        P(on_pass, None, on_head, None),
        P(on_head, on_pass),
        P(),
        P(),
        P(),
    )
    out_specs = P(on_pass, on_head)
    return jax.shard_map(body, mesh=grid, in_specs=in_specs, out_specs=out_specs, check_vma=False)
```

```python
import functools
import math

import jax
import jax.numpy as jnp
from jax import lax
from jax.experimental import pallas as pl
from jax.experimental.pallas import tpu as pltpu
from jax.sharding import Mesh, PartitionSpec as P

HD = 128
GROUP = 8
LQ = 128
PLEN = 512
TOPP = 8
NX, NZ, NY, NC = 4, 8, 4, 2
ROWS = GROUP * LQ
SCALE = math.log2(math.e) / math.sqrt(HD)
NEG = -1e30
WIDTH = 1024
PACK = 16
VMEM_LIMIT = 50 << 20

STAY = (0, 1, -1, 2, -2)
MOVE = (3, -3, 4)


def request_tables(lists, passage_slot, question_slot, per_device, pass_dev):
    slot_count = question_slot.shape[0]
    slot_ids = jnp.arange(slot_count, dtype=jnp.int32)
    holder = (question_slot[None, :] == slot_ids[:, None]).astype(jnp.int32)
    chosen = jnp.sum(holder[:, :, None] * lists[None, :, :], axis=1)
    catalog = jnp.arange(passage_slot.shape[0], dtype=jnp.int32)
    picked = (chosen[:, :, None] == catalog[None, None, :]).astype(jnp.int32)
    cache_rows = jnp.sum(picked * passage_slot[None, None, :], axis=2)
    cache_rows = cache_rows.reshape(slot_count // per_device, per_device * TOPP)
    return cache_rows // pass_dev, cache_rows % pass_dev


def row_copies(rows_ref, cache_ref, *refs):
    outs, (buffer, read_sems, write_sems) = refs[:-3], refs[-3:]
    places = [out_ref.at[i] for out_ref in outs for i in range(out_ref.shape[0])]
    reads, writes = [], []
    for n, place in enumerate(places):
        reads.append(
            pltpu.make_async_copy(cache_ref.at[rows_ref[n]], buffer.at[n], read_sems.at[n])
        )
        writes.append(pltpu.make_async_copy(buffer.at[n], place, write_sems.at[n]))
    for read in reads:
        read.start()
    for read, write in zip(reads, writes):
        read.wait()
        write.start()
    for write in writes:
        write.wait()


def take_rows(cache, rows, counts):
    anywhere = pl.BlockSpec(memory_space=pl.ANY)
    total = sum(counts)
    return pl.pallas_call(
        row_copies,
        out_shape=tuple(jax.ShapeDtypeStruct((n,) + cache.shape[1:], cache.dtype) for n in counts),
        in_specs=[pl.BlockSpec(memory_space=pltpu.SMEM), anywhere],
        out_specs=(anywhere,) * len(counts),
        scratch_shapes=[
            pltpu.VMEM((total,) + cache.shape[1:], cache.dtype),
            pltpu.SemaphoreType.DMA((total,)),
            pltpu.SemaphoreType.DMA((total,)),
        ],
        compiler_params=pltpu.CompilerParams(vmem_limit_bytes=VMEM_LIMIT),
        name="take_rows",
    )(rows, cache)


def absorb(keys, values_t, query_ref, group, cols, acc, top, causal=False):
    scores = lax.dot_general(
        keys,
        query_ref[group, cols, :],
        (((1,), (1,)), ((), ())),
        preferred_element_type=jnp.float32,
    )
    if causal:
        key = lax.broadcasted_iota(jnp.int32, scores.shape, 0)
        token = lax.broadcasted_iota(jnp.int32, scores.shape, 1)
        scores = jnp.where(key <= token, scores, NEG)
    old = top[group, :, cols]
    new = jnp.maximum(old, jnp.max(scores, axis=0, keepdims=True))
    weights = jnp.exp2((scores - new) * SCALE)
    keep = jnp.exp2((old - new) * SCALE)
    top[group, :, cols] = new
    acc[group, :, cols] = acc[group, :, cols] * keep + jnp.dot(
        values_t, weights.astype(jnp.bfloat16), preferred_element_type=jnp.float32
    )


def start(acc, top):
    acc[...] = jnp.zeros_like(acc)
    top[...] = jnp.full_like(top, NEG)


def with_ones(values):
    ones = jnp.ones((PACK, values.shape[0]), values.dtype)
    return jnp.concatenate([values.T, ones], axis=0)


def fetches(items_ref, picks, buffer, sems):
    return [
        pltpu.make_async_copy(items_ref.at[i, k], buffer.at[n], sems.at[n])
        for n, (i, k) in enumerate(picks)
    ]


def absorb_all(tag_ref, copies, buffer, query_ref, acc, top):
    for copy in copies:
        copy.wait()

    def step(i, carry):
        tag = tag_ref[i]

        @pl.when(tag >= 0)
        def _():
            keys = buffer[i, :, 0:HD]
            values_t = with_ones(buffer[i, :, HD : 2 * HD])
            for part in range(ROWS // WIDTH):
                cols = pl.ds(part * WIDTH, WIDTH)
                absorb(keys, values_t, query_ref, tag, cols, acc, top)

        return carry

    lax.fori_loop(0, len(copies), step, 0)


def pack(level):
    parts = []
    for _ in range(3):
        part = level.astype(jnp.bfloat16).astype(jnp.float32)
        parts.append(part)
        level = level - part
    parts.append(jnp.zeros((PACK - 3, level.shape[1]), jnp.float32))
    return jnp.concatenate(parts, axis=0).astype(jnp.bfloat16)


def store(out_ref, j, mixed, level):
    out_ref[j, 0:HD, :] = mixed.astype(jnp.bfloat16)
    out_ref[j, HD : HD + PACK, :] = pack(level)


def load(ref, j):
    parts = ref[j, HD : HD + PACK, :].astype(jnp.float32)
    level = parts[0:1] + parts[1:2] + parts[2:3]
    return ref[j, 0:HD, :].astype(jnp.float32), level


def state_of(group, acc, top):
    sums = jnp.maximum(acc[group, HD : HD + 1, :], 1e-30)
    return acc[group, 0:HD, :] / sums, top[group] * SCALE + jnp.log2(sums)


def merge(pairs):
    level = pairs[0][1]
    for _, other in pairs[1:]:
        level = jnp.maximum(level, other)
    shares = [jnp.exp2(l - level) for _, l in pairs]
    whole = functools.reduce(jnp.add, shares)
    mixed = functools.reduce(jnp.add, [o * s for (o, _), s in zip(pairs, shares)])
    return mixed / whole, level + jnp.log2(whole)


def near_kernel(tags, here, own, query, o0, o1, o2, buffer, sems, *state):
    copies = fetches(here, [(i, k) for k in range(3) for i in range(NX)], buffer, sems)
    for copy in copies:
        copy.start()
    start(*state)
    n = o0.shape[0]
    for j in range(n):
        rows = slice(j * LQ, (j + 1) * LQ)
        keys = own[rows, 0:HD]
        values_t = with_ones(own[rows, HD : 2 * HD])

        def head(part, carry, j=j, keys=keys, values_t=values_t):
            cols = pl.ds(pl.multiple_of(part * LQ, LQ), LQ)
            absorb(keys, values_t, query, j, cols, *state, causal=True)
            return carry

        lax.fori_loop(0, GROUP, head, 0)
    absorb_all(tags, copies, buffer, query, *state)
    for k, out_ref in enumerate((o0, o1, o2)):
        for j in range(n):
            store(out_ref, j, *state_of(k * n + j, *state))


def far_kernel(tags, here, query, o_up, o_down, buffer, sems, *state):
    copies = fetches(here, [(i, k) for k in (3, 4) for i in range(NX)], buffer, sems)
    for copy in copies:
        copy.start()
    start(*state)
    absorb_all(tags, copies, buffer, query, *state)
    n = o_up.shape[0]
    for j in range(n):
        store(o_up, j, *state_of(j, *state))
        store(o_down, j, *state_of(n + j, *state))


def move_kernel(tags, moved, query, so_far_up, so_far_down, o_up, o_down, buffer, sems, *state):
    copies = fetches(moved, [(i, k) for k in range(3) for i in range(NX)], buffer, sems)
    for copy in copies:
        copy.start()
    start(*state)
    absorb_all(tags, copies, buffer, query, *state)
    n = o_up.shape[0]
    for j in range(n):
        store(o_up, j, *merge([state_of(j, *state), load(so_far_up, j)]))
        store(o_down, j, *merge([state_of(n + j, *state), load(so_far_down, j)]))


def attention(kernel, name, tags, items, arrays, n, groups, slots, work):
    vmem = pl.BlockSpec(memory_space=pltpu.VMEM)
    return pl.pallas_call(
        kernel,
        out_shape=(jax.ShapeDtypeStruct((n, HD + PACK, ROWS), jnp.bfloat16),) * groups,
        in_specs=[pl.BlockSpec(memory_space=pltpu.SMEM), pl.BlockSpec(memory_space=pl.ANY)]
        + [vmem] * len(arrays),
        out_specs=(vmem,) * groups,
        scratch_shapes=[
            pltpu.VMEM((slots, PLEN, 2 * HD), jnp.bfloat16),
            pltpu.SemaphoreType.DMA((slots,)),
            pltpu.VMEM((groups * n, HD + PACK, ROWS), jnp.float32),
            pltpu.VMEM((groups * n, 1, ROWS), jnp.float32),
        ],
        compiler_params=pltpu.CompilerParams(vmem_limit_bytes=VMEM_LIMIT),
        cost_estimate=pl.CostEstimate(
            flops=work * ROWS * PLEN,
            bytes_accessed=work * PLEN,
            transcendentals=0,
        ),
        name=name,
    )(tags, items, *arrays)


def last_kernel(*refs):
    parts, out_ref = refs[:-1], refs[-1]
    for j in range(parts[0].shape[0]):
        mixed, _ = merge([load(part, j) for part in parts])
        for head in range(GROUP):
            cols = slice(head * LQ, (head + 1) * LQ)
            out_ref[j * LQ : (j + 1) * LQ, head * HD : (head + 1) * HD] = mixed[:, cols].T.astype(
                jnp.bfloat16
            )


def project_kernel(core_ref, context_ref, weight_ref, out_ref):
    out_ref[0] = jnp.dot(
        context_ref[...], weight_ref[...], preferred_element_type=jnp.float32
    ).astype(jnp.bfloat16)


def project(context, weight, core, name):
    width = weight.shape[1] // (NY * NC)
    return pl.pallas_call(
        project_kernel,
        out_shape=jax.ShapeDtypeStruct((NY, context.shape[0], width), jnp.bfloat16),
        grid_spec=pltpu.PrefetchScalarGridSpec(
            num_scalar_prefetch=1,
            grid=(NY,),
            in_specs=[
                pl.BlockSpec(context.shape, lambda i, core_ref: (0, 0)),
                pl.BlockSpec(
                    (weight.shape[0], width), lambda i, core_ref: (0, NC * i + core_ref[0])
                ),
            ],
            out_specs=pl.BlockSpec((1, context.shape[0], width), lambda i, core_ref: (i, 0, 0)),
        ),
        compiler_params=pltpu.CompilerParams(vmem_limit_bytes=VMEM_LIMIT),
        cost_estimate=pl.CostEstimate(
            flops=2 * context.shape[0] * weight.shape[0] * width * NY,
            bytes_accessed=weight.shape[0] * width * NY * 2,
            transcendentals=0,
        ),
        name=name,
    )(core.reshape(1), context, weight)


def in_vmem(kernel, name, out, *arrays):
    vmem = pl.BlockSpec(memory_space=pltpu.VMEM)
    return pl.pallas_call(
        kernel,
        out_shape=out,
        in_specs=[vmem] * len(arrays),
        out_specs=jax.tree.map(lambda _: vmem, out),
        compiler_params=pltpu.CompilerParams(vmem_limit_bytes=VMEM_LIMIT),
        name=name,
    )(*arrays)


def along_z(array, shift):
    return lax.ppermute(array, "z", [(i, (i + shift) % NZ) for i in range(NZ)])


def over_x(items):
    return lax.all_to_all(items, "x", split_axis=0, concat_axis=0, tiled=True)


def body(queries, own_kv, passage_cache, out_weight, lists, passage_slot, question_slot):
    x, z = lax.axis_index("x"), lax.axis_index("z")
    per_device = queries.shape[0] // LQ
    pass_dev = passage_cache.shape[0]
    cache = passage_cache.reshape(pass_dev, PLEN, 2 * HD)
    own = own_kv.reshape(per_device * LQ, 2 * HD)

    q_own = queries.reshape(per_device, LQ, GROUP, HD).transpose(0, 2, 1, 3)
    q_own = q_own.reshape(per_device, ROWS, HD)
    owners, local_rows = request_tables(lists, passage_slot, question_slot, per_device, pass_dev)
    mine = jnp.sum(jnp.where(owners == x * NZ + z, local_rows, 0), axis=1).reshape(NX, NZ)
    target_z = (z + jnp.array(STAY + MOVE, jnp.int32)) % NZ
    rows = jnp.sum(
        jnp.where(target_z[None, :, None] == jnp.arange(NZ)[None, None, :], mine[:, None, :], 0),
        axis=2,
    )
    stay = len(STAY)
    moving = take_rows(cache, rows[:, stay:].T.reshape(-1), (4, 4, 2, 2))
    moving, staying = lax.optimization_barrier((moving, rows[:, :stay].reshape(-1)))
    (here,) = take_rows(cache, staying, (NX * stay,))
    q_up = along_z(q_own, -1)
    q_down = along_z(q_own, 1)
    here, q_up, q_down = lax.optimization_barrier((here, q_up, q_down))
    here = over_x(here.reshape(NX, stay, PLEN, 2 * HD))
    up3, down3, up4, down4 = moving
    up3 = along_z(up3, 1)
    down3 = along_z(down3, -1)
    up4 = along_z(up4, 2)
    down4 = along_z(down4, -2)
    up3, down3, up4, down4, q_up, q_down = lax.optimization_barrier(
        (up3, down3, up4, down4, q_up, q_down)
    )
    q_up2 = along_z(q_up, -1)
    q_down2 = along_z(q_down, 1)
    weight = lax.all_gather(out_weight, "z", axis=1, tiled=True)
    moved = jnp.stack([up3, down3, jnp.concatenate([up4, down4], axis=0)], axis=1)
    moved, here = lax.optimization_barrier((moved, here))
    moved = over_x(moved)

    slots = [(d, i, 0, k) for k, d in enumerate(STAY[:3]) for i in range(NX)]
    slots += [(d, i, 0, k) for k, d in enumerate(STAY[3:]) for i in range(NX)]
    slots += [(2, i, -1, 0) for i in range(NX)]
    slots += [(-2, i, 1, 1) for i in range(NX)]
    slots += [(2, i, -2, 0) for i in range(NX)]
    slots = jnp.array(slots, jnp.int32)
    last = jnp.arange(slots.shape[0]) >= slots.shape[0] - NX
    turn = jnp.where(last & (x >= 2), -1, 1)
    slot_question = (z + slots[:, 0] * turn) % NZ
    slot_owner = slots[:, 1] * NZ + (z + slots[:, 2] * turn) % NZ
    base = per_device * jnp.where(turn < 0, 1, slots[:, 3])
    column = lax.dynamic_index_in_dim(owners.reshape(NX, NZ, -1), x, 0, keepdims=False)
    number = jnp.arange(column.shape[1], dtype=jnp.int32) // TOPP + 1
    hit = (slot_question[:, None, None] == jnp.arange(NZ)[None, :, None]) & (
        slot_owner[:, None, None] == column[None, :, :]
    )
    tags = jnp.sum(jnp.where(hit, number[None, None, :], 0), axis=(1, 2)) - 1
    tags = jnp.where(tags < 0, -1, tags + base)

    split = NX * stay
    near = attention(
        near_kernel,
        "near",
        tags[: 3 * NX],
        here,
        [own, jnp.concatenate([q_own, q_up, q_down])],
        per_device,
        3,
        3 * NX,
        10,
    )
    near, q_up2, q_down2, weight = lax.optimization_barrier((near, q_up2, q_down2, weight))
    weight = lax.all_gather(weight, "x", axis=1, tiled=True)
    own_part, near_up, near_down = near
    home_up = along_z(near_up, 1)
    home_down = along_z(near_down, -1)
    q_far = jnp.concatenate([q_up2, q_down2])
    far = attention(
        far_kernel,
        "far",
        tags[3 * NX : split],
        here,
        [q_far],
        per_device,
        2,
        2 * NX,
        6,
    )
    moved, far, home_up, home_down = lax.optimization_barrier((moved, far, home_up, home_down))
    far_up, far_down = attention(
        move_kernel,
        "move",
        tags[split:],
        moved,
        [q_far, *far],
        per_device,
        2,
        3 * NX,
        400000,
    )
    far_up = along_z(far_up, 2)
    far_down = along_z(far_down, -2)
    context = in_vmem(
        last_kernel,
        "last",
        jax.ShapeDtypeStruct(queries.shape, jnp.bfloat16),
        own_part,
        home_up,
        home_down,
        far_up,
        far_down,
    )
    core = lax.axis_index("core")
    theirs = project(context, weight, 1 - core, "theirs")
    theirs = lax.ppermute(theirs, "core", [(0, 1), (1, 0)])
    ours = project(context, weight, core, "ours")
    chip = (ours.astype(jnp.float32) + theirs.astype(jnp.float32)).astype(jnp.bfloat16)
    chips = lax.all_to_all(chip, "y", split_axis=0, concat_axis=0, tiled=True)
    return jnp.sum(chips.astype(jnp.float32), axis=0).astype(jnp.bfloat16)


def solution(mesh):
    grid = Mesh(mesh.devices.reshape(NX, NZ, NY, NC), ("x", "z", "y", "core"))
    on_pass, on_head = ("x", "z"), ("y", "core")
    in_specs = (
        P(on_pass, on_head),
        P(on_pass, on_head, None),
        P(on_pass, None, on_head, None),
        P(on_head, on_pass),
        P(),
        P(),
        P(),
    )
    out_specs = P(on_pass, on_head)
    return jax.shard_map(body, mesh=grid, in_specs=in_specs, out_specs=out_specs, check_vma=False)
```

```python
import functools
import math

import jax
import jax.numpy as jnp
from jax import lax
from jax.experimental import pallas as pl
from jax.experimental.pallas import tpu as pltpu
from jax.sharding import Mesh, PartitionSpec as P

HD = 128
GROUP = 8
LQ = 128
PLEN = 512
TOPP = 8
NX, NZ, NY, NC = 4, 8, 4, 2
ROWS = GROUP * LQ
SCALE = math.log2(math.e) / math.sqrt(HD)
NEG = -1e30
WIDTH = 1024
PACK = 16
VMEM_LIMIT = 50 << 20

STAY = (0, 1, -1, 2, -2)
MOVE = (3, -3, 4)


def request_tables(lists, passage_slot, question_slot, per_device, pass_dev):
    slot_count = question_slot.shape[0]
    slot_ids = jnp.arange(slot_count, dtype=jnp.int32)
    holder = (question_slot[None, :] == slot_ids[:, None]).astype(jnp.int32)
    chosen = jnp.sum(holder[:, :, None] * lists[None, :, :], axis=1)
    catalog = jnp.arange(passage_slot.shape[0], dtype=jnp.int32)
    picked = (chosen[:, :, None] == catalog[None, None, :]).astype(jnp.int32)
    cache_rows = jnp.sum(picked * passage_slot[None, None, :], axis=2)
    cache_rows = cache_rows.reshape(slot_count // per_device, per_device * TOPP)
    return cache_rows // pass_dev, cache_rows % pass_dev


def staged(sources, places, buffer, read_sems, write_sems):
    reads, writes = [], []
    for n, (source, place) in enumerate(zip(sources, places)):
        reads.append(pltpu.make_async_copy(source, buffer.at[n], read_sems.at[n]))
        writes.append(pltpu.make_async_copy(buffer.at[n], place, write_sems.at[n]))
    for read in reads:
        read.start()
    for read, write in zip(reads, writes):
        read.wait()
        write.start()
    for write in writes:
        write.wait()


def row_copies(rows_ref, cache_ref, *refs):
    outs, scratch = refs[:-3], refs[-3:]
    places = [out_ref.at[i] for out_ref in outs for i in range(out_ref.shape[0])]
    staged([cache_ref.at[rows_ref[n]] for n in range(len(places))], places, *scratch)


def assemble_copies(up3, down3, up4, down4, out_ref, *scratch):
    sources = [ref.at[i] for ref in (up3, down3, up4, down4) for i in range(ref.shape[0])]
    places = [out_ref.at[i, k] for k in range(3) for i in range(NX)]
    staged(sources, places, *scratch)


def assemble(parts):
    anywhere = pl.BlockSpec(memory_space=pl.ANY)
    shape, dtype = parts[0].shape[1:], parts[0].dtype
    return pl.pallas_call(
        assemble_copies,
        out_shape=jax.ShapeDtypeStruct((NX, 3) + shape, dtype),
        in_specs=[anywhere] * len(parts),
        out_specs=anywhere,
        scratch_shapes=[
            pltpu.VMEM((3 * NX,) + shape, dtype),
            pltpu.SemaphoreType.DMA((3 * NX,)),
            pltpu.SemaphoreType.DMA((3 * NX,)),
        ],
        compiler_params=pltpu.CompilerParams(vmem_limit_bytes=VMEM_LIMIT),
        name="assemble",
    )(*parts)


def take_rows(cache, rows, counts):
    anywhere = pl.BlockSpec(memory_space=pl.ANY)
    total = sum(counts)
    return pl.pallas_call(
        row_copies,
        out_shape=tuple(jax.ShapeDtypeStruct((n,) + cache.shape[1:], cache.dtype) for n in counts),
        in_specs=[pl.BlockSpec(memory_space=pltpu.SMEM), anywhere],
        out_specs=(anywhere,) * len(counts),
        scratch_shapes=[
            pltpu.VMEM((total,) + cache.shape[1:], cache.dtype),
            pltpu.SemaphoreType.DMA((total,)),
            pltpu.SemaphoreType.DMA((total,)),
        ],
        compiler_params=pltpu.CompilerParams(vmem_limit_bytes=VMEM_LIMIT),
        name="take_rows",
    )(rows, cache)


def absorb(keys, values_t, query_ref, group, cols, acc, top, causal=False):
    scores = lax.dot_general(
        keys,
        query_ref[group, cols, :],
        (((1,), (1,)), ((), ())),
        preferred_element_type=jnp.float32,
    )
    if causal:
        key = lax.broadcasted_iota(jnp.int32, scores.shape, 0)
        token = lax.broadcasted_iota(jnp.int32, scores.shape, 1)
        scores = jnp.where(key <= token, scores, NEG)
    old = top[group, :, cols]
    new = jnp.maximum(old, jnp.max(scores, axis=0, keepdims=True))
    weights = jnp.exp2((scores - new) * SCALE)
    keep = jnp.exp2((old - new) * SCALE)
    top[group, :, cols] = new
    acc[group, :, cols] = acc[group, :, cols] * keep + jnp.dot(
        values_t, weights.astype(jnp.bfloat16), preferred_element_type=jnp.float32
    )


def start(acc, top):
    acc[...] = jnp.zeros_like(acc)
    top[...] = jnp.full_like(top, NEG)


def with_ones(values):
    ones = jnp.ones((PACK, values.shape[0]), values.dtype)
    return jnp.concatenate([values.T, ones], axis=0)


def fetches(items_ref, picks, buffer, sems):
    return [
        pltpu.make_async_copy(items_ref.at[i, k], buffer.at[n], sems.at[n])
        for n, (i, k) in enumerate(picks)
    ]


def absorb_all(tag_ref, copies, buffer, query_ref, acc, top):
    for copy in copies:
        copy.wait()

    def step(i, carry):
        tag = tag_ref[i]

        @pl.when(tag >= 0)
        def _():
            keys = buffer[i, :, 0:HD]
            values_t = with_ones(buffer[i, :, HD : 2 * HD])
            for part in range(ROWS // WIDTH):
                cols = pl.ds(part * WIDTH, WIDTH)
                absorb(keys, values_t, query_ref, tag, cols, acc, top)

        return carry

    lax.fori_loop(0, len(copies), step, 0)


def pack(level):
    parts = []
    for _ in range(3):
        part = level.astype(jnp.bfloat16).astype(jnp.float32)
        parts.append(part)
        level = level - part
    parts.append(jnp.zeros((PACK - 3, level.shape[1]), jnp.float32))
    return jnp.concatenate(parts, axis=0).astype(jnp.bfloat16)


def store(out_ref, j, mixed, level):
    out_ref[j, 0:HD, :] = mixed.astype(jnp.bfloat16)
    out_ref[j, HD : HD + PACK, :] = pack(level)


def load(ref, j):
    parts = ref[j, HD : HD + PACK, :].astype(jnp.float32)
    level = parts[0:1] + parts[1:2] + parts[2:3]
    return ref[j, 0:HD, :].astype(jnp.float32), level


def state_of(group, acc, top):
    sums = jnp.maximum(acc[group, HD : HD + 1, :], 1e-30)
    return acc[group, 0:HD, :] / sums, top[group] * SCALE + jnp.log2(sums)


def merge(pairs):
    level = pairs[0][1]
    for _, other in pairs[1:]:
        level = jnp.maximum(level, other)
    shares = [jnp.exp2(l - level) for _, l in pairs]
    whole = functools.reduce(jnp.add, shares)
    mixed = functools.reduce(jnp.add, [o * s for (o, _), s in zip(pairs, shares)])
    return mixed / whole, level + jnp.log2(whole)


def queries_of(refs, query, sems):
    n = refs[0].shape[0]
    copies = [
        pltpu.make_async_copy(ref, query.at[pl.ds(k * n, n)], sems.at[k])
        for k, ref in enumerate(refs)
    ]
    for copy in copies:
        copy.start()
    return copies


def near_kernel(
    tags, here, q0, q1, q2, own, o0, o1, o2, buffer, sems, query, query_sems, *state
):
    arriving = queries_of((q0, q1, q2), query, query_sems)
    copies = fetches(here, [(i, k) for k in range(3) for i in range(NX)], buffer, sems)
    for copy in copies:
        copy.start()
    start(*state)
    for copy in arriving:
        copy.wait()
    n = o0.shape[0]
    for j in range(n):
        rows = slice(j * LQ, (j + 1) * LQ)
        keys = own[rows, 0:HD]
        values_t = with_ones(own[rows, HD : 2 * HD])

        def head(part, carry, j=j, keys=keys, values_t=values_t):
            cols = pl.ds(pl.multiple_of(part * LQ, LQ), LQ)
            absorb(keys, values_t, query, j, cols, *state, causal=True)
            return carry

        lax.fori_loop(0, GROUP, head, 0)
    absorb_all(tags, copies, buffer, query, *state)
    for k, out_ref in enumerate((o0, o1, o2)):
        for j in range(n):
            store(out_ref, j, *state_of(k * n + j, *state))


def far_kernel(tags, here, q0, q1, o_up, o_down, buffer, sems, query, query_sems, *state):
    arriving = queries_of((q0, q1), query, query_sems)
    copies = fetches(here, [(i, k) for k in (3, 4) for i in range(NX)], buffer, sems)
    for copy in copies:
        copy.start()
    start(*state)
    for copy in arriving:
        copy.wait()
    absorb_all(tags, copies, buffer, query, *state)
    n = o_up.shape[0]
    for j in range(n):
        store(o_up, j, *state_of(j, *state))
        store(o_down, j, *state_of(n + j, *state))


def move_kernel(
    tags,
    moved,
    q0,
    q1,
    so_far_up,
    so_far_down,
    o_up,
    o_down,
    buffer,
    sems,
    query,
    query_sems,
    *state,
):
    arriving = queries_of((q0, q1), query, query_sems)
    copies = fetches(moved, [(i, k) for k in range(3) for i in range(NX)], buffer, sems)
    for copy in copies:
        copy.start()
    start(*state)
    for copy in arriving:
        copy.wait()
    absorb_all(tags, copies, buffer, query, *state)
    n = o_up.shape[0]
    for j in range(n):
        store(o_up, j, *merge([state_of(j, *state), load(so_far_up, j)]))
        store(o_down, j, *merge([state_of(n + j, *state), load(so_far_down, j)]))


def attention(kernel, name, tags, items, queries, arrays, groups, slots, work):
    vmem, anywhere = pl.BlockSpec(memory_space=pltpu.VMEM), pl.BlockSpec(memory_space=pl.ANY)
    n = queries[0].shape[0]
    return pl.pallas_call(
        kernel,
        out_shape=(jax.ShapeDtypeStruct((n, HD + PACK, ROWS), jnp.bfloat16),) * groups,
        in_specs=[pl.BlockSpec(memory_space=pltpu.SMEM), anywhere]
        + [anywhere] * len(queries)
        + [vmem] * len(arrays),
        out_specs=(vmem,) * groups,
        scratch_shapes=[
            pltpu.VMEM((slots, PLEN, 2 * HD), jnp.bfloat16),
            pltpu.SemaphoreType.DMA((slots,)),
            pltpu.VMEM((groups * n, ROWS, HD), jnp.bfloat16),
            pltpu.SemaphoreType.DMA((groups,)),
            pltpu.VMEM((groups * n, HD + PACK, ROWS), jnp.float32),
            pltpu.VMEM((groups * n, 1, ROWS), jnp.float32),
        ],
        compiler_params=pltpu.CompilerParams(vmem_limit_bytes=VMEM_LIMIT),
        cost_estimate=pl.CostEstimate(
            flops=work * ROWS * PLEN,
            bytes_accessed=work * PLEN,
            transcendentals=0,
        ),
        name=name,
    )(tags, items, *queries, *arrays)


def last_kernel(*refs):
    parts, out_ref = refs[:-1], refs[-1]
    for j in range(parts[0].shape[0]):
        mixed, _ = merge([load(part, j) for part in parts])
        for head in range(GROUP):
            cols = slice(head * LQ, (head + 1) * LQ)
            out_ref[j * LQ : (j + 1) * LQ, head * HD : (head + 1) * HD] = mixed[:, cols].T.astype(
                jnp.bfloat16
            )


def project_kernel(place, context_ref, most_ref, rest_ref, out_ref):
    cut = most_ref.shape[0]
    products = jnp.dot(
        context_ref[:, :cut], most_ref[...], preferred_element_type=jnp.float32
    ) + jnp.dot(context_ref[:, cut:], rest_ref[0], preferred_element_type=jnp.float32)
    out_ref[0] = products.astype(jnp.bfloat16)


def project(context, most, rest, core, x, name):
    width = most.shape[1] // (NY * NC)
    return pl.pallas_call(
        project_kernel,
        out_shape=jax.ShapeDtypeStruct((NY, context.shape[0], width), jnp.bfloat16),
        grid_spec=pltpu.PrefetchScalarGridSpec(
            num_scalar_prefetch=1,
            grid=(NY,),
            in_specs=[
                pl.BlockSpec(context.shape, lambda i, place: (0, 0)),
                pl.BlockSpec((most.shape[0], width), lambda i, place: (0, NC * i + place[0])),
                pl.BlockSpec(
                    (1, rest.shape[1], width),
                    lambda i, place: (lax.rem(i + NX - place[1], NX), 0, place[0]),
                ),
            ],
            out_specs=pl.BlockSpec((1, context.shape[0], width), lambda i, place: (i, 0, 0)),
        ),
        compiler_params=pltpu.CompilerParams(vmem_limit_bytes=VMEM_LIMIT),
        cost_estimate=pl.CostEstimate(
            flops=2 * context.shape[0] * context.shape[1] * width * NY,
            bytes_accessed=context.shape[1] * width * NY * 2,
            transcendentals=0,
        ),
        name=name,
    )(jnp.stack([core, x]), context, most, rest)


def in_vmem(kernel, name, out, *arrays):
    vmem = pl.BlockSpec(memory_space=pltpu.VMEM)
    return pl.pallas_call(
        kernel,
        out_shape=out,
        in_specs=[vmem] * len(arrays),
        out_specs=jax.tree.map(lambda _: vmem, out),
        compiler_params=pltpu.CompilerParams(vmem_limit_bytes=VMEM_LIMIT),
        name=name,
    )(*arrays)


def along_z(array, shift):
    return lax.ppermute(array, "z", [(i, (i + shift) % NZ) for i in range(NZ)])


def along_x(array, shift):
    return lax.ppermute(array, "x", [(i, (i + shift) % NX) for i in range(NX)])


def over_x(items):
    return lax.all_to_all(items, "x", split_axis=0, concat_axis=0, tiled=True)


def body(queries, own_kv, passage_cache, out_weight, lists, passage_slot, question_slot):
    x, z = lax.axis_index("x"), lax.axis_index("z")
    per_device = queries.shape[0] // LQ
    pass_dev = passage_cache.shape[0]
    cache = passage_cache.reshape(pass_dev, PLEN, 2 * HD)
    own = own_kv.reshape(per_device * LQ, 2 * HD)

    q_own = queries.reshape(per_device, LQ, GROUP, HD).transpose(0, 2, 1, 3)
    q_own = q_own.reshape(per_device, ROWS, HD)
    owners, local_rows = request_tables(lists, passage_slot, question_slot, per_device, pass_dev)
    mine = jnp.sum(jnp.where(owners == x * NZ + z, local_rows, 0), axis=1).reshape(NX, NZ)
    target_z = (z + jnp.array(STAY + MOVE, jnp.int32)) % NZ
    rows = jnp.sum(
        jnp.where(target_z[None, :, None] == jnp.arange(NZ)[None, None, :], mine[:, None, :], 0),
        axis=2,
    )
    stay = len(STAY)
    moving = take_rows(cache, rows[:, stay:].T.reshape(-1), (4, 4, 2, 2))
    moving, staying = lax.optimization_barrier((moving, rows[:, :stay].reshape(-1)))
    (here,) = take_rows(cache, staying, (NX * stay,))
    q_up = along_z(q_own, -1)
    q_down = along_z(q_own, 1)
    cut = out_weight.shape[0] * 3 // 4
    most = lax.all_gather(out_weight[:cut], "z", axis=1, tiled=True)
    rest = out_weight[cut:]
    rest = jnp.stack([rest] + [along_x(rest, -distance) for distance in range(1, NX)])
    here, q_up, q_down, rest = lax.optimization_barrier((here, q_up, q_down, rest))
    rest = lax.all_gather(rest, "z", axis=2, tiled=True)
    here = over_x(here.reshape(NX, stay, PLEN, 2 * HD))
    up3, down3, up4, down4 = moving
    up3 = along_z(up3, 1)
    down3 = along_z(down3, -1)
    up4 = along_z(up4, 2)
    down4 = along_z(down4, -2)
    up3, down3, up4, down4, q_up, q_down = lax.optimization_barrier(
        (up3, down3, up4, down4, q_up, q_down)
    )
    q_up2 = along_z(q_up, -1)
    q_down2 = along_z(q_down, 1)
    moved = assemble((up3, down3, up4, down4))
    moved, here = lax.optimization_barrier((moved, here))
    moved = over_x(moved)

    slots = [(d, i, 0, k) for k, d in enumerate(STAY[:3]) for i in range(NX)]
    slots += [(d, i, 0, k) for k, d in enumerate(STAY[3:]) for i in range(NX)]
    slots += [(2, i, -1, 0) for i in range(NX)]
    slots += [(-2, i, 1, 1) for i in range(NX)]
    slots += [(2, i, -2, 0) for i in range(NX)]
    slots = jnp.array(slots, jnp.int32)
    last = jnp.arange(slots.shape[0]) >= slots.shape[0] - NX
    turn = jnp.where(last & (x >= 2), -1, 1)
    slot_question = (z + slots[:, 0] * turn) % NZ
    slot_owner = slots[:, 1] * NZ + (z + slots[:, 2] * turn) % NZ
    base = per_device * jnp.where(turn < 0, 1, slots[:, 3])
    column = lax.dynamic_index_in_dim(owners.reshape(NX, NZ, -1), x, 0, keepdims=False)
    number = jnp.arange(column.shape[1], dtype=jnp.int32) // TOPP + 1
    hit = (slot_question[:, None, None] == jnp.arange(NZ)[None, :, None]) & (
        slot_owner[:, None, None] == column[None, :, :]
    )
    tags = jnp.sum(jnp.where(hit, number[None, None, :], 0), axis=(1, 2)) - 1
    tags = jnp.where(tags < 0, -1, tags + base)

    split = NX * stay
    near = attention(
        near_kernel,
        "near",
        tags[: 3 * NX],
        here,
        [q_own, q_up, q_down],
        [own],
        3,
        3 * NX,
        10,
    )
    near, q_up2, q_down2, most, rest = lax.optimization_barrier((near, q_up2, q_down2, most, rest))
    most = lax.all_gather(most, "x", axis=1, tiled=True)
    own_part, near_up, near_down = near
    home_up = along_z(near_up, 1)
    home_down = along_z(near_down, -1)
    far = attention(
        far_kernel,
        "far",
        tags[3 * NX : split],
        here,
        [q_up2, q_down2],
        [],
        2,
        2 * NX,
        6,
    )
    far_up, far_down = attention(
        move_kernel,
        "move",
        tags[split:],
        moved,
        [q_up2, q_down2],
        far,
        2,
        3 * NX,
        400000,
    )
    far_up = along_z(far_up, 2)
    far_down = along_z(far_down, -2)
    context = in_vmem(
        last_kernel,
        "last",
        jax.ShapeDtypeStruct(queries.shape, jnp.bfloat16),
        own_part,
        home_up,
        home_down,
        far_up,
        far_down,
    )
    core = lax.axis_index("core")
    theirs = project(context, most, rest, 1 - core, x, "theirs")
    theirs = lax.ppermute(theirs, "core", [(0, 1), (1, 0)])
    ours = project(context, most, rest, core, x, "ours")
    chip = (ours.astype(jnp.float32) + theirs.astype(jnp.float32)).astype(jnp.bfloat16)
    chips = lax.all_to_all(chip, "y", split_axis=0, concat_axis=0, tiled=True)
    return jnp.sum(chips.astype(jnp.float32), axis=0).astype(jnp.bfloat16)


def solution(mesh):
    grid = Mesh(mesh.devices.reshape(NX, NZ, NY, NC), ("x", "z", "y", "core"))
    on_pass, on_head = ("x", "z"), ("y", "core")
    in_specs = (
        P(on_pass, on_head),
        P(on_pass, on_head, None),
        P(on_pass, None, on_head, None),
        P(on_head, on_pass),
        P(),
        P(),
        P(),
    )
    out_specs = P(on_pass, on_head)
    return jax.shard_map(body, mesh=grid, in_specs=in_specs, out_specs=out_specs, check_vma=False)
```

```python
import functools
import math

import jax
import jax.numpy as jnp
from jax import lax
from jax.experimental import pallas as pl
from jax.experimental.pallas import tpu as pltpu
from jax.sharding import Mesh, PartitionSpec as P

HD = 128
GROUP = 8
LQ = 128
PLEN = 512
TOPP = 8
NX, NZ, NY, NC = 4, 8, 4, 2
ROWS = GROUP * LQ
SCALE = math.log2(math.e) / math.sqrt(HD)
NEG = -1e30
WIDTH = 1024
PACK = 16
VMEM_LIMIT = 50 << 20

STAY = (0, 1, -1, 2, -2)
MOVE = (3, -3, 4)


def request_tables(lists, passage_slot, question_slot, per_device, pass_dev):
    slot_count = question_slot.shape[0]
    slot_ids = jnp.arange(slot_count, dtype=jnp.int32)
    holder = (question_slot[None, :] == slot_ids[:, None]).astype(jnp.int32)
    chosen = jnp.sum(holder[:, :, None] * lists[None, :, :], axis=1)
    catalog = jnp.arange(passage_slot.shape[0], dtype=jnp.int32)
    picked = (chosen[:, :, None] == catalog[None, None, :]).astype(jnp.int32)
    cache_rows = jnp.sum(picked * passage_slot[None, None, :], axis=2)
    cache_rows = cache_rows.reshape(slot_count // per_device, per_device * TOPP)
    return cache_rows // pass_dev, cache_rows % pass_dev


def staged(sources, places, buffer, read_sems, write_sems):
    reads, writes = [], []
    for n, (source, place) in enumerate(zip(sources, places)):
        reads.append(pltpu.make_async_copy(source, buffer.at[n], read_sems.at[n]))
        writes.append(pltpu.make_async_copy(buffer.at[n], place, write_sems.at[n]))
    for read in reads:
        read.start()
    for read, write in zip(reads, writes):
        read.wait()
        write.start()
    for write in writes:
        write.wait()


def row_copies(rows_ref, cache_ref, *refs):
    outs, scratch = refs[:-3], refs[-3:]
    places = [out_ref.at[i] for out_ref in outs for i in range(out_ref.shape[0])]
    staged([cache_ref.at[rows_ref[n]] for n in range(len(places))], places, *scratch)


def assemble_copies(up3, down3, up4, down4, out_ref, *scratch):
    sources = [ref.at[i] for ref in (up3, down3, up4, down4) for i in range(ref.shape[0])]
    places = [out_ref.at[i, k] for k in range(3) for i in range(NX)]
    staged(sources, places, *scratch)


def assemble(parts):
    anywhere = pl.BlockSpec(memory_space=pl.ANY)
    shape, dtype = parts[0].shape[1:], parts[0].dtype
    return pl.pallas_call(
        assemble_copies,
        out_shape=jax.ShapeDtypeStruct((NX, 3) + shape, dtype),
        in_specs=[anywhere] * len(parts),
        out_specs=anywhere,
        scratch_shapes=[
            pltpu.VMEM((3 * NX,) + shape, dtype),
            pltpu.SemaphoreType.DMA((3 * NX,)),
            pltpu.SemaphoreType.DMA((3 * NX,)),
        ],
        compiler_params=pltpu.CompilerParams(vmem_limit_bytes=VMEM_LIMIT),
        name="assemble",
    )(*parts)


def take_rows(cache, rows, counts):
    anywhere = pl.BlockSpec(memory_space=pl.ANY)
    total = sum(counts)
    return pl.pallas_call(
        row_copies,
        out_shape=tuple(jax.ShapeDtypeStruct((n,) + cache.shape[1:], cache.dtype) for n in counts),
        in_specs=[pl.BlockSpec(memory_space=pltpu.SMEM), anywhere],
        out_specs=(anywhere,) * len(counts),
        scratch_shapes=[
            pltpu.VMEM((total,) + cache.shape[1:], cache.dtype),
            pltpu.SemaphoreType.DMA((total,)),
            pltpu.SemaphoreType.DMA((total,)),
        ],
        compiler_params=pltpu.CompilerParams(vmem_limit_bytes=VMEM_LIMIT),
        name="take_rows",
    )(rows, cache)


def absorb(keys, values_t, query_ref, group, cols, acc, top, causal=False):
    scores = lax.dot_general(
        keys,
        query_ref[group, cols, :],
        (((1,), (1,)), ((), ())),
        preferred_element_type=jnp.float32,
    )
    if causal:
        key = lax.broadcasted_iota(jnp.int32, scores.shape, 0)
        token = lax.broadcasted_iota(jnp.int32, scores.shape, 1)
        scores = jnp.where(key <= token, scores, NEG)
    old = top[group, :, cols]
    new = jnp.maximum(old, jnp.max(scores, axis=0, keepdims=True))
    weights = jnp.exp2((scores - new) * SCALE)
    keep = jnp.exp2((old - new) * SCALE)
    top[group, :, cols] = new
    acc[group, :, cols] = acc[group, :, cols] * keep + jnp.dot(
        values_t, weights.astype(jnp.bfloat16), preferred_element_type=jnp.float32
    )


def start(acc, top):
    acc[...] = jnp.zeros_like(acc)
    top[...] = jnp.full_like(top, NEG)


def with_ones(values):
    ones = jnp.ones((PACK, values.shape[0]), values.dtype)
    return jnp.concatenate([values.T, ones], axis=0)


def fetches(items_ref, picks, buffer, sems):
    return [
        pltpu.make_async_copy(items_ref.at[i, k], buffer.at[n], sems.at[n])
        for n, (i, k) in enumerate(picks)
    ]


def absorb_all(tag_ref, copies, buffer, query_ref, acc, top):
    for copy in copies:
        copy.wait()

    def step(i, carry):
        tag = tag_ref[i]

        @pl.when(tag >= 0)
        def _():
            keys = buffer[i, :, 0:HD]
            values_t = with_ones(buffer[i, :, HD : 2 * HD])
            for part in range(ROWS // WIDTH):
                cols = pl.ds(part * WIDTH, WIDTH)
                absorb(keys, values_t, query_ref, tag, cols, acc, top)

        return carry

    lax.fori_loop(0, len(copies), step, 0)


def pack(level):
    parts = []
    for _ in range(3):
        part = level.astype(jnp.bfloat16).astype(jnp.float32)
        parts.append(part)
        level = level - part
    parts.append(jnp.zeros((PACK - 3, level.shape[1]), jnp.float32))
    return jnp.concatenate(parts, axis=0).astype(jnp.bfloat16)


def store(out_ref, j, mixed, level):
    out_ref[j, 0:HD, :] = mixed.astype(jnp.bfloat16)
    out_ref[j, HD : HD + PACK, :] = pack(level)


def load(ref, j):
    parts = ref[j, HD : HD + PACK, :].astype(jnp.float32)
    level = parts[0:1] + parts[1:2] + parts[2:3]
    return ref[j, 0:HD, :].astype(jnp.float32), level


def state_of(group, acc, top):
    sums = jnp.maximum(acc[group, HD : HD + 1, :], 1e-30)
    return acc[group, 0:HD, :] / sums, top[group] * SCALE + jnp.log2(sums)


def merge(pairs):
    level = pairs[0][1]
    for _, other in pairs[1:]:
        level = jnp.maximum(level, other)
    shares = [jnp.exp2(l - level) for _, l in pairs]
    whole = functools.reduce(jnp.add, shares)
    mixed = functools.reduce(jnp.add, [o * s for (o, _), s in zip(pairs, shares)])
    return mixed / whole, level + jnp.log2(whole)


def queries_of(refs, query, sems):
    n = refs[0].shape[0]
    copies = [
        pltpu.make_async_copy(ref, query.at[pl.ds(k * n, n)], sems.at[k])
        for k, ref in enumerate(refs)
    ]
    for copy in copies:
        copy.start()
    return copies


def self_kernel(q_own, own, out_ref, *state):
    start(*state)
    n = q_own.shape[0]
    for j in range(n):
        rows = slice(j * LQ, (j + 1) * LQ)
        keys = own[rows, 0:HD]
        values_t = with_ones(own[rows, HD : 2 * HD])

        def head(part, carry, j=j, keys=keys, values_t=values_t):
            cols = pl.ds(pl.multiple_of(part * LQ, LQ), LQ)
            absorb(keys, values_t, q_own, j, cols, *state, causal=True)
            return carry

        lax.fori_loop(0, GROUP, head, 0)
        store(out_ref, j, *state_of(j, *state))


def near_kernel(tags, here, q0, q1, q2, o0, o1, o2, buffer, sems, query, query_sems, *state):
    arriving = queries_of((q0, q1, q2), query, query_sems)
    copies = fetches(here, [(i, k) for k in range(3) for i in range(NX)], buffer, sems)
    for copy in copies:
        copy.start()
    start(*state)
    for copy in arriving:
        copy.wait()
    absorb_all(tags, copies, buffer, query, *state)
    n = o0.shape[0]
    for k, out_ref in enumerate((o0, o1, o2)):
        for j in range(n):
            store(out_ref, j, *state_of(k * n + j, *state))


def far_kernel(tags, here, q0, q1, o_up, o_down, buffer, sems, query, query_sems, *state):
    arriving = queries_of((q0, q1), query, query_sems)
    copies = fetches(here, [(i, k) for k in (3, 4) for i in range(NX)], buffer, sems)
    for copy in copies:
        copy.start()
    start(*state)
    for copy in arriving:
        copy.wait()
    absorb_all(tags, copies, buffer, query, *state)
    n = o_up.shape[0]
    for j in range(n):
        store(o_up, j, *state_of(j, *state))
        store(o_down, j, *state_of(n + j, *state))


def move_kernel(
    tags,
    moved,
    q0,
    q1,
    so_far_up,
    so_far_down,
    o_up,
    o_down,
    buffer,
    sems,
    query,
    query_sems,
    *state,
):
    arriving = queries_of((q0, q1), query, query_sems)
    copies = fetches(moved, [(i, k) for k in range(3) for i in range(NX)], buffer, sems)
    for copy in copies:
        copy.start()
    start(*state)
    for copy in arriving:
        copy.wait()
    absorb_all(tags, copies, buffer, query, *state)
    n = o_up.shape[0]
    for j in range(n):
        store(o_up, j, *merge([state_of(j, *state), load(so_far_up, j)]))
        store(o_down, j, *merge([state_of(n + j, *state), load(so_far_down, j)]))


def attention(kernel, name, tags, items, queries, arrays, groups, slots, work):
    vmem, anywhere = pl.BlockSpec(memory_space=pltpu.VMEM), pl.BlockSpec(memory_space=pl.ANY)
    n = queries[0].shape[0]
    return pl.pallas_call(
        kernel,
        out_shape=(jax.ShapeDtypeStruct((n, HD + PACK, ROWS), jnp.bfloat16),) * groups,
        in_specs=[pl.BlockSpec(memory_space=pltpu.SMEM), anywhere]
        + [anywhere] * len(queries)
        + [vmem] * len(arrays),
        out_specs=(vmem,) * groups,
        scratch_shapes=[
            pltpu.VMEM((slots, PLEN, 2 * HD), jnp.bfloat16),
            pltpu.SemaphoreType.DMA((slots,)),
            pltpu.VMEM((groups * n, ROWS, HD), jnp.bfloat16),
            pltpu.SemaphoreType.DMA((groups,)),
            pltpu.VMEM((groups * n, HD + PACK, ROWS), jnp.float32),
            pltpu.VMEM((groups * n, 1, ROWS), jnp.float32),
        ],
        compiler_params=pltpu.CompilerParams(vmem_limit_bytes=VMEM_LIMIT),
        cost_estimate=pl.CostEstimate(
            flops=work * ROWS * PLEN,
            bytes_accessed=work * PLEN,
            transcendentals=0,
        ),
        name=name,
    )(tags, items, *queries, *arrays)


def last_kernel(*refs):
    parts, out_ref = refs[:-1], refs[-1]
    for j in range(parts[0].shape[0]):
        mixed, _ = merge([load(part, j) for part in parts])
        for head in range(GROUP):
            cols = slice(head * LQ, (head + 1) * LQ)
            out_ref[j * LQ : (j + 1) * LQ, head * HD : (head + 1) * HD] = mixed[:, cols].T.astype(
                jnp.bfloat16
            )


def project_kernel(place, context_ref, most_ref, rest_ref, out_ref):
    cut = most_ref.shape[0]
    products = jnp.dot(
        context_ref[:, :cut], most_ref[...], preferred_element_type=jnp.float32
    ) + jnp.dot(context_ref[:, cut:], rest_ref[0], preferred_element_type=jnp.float32)
    out_ref[0] = products.astype(jnp.bfloat16)


def project(context, most, rest, core, x, name):
    width = most.shape[1] // (NY * NC)
    return pl.pallas_call(
        project_kernel,
        out_shape=jax.ShapeDtypeStruct((NY, context.shape[0], width), jnp.bfloat16),
        grid_spec=pltpu.PrefetchScalarGridSpec(
            num_scalar_prefetch=1,
            grid=(NY,),
            in_specs=[
                pl.BlockSpec(context.shape, lambda i, place: (0, 0)),
                pl.BlockSpec((most.shape[0], width), lambda i, place: (0, NC * i + place[0])),
                pl.BlockSpec(
                    (1, rest.shape[1], width),
                    lambda i, place: (lax.rem(i + NX - place[1], NX), 0, place[0]),
                ),
            ],
            out_specs=pl.BlockSpec((1, context.shape[0], width), lambda i, place: (i, 0, 0)),
        ),
        compiler_params=pltpu.CompilerParams(vmem_limit_bytes=VMEM_LIMIT),
        cost_estimate=pl.CostEstimate(
            flops=2 * context.shape[0] * context.shape[1] * width * NY,
            bytes_accessed=context.shape[1] * width * NY * 2,
            transcendentals=0,
        ),
        name=name,
    )(jnp.stack([core, x]), context, most, rest)


def in_vmem(kernel, name, out, *arrays, scratch=()):
    vmem = pl.BlockSpec(memory_space=pltpu.VMEM)
    return pl.pallas_call(
        kernel,
        out_shape=out,
        in_specs=[vmem] * len(arrays),
        out_specs=jax.tree.map(lambda _: vmem, out),
        scratch_shapes=scratch,
        compiler_params=pltpu.CompilerParams(vmem_limit_bytes=VMEM_LIMIT),
        name=name,
    )(*arrays)


def along_z(array, shift):
    return lax.ppermute(array, "z", [(i, (i + shift) % NZ) for i in range(NZ)])


def along_x(array, shift):
    return lax.ppermute(array, "x", [(i, (i + shift) % NX) for i in range(NX)])


def over_x(items):
    return lax.all_to_all(items, "x", split_axis=0, concat_axis=0, tiled=True)


def body(queries, own_kv, passage_cache, out_weight, lists, passage_slot, question_slot):
    x, z = lax.axis_index("x"), lax.axis_index("z")
    per_device = queries.shape[0] // LQ
    pass_dev = passage_cache.shape[0]
    cache = passage_cache.reshape(pass_dev, PLEN, 2 * HD)
    own = own_kv.reshape(per_device * LQ, 2 * HD)

    q_own = queries.reshape(per_device, LQ, GROUP, HD).transpose(0, 2, 1, 3)
    q_own = q_own.reshape(per_device, ROWS, HD)
    owners, local_rows = request_tables(lists, passage_slot, question_slot, per_device, pass_dev)
    mine = jnp.sum(jnp.where(owners == x * NZ + z, local_rows, 0), axis=1).reshape(NX, NZ)
    target_z = (z + jnp.array(STAY + MOVE, jnp.int32)) % NZ
    rows = jnp.sum(
        jnp.where(target_z[None, :, None] == jnp.arange(NZ)[None, None, :], mine[:, None, :], 0),
        axis=2,
    )
    stay = len(STAY)
    moving = take_rows(cache, rows[:, stay:].T.reshape(-1), (4, 4, 2, 2))
    moving, staying = lax.optimization_barrier((moving, rows[:, :stay].reshape(-1)))
    (here,) = take_rows(cache, staying, (NX * stay,))
    cut = out_weight.shape[0] * 3 // 4
    most = lax.all_gather(out_weight[:cut], "z", axis=1, tiled=True)
    rest = out_weight[cut:]
    rest = jnp.stack([rest] + [along_x(rest, -distance) for distance in range(1, NX)])
    here, rest = lax.optimization_barrier((here, rest))
    rest = lax.all_gather(rest, "z", axis=2, tiled=True)
    here = over_x(here.reshape(NX, stay, PLEN, 2 * HD))
    up3, down3, up4, down4 = moving
    up3 = along_z(up3, 1)
    down3 = along_z(down3, -1)
    up4 = along_z(up4, 2)
    down4 = along_z(down4, -2)
    up3, down3, up4, down4, q_own = lax.optimization_barrier((up3, down3, up4, down4, q_own))
    q_up = along_z(q_own, -1)
    q_down = along_z(q_own, 1)
    q_up2 = along_z(q_up, -1)
    q_down2 = along_z(q_down, 1)
    moved = assemble((up3, down3, up4, down4))
    moved, here = lax.optimization_barrier((moved, here))
    moved = over_x(moved)

    slots = [(d, i, 0, k) for k, d in enumerate(STAY[:3]) for i in range(NX)]
    slots += [(d, i, 0, k) for k, d in enumerate(STAY[3:]) for i in range(NX)]
    slots += [(2, i, -1, 0) for i in range(NX)]
    slots += [(-2, i, 1, 1) for i in range(NX)]
    slots += [(2, i, -2, 0) for i in range(NX)]
    slots = jnp.array(slots, jnp.int32)
    last = jnp.arange(slots.shape[0]) >= slots.shape[0] - NX
    turn = jnp.where(last & (x >= 2), -1, 1)
    slot_question = (z + slots[:, 0] * turn) % NZ
    slot_owner = slots[:, 1] * NZ + (z + slots[:, 2] * turn) % NZ
    base = per_device * jnp.where(turn < 0, 1, slots[:, 3])
    column = lax.dynamic_index_in_dim(owners.reshape(NX, NZ, -1), x, 0, keepdims=False)
    number = jnp.arange(column.shape[1], dtype=jnp.int32) // TOPP + 1
    hit = (slot_question[:, None, None] == jnp.arange(NZ)[None, :, None]) & (
        slot_owner[:, None, None] == column[None, :, :]
    )
    tags = jnp.sum(jnp.where(hit, number[None, None, :], 0), axis=(1, 2)) - 1
    tags = jnp.where(tags < 0, -1, tags + base)

    split = NX * stay
    itself = in_vmem(
        self_kernel,
        "itself",
        jax.ShapeDtypeStruct((per_device, HD + PACK, ROWS), jnp.bfloat16),
        q_own,
        own,
        scratch=[
            pltpu.VMEM((per_device, HD + PACK, ROWS), jnp.float32),
            pltpu.VMEM((per_device, 1, ROWS), jnp.float32),
        ],
    )
    near = attention(
        near_kernel,
        "near",
        tags[: 3 * NX],
        here,
        [q_own, q_up, q_down],
        [],
        3,
        3 * NX,
        10,
    )
    near, q_up2, q_down2, most, rest = lax.optimization_barrier((near, q_up2, q_down2, most, rest))
    most = lax.all_gather(most, "x", axis=1, tiled=True)
    own_part, near_up, near_down = near
    home_up = along_z(near_up, 1)
    home_down = along_z(near_down, -1)
    far = attention(
        far_kernel,
        "far",
        tags[3 * NX : split],
        here,
        [q_up2, q_down2],
        [],
        2,
        2 * NX,
        6,
    )
    far_up, far_down = attention(
        move_kernel,
        "move",
        tags[split:],
        moved,
        [q_up2, q_down2],
        far,
        2,
        3 * NX,
        400000,
    )
    far_up = along_z(far_up, 2)
    far_down = along_z(far_down, -2)
    context = in_vmem(
        last_kernel,
        "last",
        jax.ShapeDtypeStruct(queries.shape, jnp.bfloat16),
        itself,
        own_part,
        home_up,
        home_down,
        far_up,
        far_down,
    )
    core = lax.axis_index("core")
    theirs = project(context, most, rest, 1 - core, x, "theirs")
    theirs = lax.ppermute(theirs, "core", [(0, 1), (1, 0)])
    ours = project(context, most, rest, core, x, "ours")
    chip = (ours.astype(jnp.float32) + theirs.astype(jnp.float32)).astype(jnp.bfloat16)
    chips = lax.all_to_all(chip, "y", split_axis=0, concat_axis=0, tiled=True)
    return jnp.sum(chips.astype(jnp.float32), axis=0).astype(jnp.bfloat16)


def solution(mesh):
    grid = Mesh(mesh.devices.reshape(NX, NZ, NY, NC), ("x", "z", "y", "core"))
    on_pass, on_head = ("x", "z"), ("y", "core")
    in_specs = (
        P(on_pass, on_head),
        P(on_pass, on_head, None),
        P(on_pass, None, on_head, None),
        P(on_head, on_pass),
        P(),
        P(),
        P(),
    )
    out_specs = P(on_pass, on_head)
    return jax.shard_map(body, mesh=grid, in_specs=in_specs, out_specs=out_specs, check_vma=False)
```

```python
import functools
import math

import jax
import jax.numpy as jnp
from jax import lax
from jax.experimental import pallas as pl
from jax.experimental.pallas import tpu as pltpu
from jax.sharding import Mesh, PartitionSpec as P

HD = 128
GROUP = 8
LQ = 128
PLEN = 512
TOPP = 8
NX, NZ, NY, NC = 4, 8, 4, 2
ROWS = GROUP * LQ
SCALE = math.log2(math.e) / math.sqrt(HD)
NEG = -1e30
WIDTH = 1024
PACK = 16
VMEM_LIMIT = 50 << 20

STAY = (0, 1, -1, 2, -2)
MOVE = (3, -3, 4)


def request_tables(lists, passage_slot, question_slot, per_device, pass_dev):
    slot_count = question_slot.shape[0]
    slot_ids = jnp.arange(slot_count, dtype=jnp.int32)
    holder = (question_slot[None, :] == slot_ids[:, None]).astype(jnp.int32)
    chosen = jnp.sum(holder[:, :, None] * lists[None, :, :], axis=1)
    catalog = jnp.arange(passage_slot.shape[0], dtype=jnp.int32)
    picked = (chosen[:, :, None] == catalog[None, None, :]).astype(jnp.int32)
    cache_rows = jnp.sum(picked * passage_slot[None, None, :], axis=2)
    cache_rows = cache_rows.reshape(slot_count // per_device, per_device * TOPP)
    return cache_rows // pass_dev, cache_rows % pass_dev


def staged(sources, places, buffer, read_sems, write_sems):
    reads, writes = [], []
    for n, (source, place) in enumerate(zip(sources, places)):
        reads.append(pltpu.make_async_copy(source, buffer.at[n], read_sems.at[n]))
        writes.append(pltpu.make_async_copy(buffer.at[n], place, write_sems.at[n]))
    for read in reads:
        read.start()
    for read, write in zip(reads, writes):
        read.wait()
        write.start()
    for write in writes:
        write.wait()


def row_copies(rows_ref, cache_ref, *refs):
    outs, scratch = refs[:-3], refs[-3:]
    places = [out_ref.at[i] for out_ref in outs for i in range(out_ref.shape[0])]
    staged([cache_ref.at[rows_ref[n]] for n in range(len(places))], places, *scratch)


def assemble_copies(up3, down3, up4, down4, out_ref, *scratch):
    sources = [ref.at[i] for ref in (up3, down3, up4, down4) for i in range(ref.shape[0])]
    places = [out_ref.at[i, k] for k in range(3) for i in range(NX)]
    staged(sources, places, *scratch)


def assemble(parts):
    anywhere = pl.BlockSpec(memory_space=pl.ANY)
    shape, dtype = parts[0].shape[1:], parts[0].dtype
    return pl.pallas_call(
        assemble_copies,
        out_shape=jax.ShapeDtypeStruct((NX, 3) + shape, dtype),
        in_specs=[anywhere] * len(parts),
        out_specs=anywhere,
        scratch_shapes=[
            pltpu.VMEM((3 * NX,) + shape, dtype),
            pltpu.SemaphoreType.DMA((3 * NX,)),
            pltpu.SemaphoreType.DMA((3 * NX,)),
        ],
        compiler_params=pltpu.CompilerParams(vmem_limit_bytes=VMEM_LIMIT),
        name="assemble",
    )(*parts)


def take_rows(cache, rows, counts):
    anywhere = pl.BlockSpec(memory_space=pl.ANY)
    total = sum(counts)
    return pl.pallas_call(
        row_copies,
        out_shape=tuple(jax.ShapeDtypeStruct((n,) + cache.shape[1:], cache.dtype) for n in counts),
        in_specs=[pl.BlockSpec(memory_space=pltpu.SMEM), anywhere],
        out_specs=(anywhere,) * len(counts),
        scratch_shapes=[
            pltpu.VMEM((total,) + cache.shape[1:], cache.dtype),
            pltpu.SemaphoreType.DMA((total,)),
            pltpu.SemaphoreType.DMA((total,)),
        ],
        compiler_params=pltpu.CompilerParams(vmem_limit_bytes=VMEM_LIMIT),
        name="take_rows",
    )(rows, cache)


def absorb(keys, values_t, query_ref, group, cols, acc, top, causal=False):
    scores = lax.dot_general(
        keys,
        query_ref[group, cols, :],
        (((1,), (1,)), ((), ())),
        preferred_element_type=jnp.float32,
    )
    if causal:
        key = lax.broadcasted_iota(jnp.int32, scores.shape, 0)
        token = lax.broadcasted_iota(jnp.int32, scores.shape, 1)
        scores = jnp.where(key <= token, scores, NEG)
    old = top[group, :, cols]
    new = jnp.maximum(old, jnp.max(scores, axis=0, keepdims=True))
    weights = jnp.exp2((scores - new) * SCALE)
    keep = jnp.exp2((old - new) * SCALE)
    top[group, :, cols] = new
    acc[group, :, cols] = acc[group, :, cols] * keep + jnp.dot(
        values_t, weights.astype(jnp.bfloat16), preferred_element_type=jnp.float32
    )


def start(acc, top):
    acc[...] = jnp.zeros_like(acc)
    top[...] = jnp.full_like(top, NEG)


def with_ones(values):
    ones = jnp.ones((PACK, values.shape[0]), values.dtype)
    return jnp.concatenate([values.T, ones], axis=0)


def fetches(items_ref, picks, buffer, sems):
    return [
        pltpu.make_async_copy(items_ref.at[i, k], buffer.at[n], sems.at[n])
        for n, (i, k) in enumerate(picks)
    ]


def absorb_all(tag_ref, copies, buffer, query_ref, acc, top):
    for copy in copies:
        copy.wait()

    def step(i, carry):
        tag = tag_ref[i]

        @pl.when(tag >= 0)
        def _():
            keys = buffer[i, :, 0:HD]
            values_t = with_ones(buffer[i, :, HD : 2 * HD])
            for part in range(ROWS // WIDTH):
                cols = pl.ds(part * WIDTH, WIDTH)
                absorb(keys, values_t, query_ref, tag, cols, acc, top)

        return carry

    lax.fori_loop(0, len(copies), step, 0)


def pack(level):
    parts = []
    for _ in range(3):
        part = level.astype(jnp.bfloat16).astype(jnp.float32)
        parts.append(part)
        level = level - part
    parts.append(jnp.zeros((PACK - 3, level.shape[1]), jnp.float32))
    return jnp.concatenate(parts, axis=0).astype(jnp.bfloat16)


def store(out_ref, j, mixed, level):
    out_ref[j, 0:HD, :] = mixed.astype(jnp.bfloat16)
    out_ref[j, HD : HD + PACK, :] = pack(level)


def load(ref, j):
    parts = ref[j, HD : HD + PACK, :].astype(jnp.float32)
    level = parts[0:1] + parts[1:2] + parts[2:3]
    return ref[j, 0:HD, :].astype(jnp.float32), level


def state_of(group, acc, top):
    sums = jnp.maximum(acc[group, HD : HD + 1, :], 1e-30)
    return acc[group, 0:HD, :] / sums, top[group] * SCALE + jnp.log2(sums)


def merge(pairs):
    level = pairs[0][1]
    for _, other in pairs[1:]:
        level = jnp.maximum(level, other)
    shares = [jnp.exp2(l - level) for _, l in pairs]
    whole = functools.reduce(jnp.add, shares)
    mixed = functools.reduce(jnp.add, [o * s for (o, _), s in zip(pairs, shares)])
    return mixed / whole, level + jnp.log2(whole)


def queries_of(refs, query, sems):
    n = refs[0].shape[0]
    copies = [
        pltpu.make_async_copy(ref, query.at[pl.ds(k * n, n)], sems.at[k])
        for k, ref in enumerate(refs)
    ]
    for copy in copies:
        copy.start()
    return copies


def self_kernel(q_own, own, out_ref, *state):
    start(*state)
    n = q_own.shape[0]
    for j in range(n):
        rows = slice(j * LQ, (j + 1) * LQ)
        keys = own[rows, 0:HD]
        values_t = with_ones(own[rows, HD : 2 * HD])

        def head(part, carry, j=j, keys=keys, values_t=values_t):
            cols = pl.ds(pl.multiple_of(part * LQ, LQ), LQ)
            absorb(keys, values_t, q_own, j, cols, *state, causal=True)
            return carry

        lax.fori_loop(0, GROUP, head, 0)
        store(out_ref, j, *state_of(j, *state))


def near_kernel(tags, here, q0, q1, q2, o0, o1, o2, buffer, sems, query, query_sems, *state):
    arriving = queries_of((q0, q1, q2), query, query_sems)
    copies = fetches(here, [(i, k) for k in range(3) for i in range(NX)], buffer, sems)
    for copy in copies:
        copy.start()
    start(*state)
    for copy in arriving:
        copy.wait()
    absorb_all(tags, copies, buffer, query, *state)
    n = o0.shape[0]
    for k, out_ref in enumerate((o0, o1, o2)):
        for j in range(n):
            store(out_ref, j, *state_of(k * n + j, *state))


def far_kernel(tags, here, q0, q1, o_up, o_down, buffer, sems, query, query_sems, *state):
    arriving = queries_of((q0, q1), query, query_sems)
    copies = fetches(here, [(i, k) for k in (3, 4) for i in range(NX)], buffer, sems)
    for copy in copies:
        copy.start()
    start(*state)
    for copy in arriving:
        copy.wait()
    absorb_all(tags, copies, buffer, query, *state)
    n = o_up.shape[0]
    for j in range(n):
        store(o_up, j, *state_of(j, *state))
        store(o_down, j, *state_of(n + j, *state))


def move_kernel(
    tags,
    moved,
    q0,
    q1,
    so_far_up,
    so_far_down,
    o_up,
    o_down,
    buffer,
    sems,
    query,
    query_sems,
    *state,
):
    arriving = queries_of((q0, q1), query, query_sems)
    copies = fetches(moved, [(i, k) for k in range(3) for i in range(NX)], buffer, sems)
    for copy in copies:
        copy.start()
    start(*state)
    for copy in arriving:
        copy.wait()
    absorb_all(tags, copies, buffer, query, *state)
    n = o_up.shape[0]
    for j in range(n):
        store(o_up, j, *merge([state_of(j, *state), load(so_far_up, j)]))
        store(o_down, j, *merge([state_of(n + j, *state), load(so_far_down, j)]))


def attention(kernel, name, tags, items, queries, arrays, groups, slots, work):
    vmem, anywhere = pl.BlockSpec(memory_space=pltpu.VMEM), pl.BlockSpec(memory_space=pl.ANY)
    n = queries[0].shape[0]
    return pl.pallas_call(
        kernel,
        out_shape=(jax.ShapeDtypeStruct((n, HD + PACK, ROWS), jnp.bfloat16),) * groups,
        in_specs=[pl.BlockSpec(memory_space=pltpu.SMEM), anywhere]
        + [anywhere] * len(queries)
        + [vmem] * len(arrays),
        out_specs=(vmem,) * groups,
        scratch_shapes=[
            pltpu.VMEM((slots, PLEN, 2 * HD), jnp.bfloat16),
            pltpu.SemaphoreType.DMA((slots,)),
            pltpu.VMEM((groups * n, ROWS, HD), jnp.bfloat16),
            pltpu.SemaphoreType.DMA((groups,)),
            pltpu.VMEM((groups * n, HD + PACK, ROWS), jnp.float32),
            pltpu.VMEM((groups * n, 1, ROWS), jnp.float32),
        ],
        compiler_params=pltpu.CompilerParams(vmem_limit_bytes=VMEM_LIMIT),
        cost_estimate=pl.CostEstimate(
            flops=work * ROWS * PLEN,
            bytes_accessed=work * PLEN,
            transcendentals=0,
        ),
        name=name,
    )(tags, items, *queries, *arrays)


def last_kernel(*refs):
    parts, out_ref = refs[:-1], refs[-1]
    for j in range(parts[0].shape[0]):
        mixed, _ = merge([load(part, j) for part in parts])
        for head in range(GROUP):
            cols = slice(head * LQ, (head + 1) * LQ)
            out_ref[j * LQ : (j + 1) * LQ, head * HD : (head + 1) * HD] = mixed[:, cols].T.astype(
                jnp.bfloat16
            )


def project_kernel(place, context_ref, most_ref, rest_ref, out_ref):
    cut = most_ref.shape[0]
    products = jnp.dot(
        context_ref[:, :cut], most_ref[...], preferred_element_type=jnp.float32
    ) + jnp.dot(context_ref[:, cut:], rest_ref[0], preferred_element_type=jnp.float32)
    out_ref[0] = products.astype(jnp.bfloat16)


def project(context, most, rest, core, x, name):
    width = most.shape[1] // (NY * NC)
    return pl.pallas_call(
        project_kernel,
        out_shape=jax.ShapeDtypeStruct((NY, context.shape[0], width), jnp.bfloat16),
        grid_spec=pltpu.PrefetchScalarGridSpec(
            num_scalar_prefetch=1,
            grid=(NY,),
            in_specs=[
                pl.BlockSpec(context.shape, lambda i, place: (0, 0)),
                pl.BlockSpec((most.shape[0], width), lambda i, place: (0, NC * i + place[0])),
                pl.BlockSpec(
                    (1, rest.shape[1], width),
                    lambda i, place: (lax.rem(i + NX - place[1], NX), 0, place[0]),
                ),
            ],
            out_specs=pl.BlockSpec((1, context.shape[0], width), lambda i, place: (i, 0, 0)),
        ),
        compiler_params=pltpu.CompilerParams(vmem_limit_bytes=VMEM_LIMIT),
        cost_estimate=pl.CostEstimate(
            flops=2 * context.shape[0] * context.shape[1] * width * NY,
            bytes_accessed=context.shape[1] * width * NY * 2,
            transcendentals=0,
        ),
        name=name,
    )(jnp.stack([core, x]), context, most, rest)


def in_vmem(kernel, name, out, *arrays, scratch=()):
    vmem = pl.BlockSpec(memory_space=pltpu.VMEM)
    return pl.pallas_call(
        kernel,
        out_shape=out,
        in_specs=[vmem] * len(arrays),
        out_specs=jax.tree.map(lambda _: vmem, out),
        scratch_shapes=scratch,
        compiler_params=pltpu.CompilerParams(vmem_limit_bytes=VMEM_LIMIT),
        name=name,
    )(*arrays)


def along_z(array, shift):
    return lax.ppermute(array, "z", [(i, (i + shift) % NZ) for i in range(NZ)])


def along_x(array, shift):
    return lax.ppermute(array, "x", [(i, (i + shift) % NX) for i in range(NX)])


def over_x(items):
    return lax.all_to_all(items, "x", split_axis=0, concat_axis=0, tiled=True)


def body(queries, own_kv, passage_cache, out_weight, lists, passage_slot, question_slot):
    x, z = lax.axis_index("x"), lax.axis_index("z")
    per_device = queries.shape[0] // LQ
    pass_dev = passage_cache.shape[0]
    cache = passage_cache.reshape(pass_dev, PLEN, 2 * HD)
    own = own_kv.reshape(per_device * LQ, 2 * HD)

    q_own = queries.reshape(per_device, LQ, GROUP, HD).transpose(0, 2, 1, 3)
    q_own = q_own.reshape(per_device, ROWS, HD)
    owners, local_rows = request_tables(lists, passage_slot, question_slot, per_device, pass_dev)
    mine = jnp.sum(jnp.where(owners == x * NZ + z, local_rows, 0), axis=1).reshape(NX, NZ)
    target_z = (z + jnp.array(STAY + MOVE, jnp.int32)) % NZ
    rows = jnp.sum(
        jnp.where(target_z[None, :, None] == jnp.arange(NZ)[None, None, :], mine[:, None, :], 0),
        axis=2,
    )
    stay = len(STAY)
    moving = take_rows(cache, rows[:, stay:].T.reshape(-1), (4, 4, 2, 2))
    moving, staying = lax.optimization_barrier((moving, rows[:, :stay].reshape(-1)))
    (here,) = take_rows(cache, staying, (NX * stay,))
    q_up = along_z(q_own, -1)
    q_down = along_z(q_own, 1)
    cut = out_weight.shape[0] * 3 // 4
    most = lax.all_gather(out_weight[:cut], "z", axis=1, tiled=True)
    rest = out_weight[cut:]
    rest = jnp.stack([rest] + [along_x(rest, -distance) for distance in range(1, NX)])
    here, q_up, q_down, rest = lax.optimization_barrier((here, q_up, q_down, rest))
    rest = lax.all_gather(rest, "z", axis=2, tiled=True)
    here = over_x(here.reshape(NX, stay, PLEN, 2 * HD))
    up3, down3, up4, down4 = moving
    up3 = along_z(up3, 1)
    down3 = along_z(down3, -1)
    up4 = along_z(up4, 2)
    down4 = along_z(down4, -2)
    up3, down3, up4, down4, q_up, q_down = lax.optimization_barrier(
        (up3, down3, up4, down4, q_up, q_down)
    )
    q_up2 = along_z(q_up, -1)
    q_down2 = along_z(q_down, 1)
    moved = assemble((up3, down3, up4, down4))
    moved, here = lax.optimization_barrier((moved, here))
    moved = over_x(moved)

    slots = [(d, i, 0, k) for k, d in enumerate(STAY[:3]) for i in range(NX)]
    slots += [(d, i, 0, k) for k, d in enumerate(STAY[3:]) for i in range(NX)]
    slots += [(2, i, -1, 0) for i in range(NX)]
    slots += [(-2, i, 1, 1) for i in range(NX)]
    slots += [(2, i, -2, 0) for i in range(NX)]
    slots = jnp.array(slots, jnp.int32)
    last = jnp.arange(slots.shape[0]) >= slots.shape[0] - NX
    turn = jnp.where(last & (x >= 2), -1, 1)
    slot_question = (z + slots[:, 0] * turn) % NZ
    slot_owner = slots[:, 1] * NZ + (z + slots[:, 2] * turn) % NZ
    base = per_device * jnp.where(turn < 0, 1, slots[:, 3])
    column = lax.dynamic_index_in_dim(owners.reshape(NX, NZ, -1), x, 0, keepdims=False)
    number = jnp.arange(column.shape[1], dtype=jnp.int32) // TOPP + 1
    hit = (slot_question[:, None, None] == jnp.arange(NZ)[None, :, None]) & (
        slot_owner[:, None, None] == column[None, :, :]
    )
    tags = jnp.sum(jnp.where(hit, number[None, None, :], 0), axis=(1, 2)) - 1
    tags = jnp.where(tags < 0, -1, tags + base)

    split = NX * stay
    itself = in_vmem(
        self_kernel,
        "itself",
        jax.ShapeDtypeStruct((per_device, HD + PACK, ROWS), jnp.bfloat16),
        q_own,
        own,
        scratch=[
            pltpu.VMEM((per_device, HD + PACK, ROWS), jnp.float32),
            pltpu.VMEM((per_device, 1, ROWS), jnp.float32),
        ],
    )
    near = attention(
        near_kernel,
        "near",
        tags[: 3 * NX],
        here,
        [q_own, q_up, q_down],
        [],
        3,
        3 * NX,
        10,
    )
    near, most, rest = lax.optimization_barrier((near, most, rest))
    near, q_up2, q_down2 = lax.optimization_barrier((near, q_up2, q_down2))
    most = lax.all_gather(most, "x", axis=1, tiled=True)
    own_part, near_up, near_down = near
    home_up = along_z(near_up, 1)
    home_down = along_z(near_down, -1)
    far = attention(
        far_kernel,
        "far",
        tags[3 * NX : split],
        here,
        [q_up2, q_down2],
        [],
        2,
        2 * NX,
        6,
    )
    far_up, far_down = attention(
        move_kernel,
        "move",
        tags[split:],
        moved,
        [q_up2, q_down2],
        far,
        2,
        3 * NX,
        400000,
    )
    far_up = along_z(far_up, 2)
    far_down = along_z(far_down, -2)
    context = in_vmem(
        last_kernel,
        "last",
        jax.ShapeDtypeStruct(queries.shape, jnp.bfloat16),
        itself,
        own_part,
        home_up,
        home_down,
        far_up,
        far_down,
    )
    core = lax.axis_index("core")
    theirs = project(context, most, rest, 1 - core, x, "theirs")
    theirs = lax.ppermute(theirs, "core", [(0, 1), (1, 0)])
    ours = project(context, most, rest, core, x, "ours")
    chip = (ours.astype(jnp.float32) + theirs.astype(jnp.float32)).astype(jnp.bfloat16)
    chips = lax.all_to_all(chip, "y", split_axis=0, concat_axis=0, tiled=True)
    return jnp.sum(chips.astype(jnp.float32), axis=0).astype(jnp.bfloat16)


def solution(mesh):
    grid = Mesh(mesh.devices.reshape(NX, NZ, NY, NC), ("x", "z", "y", "core"))
    on_pass, on_head = ("x", "z"), ("y", "core")
    in_specs = (
        P(on_pass, on_head),
        P(on_pass, on_head, None),
        P(on_pass, None, on_head, None),
        P(on_head, on_pass),
        P(),
        P(),
        P(),
    )
    out_specs = P(on_pass, on_head)
    return jax.shard_map(body, mesh=grid, in_specs=in_specs, out_specs=out_specs, check_vma=False)
```

```python
import functools
import math

import jax
import jax.numpy as jnp
from jax import lax
from jax.experimental import pallas as pl
from jax.experimental.pallas import tpu as pltpu
from jax.sharding import Mesh, PartitionSpec as P

HD = 128
GROUP = 8
LQ = 128
PLEN = 512
TOPP = 8
NX, NZ, NY, NC = 4, 8, 4, 2
ROWS = GROUP * LQ
SCALE = math.log2(math.e) / math.sqrt(HD)
NEG = -1e30
WIDTH = 1024
PACK = 16
VMEM_LIMIT = 50 << 20

STAY = (0, 1, -1, 2, -2)
MOVE = (3, -3, 4)


def request_tables(lists, passage_slot, question_slot, per_device, pass_dev):
    slot_count = question_slot.shape[0]
    slot_ids = jnp.arange(slot_count, dtype=jnp.int32)
    holder = (question_slot[None, :] == slot_ids[:, None]).astype(jnp.int32)
    chosen = jnp.sum(holder[:, :, None] * lists[None, :, :], axis=1)
    catalog = jnp.arange(passage_slot.shape[0], dtype=jnp.int32)
    picked = (chosen[:, :, None] == catalog[None, None, :]).astype(jnp.int32)
    cache_rows = jnp.sum(picked * passage_slot[None, None, :], axis=2)
    cache_rows = cache_rows.reshape(slot_count // per_device, per_device * TOPP)
    return cache_rows // pass_dev, cache_rows % pass_dev


def staged(sources, places, buffer, read_sems, write_sems):
    reads, writes = [], []
    for n, (source, place) in enumerate(zip(sources, places)):
        reads.append(pltpu.make_async_copy(source, buffer.at[n], read_sems.at[n]))
        writes.append(pltpu.make_async_copy(buffer.at[n], place, write_sems.at[n]))
    for read in reads:
        read.start()
    for read, write in zip(reads, writes):
        read.wait()
        write.start()
    for write in writes:
        write.wait()


def row_copies(rows_ref, cache_ref, *refs):
    outs, scratch = refs[:-3], refs[-3:]
    places = [out_ref.at[i] for out_ref in outs for i in range(out_ref.shape[0])]
    staged([cache_ref.at[rows_ref[n]] for n in range(len(places))], places, *scratch)


def assemble_copies(up3, down3, up4, down4, out_ref, *scratch):
    sources = [ref.at[i] for ref in (up3, down3, up4, down4) for i in range(ref.shape[0])]
    places = [out_ref.at[i, k] for k in range(3) for i in range(NX)]
    staged(sources, places, *scratch)


def assemble(parts):
    anywhere = pl.BlockSpec(memory_space=pl.ANY)
    shape, dtype = parts[0].shape[1:], parts[0].dtype
    return pl.pallas_call(
        assemble_copies,
        out_shape=jax.ShapeDtypeStruct((NX, 3) + shape, dtype),
        in_specs=[anywhere] * len(parts),
        out_specs=anywhere,
        scratch_shapes=[
            pltpu.VMEM((3 * NX,) + shape, dtype),
            pltpu.SemaphoreType.DMA((3 * NX,)),
            pltpu.SemaphoreType.DMA((3 * NX,)),
        ],
        compiler_params=pltpu.CompilerParams(vmem_limit_bytes=VMEM_LIMIT),
        name="assemble",
    )(*parts)


def take_rows(cache, rows, counts):
    anywhere = pl.BlockSpec(memory_space=pl.ANY)
    total = sum(counts)
    return pl.pallas_call(
        row_copies,
        out_shape=tuple(jax.ShapeDtypeStruct((n,) + cache.shape[1:], cache.dtype) for n in counts),
        in_specs=[pl.BlockSpec(memory_space=pltpu.SMEM), anywhere],
        out_specs=(anywhere,) * len(counts),
        scratch_shapes=[
            pltpu.VMEM((total,) + cache.shape[1:], cache.dtype),
            pltpu.SemaphoreType.DMA((total,)),
            pltpu.SemaphoreType.DMA((total,)),
        ],
        compiler_params=pltpu.CompilerParams(vmem_limit_bytes=VMEM_LIMIT),
        name="take_rows",
    )(rows, cache)


def absorb(keys, values_t, query_ref, group, cols, acc, top, causal=False):
    scores = lax.dot_general(
        keys,
        query_ref[group, cols, :],
        (((1,), (1,)), ((), ())),
        preferred_element_type=jnp.float32,
    )
    if causal:
        key = lax.broadcasted_iota(jnp.int32, scores.shape, 0)
        token = lax.broadcasted_iota(jnp.int32, scores.shape, 1)
        scores = jnp.where(key <= token, scores, NEG)
    old = top[group, :, cols]
    new = jnp.maximum(old, jnp.max(scores, axis=0, keepdims=True))
    weights = jnp.exp2((scores - new) * SCALE)
    keep = jnp.exp2((old - new) * SCALE)
    top[group, :, cols] = new
    acc[group, :, cols] = acc[group, :, cols] * keep + jnp.dot(
        values_t, weights.astype(jnp.bfloat16), preferred_element_type=jnp.float32
    )


def start(acc, top):
    acc[...] = jnp.zeros_like(acc)
    top[...] = jnp.full_like(top, NEG)


def with_ones(values):
    ones = jnp.ones((PACK, values.shape[0]), values.dtype)
    return jnp.concatenate([values.T, ones], axis=0)


def fetches(items_ref, picks, buffer, sems):
    return [
        pltpu.make_async_copy(items_ref.at[i, k], buffer.at[n], sems.at[n])
        for n, (i, k) in enumerate(picks)
    ]


def absorb_all(tag_ref, copies, buffer, query_ref, acc, top):
    for copy in copies:
        copy.wait()

    def step(i, carry):
        tag = tag_ref[i]

        @pl.when(tag >= 0)
        def _():
            keys = buffer[i, :, 0:HD]
            values_t = with_ones(buffer[i, :, HD : 2 * HD])
            for part in range(ROWS // WIDTH):
                cols = pl.ds(part * WIDTH, WIDTH)
                absorb(keys, values_t, query_ref, tag, cols, acc, top)

        return carry

    lax.fori_loop(0, len(copies), step, 0)


def pack(level):
    parts = []
    for _ in range(3):
        part = level.astype(jnp.bfloat16).astype(jnp.float32)
        parts.append(part)
        level = level - part
    parts.append(jnp.zeros((PACK - 3, level.shape[1]), jnp.float32))
    return jnp.concatenate(parts, axis=0).astype(jnp.bfloat16)


def store(out_ref, j, mixed, level):
    out_ref[j, 0:HD, :] = mixed.astype(jnp.bfloat16)
    out_ref[j, HD : HD + PACK, :] = pack(level)


def load(ref, j):
    parts = ref[j, HD : HD + PACK, :].astype(jnp.float32)
    level = parts[0:1] + parts[1:2] + parts[2:3]
    return ref[j, 0:HD, :].astype(jnp.float32), level


def state_of(group, acc, top):
    sums = jnp.maximum(acc[group, HD : HD + 1, :], 1e-30)
    return acc[group, 0:HD, :] / sums, top[group] * SCALE + jnp.log2(sums)


def merge(pairs):
    level = pairs[0][1]
    for _, other in pairs[1:]:
        level = jnp.maximum(level, other)
    shares = [jnp.exp2(l - level) for _, l in pairs]
    whole = functools.reduce(jnp.add, shares)
    mixed = functools.reduce(jnp.add, [o * s for (o, _), s in zip(pairs, shares)])
    return mixed / whole, level + jnp.log2(whole)


def queries_of(refs, query, sems):
    n = refs[0].shape[0]
    copies = [
        pltpu.make_async_copy(ref, query.at[pl.ds(k * n, n)], sems.at[k])
        for k, ref in enumerate(refs)
    ]
    for copy in copies:
        copy.start()
    return copies


def self_kernel(q_own, own, out_ref, *state):
    start(*state)
    n = q_own.shape[0]
    for j in range(n):
        rows = slice(j * LQ, (j + 1) * LQ)
        keys = own[rows, 0:HD]
        values_t = with_ones(own[rows, HD : 2 * HD])

        def head(part, carry, j=j, keys=keys, values_t=values_t):
            cols = pl.ds(pl.multiple_of(part * LQ, LQ), LQ)
            absorb(keys, values_t, q_own, j, cols, *state, causal=True)
            return carry

        lax.fori_loop(0, GROUP, head, 0)
        store(out_ref, j, *state_of(j, *state))


def near_kernel(tags, here, q0, q1, q2, o0, o1, o2, buffer, sems, query, query_sems, *state):
    arriving = queries_of((q0, q1, q2), query, query_sems)
    copies = fetches(here, [(i, k) for k in range(3) for i in range(NX)], buffer, sems)
    for copy in copies:
        copy.start()
    start(*state)
    for copy in arriving:
        copy.wait()
    absorb_all(tags, copies, buffer, query, *state)
    n = o0.shape[0]
    for k, out_ref in enumerate((o0, o1, o2)):
        for j in range(n):
            store(out_ref, j, *state_of(k * n + j, *state))


def far_kernel(tags, here, q0, q1, o_up, o_down, buffer, sems, query, query_sems, *state):
    arriving = queries_of((q0, q1), query, query_sems)
    copies = fetches(here, [(i, k) for k in (3, 4) for i in range(NX)], buffer, sems)
    for copy in copies:
        copy.start()
    start(*state)
    for copy in arriving:
        copy.wait()
    absorb_all(tags, copies, buffer, query, *state)
    n = o_up.shape[0]
    for j in range(n):
        store(o_up, j, *state_of(j, *state))
        store(o_down, j, *state_of(n + j, *state))


def move_kernel(
    tags,
    moved,
    q0,
    q1,
    so_far_up,
    so_far_down,
    o_up,
    o_down,
    buffer,
    sems,
    query,
    query_sems,
    *state,
):
    arriving = queries_of((q0, q1), query, query_sems)
    copies = fetches(moved, [(i, k) for k in range(3) for i in range(NX)], buffer, sems)
    for copy in copies:
        copy.start()
    start(*state)
    for copy in arriving:
        copy.wait()
    absorb_all(tags, copies, buffer, query, *state)
    n = o_up.shape[0]
    for j in range(n):
        store(o_up, j, *merge([state_of(j, *state), load(so_far_up, j)]))
        store(o_down, j, *merge([state_of(n + j, *state), load(so_far_down, j)]))


def attention(kernel, name, tags, items, queries, arrays, groups, slots, work):
    vmem, anywhere = pl.BlockSpec(memory_space=pltpu.VMEM), pl.BlockSpec(memory_space=pl.ANY)
    n = queries[0].shape[0]
    return pl.pallas_call(
        kernel,
        out_shape=(jax.ShapeDtypeStruct((n, HD + PACK, ROWS), jnp.bfloat16),) * groups,
        in_specs=[pl.BlockSpec(memory_space=pltpu.SMEM), anywhere]
        + [anywhere] * len(queries)
        + [vmem] * len(arrays),
        out_specs=(vmem,) * groups,
        scratch_shapes=[
            pltpu.VMEM((slots, PLEN, 2 * HD), jnp.bfloat16),
            pltpu.SemaphoreType.DMA((slots,)),
            pltpu.VMEM((groups * n, ROWS, HD), jnp.bfloat16),
            pltpu.SemaphoreType.DMA((groups,)),
            pltpu.VMEM((groups * n, HD + PACK, ROWS), jnp.float32),
            pltpu.VMEM((groups * n, 1, ROWS), jnp.float32),
        ],
        compiler_params=pltpu.CompilerParams(vmem_limit_bytes=VMEM_LIMIT),
        cost_estimate=pl.CostEstimate(
            flops=work * ROWS * PLEN,
            bytes_accessed=work * PLEN,
            transcendentals=0,
        ),
        name=name,
    )(tags, items, *queries, *arrays)


def last_kernel(*refs):
    parts, out_ref = refs[:-1], refs[-1]
    for j in range(parts[0].shape[0]):
        mixed, _ = merge([load(part, j) for part in parts])
        for head in range(GROUP):
            cols = slice(head * LQ, (head + 1) * LQ)
            out_ref[j * LQ : (j + 1) * LQ, head * HD : (head + 1) * HD] = mixed[:, cols].T.astype(
                jnp.bfloat16
            )


def project_kernel(place, context_ref, most_ref, rest_ref, out_ref):
    cut = most_ref.shape[0]
    products = jnp.dot(
        context_ref[:, :cut], most_ref[...], preferred_element_type=jnp.float32
    ) + jnp.dot(context_ref[:, cut:], rest_ref[0], preferred_element_type=jnp.float32)
    out_ref[0] = products.astype(jnp.bfloat16)


def project(context, most, rest, core, x, name):
    width = most.shape[1] // (NY * NC)
    return pl.pallas_call(
        project_kernel,
        out_shape=jax.ShapeDtypeStruct((NY, context.shape[0], width), jnp.bfloat16),
        grid_spec=pltpu.PrefetchScalarGridSpec(
            num_scalar_prefetch=1,
            grid=(NY,),
            in_specs=[
                pl.BlockSpec(context.shape, lambda i, place: (0, 0)),
                pl.BlockSpec((most.shape[0], width), lambda i, place: (0, NC * i + place[0])),
                pl.BlockSpec(
                    (1, rest.shape[1], width),
                    lambda i, place: (lax.rem(i + NX - place[1], NX), 0, place[0]),
                ),
            ],
            out_specs=pl.BlockSpec((1, context.shape[0], width), lambda i, place: (i, 0, 0)),
        ),
        compiler_params=pltpu.CompilerParams(vmem_limit_bytes=VMEM_LIMIT),
        cost_estimate=pl.CostEstimate(
            flops=2 * context.shape[0] * context.shape[1] * width * NY,
            bytes_accessed=context.shape[1] * width * NY * 2,
            transcendentals=0,
        ),
        name=name,
    )(jnp.stack([core, x]), context, most, rest)


def in_vmem(kernel, name, out, *arrays, scratch=()):
    vmem = pl.BlockSpec(memory_space=pltpu.VMEM)
    return pl.pallas_call(
        kernel,
        out_shape=out,
        in_specs=[vmem] * len(arrays),
        out_specs=jax.tree.map(lambda _: vmem, out),
        scratch_shapes=scratch,
        compiler_params=pltpu.CompilerParams(vmem_limit_bytes=VMEM_LIMIT),
        name=name,
    )(*arrays)


def along_z(array, shift):
    return lax.ppermute(array, "z", [(i, (i + shift) % NZ) for i in range(NZ)])


def along_x(array, shift):
    return lax.ppermute(array, "x", [(i, (i + shift) % NX) for i in range(NX)])


def over_x(items):
    return lax.all_to_all(items, "x", split_axis=0, concat_axis=0, tiled=True)


def body(queries, own_kv, passage_cache, out_weight, lists, passage_slot, question_slot):
    x, z = lax.axis_index("x"), lax.axis_index("z")
    per_device = queries.shape[0] // LQ
    pass_dev = passage_cache.shape[0]
    cache = passage_cache.reshape(pass_dev, PLEN, 2 * HD)
    own = own_kv.reshape(per_device * LQ, 2 * HD)

    q_own = queries.reshape(per_device, LQ, GROUP, HD).transpose(0, 2, 1, 3)
    q_own = q_own.reshape(per_device, ROWS, HD)
    owners, local_rows = request_tables(lists, passage_slot, question_slot, per_device, pass_dev)
    mine = jnp.sum(jnp.where(owners == x * NZ + z, local_rows, 0), axis=1).reshape(NX, NZ)
    target_z = (z + jnp.array(STAY + MOVE, jnp.int32)) % NZ
    rows = jnp.sum(
        jnp.where(target_z[None, :, None] == jnp.arange(NZ)[None, None, :], mine[:, None, :], 0),
        axis=2,
    )
    stay = len(STAY)
    moving = take_rows(cache, rows[:, stay:].T.reshape(-1), (4, 4, 2, 2))
    moving, staying = lax.optimization_barrier((moving, rows[:, :stay].reshape(-1)))
    (here,) = take_rows(cache, staying, (NX * stay,))
    q_up = along_z(q_own, -1)
    q_down = along_z(q_own, 1)
    cut = out_weight.shape[0] * 3 // 4
    most = lax.all_gather(out_weight[:cut], "z", axis=1, tiled=True)
    rest = out_weight[cut:]
    rest = jnp.stack([rest] + [along_x(rest, -distance) for distance in range(1, NX)])
    here, q_up, q_down, rest = lax.optimization_barrier((here, q_up, q_down, rest))
    rest = lax.all_gather(rest, "z", axis=2, tiled=True)
    here = over_x(here.reshape(NX, stay, PLEN, 2 * HD))
    up3, down3, up4, down4 = moving
    up3 = along_z(up3, 1)
    down3 = along_z(down3, -1)
    up4 = along_z(up4, 2)
    down4 = along_z(down4, -2)
    up3, down3, up4, down4, q_up, q_down = lax.optimization_barrier(
        (up3, down3, up4, down4, q_up, q_down)
    )
    q_up2 = along_z(q_up, -1)
    q_down2 = along_z(q_down, 1)
    moved = assemble((up3, down3, up4, down4))
    moved, here = lax.optimization_barrier((moved, here))
    moved = over_x(moved)

    slots = [(d, i, 0, k) for k, d in enumerate(STAY[:3]) for i in range(NX)]
    slots += [(d, i, 0, k) for k, d in enumerate(STAY[3:]) for i in range(NX)]
    slots += [(2, i, -1, 0) for i in range(NX)]
    slots += [(-2, i, 1, 1) for i in range(NX)]
    slots += [(2, i, -2, 0) for i in range(NX)]
    slots = jnp.array(slots, jnp.int32)
    last = jnp.arange(slots.shape[0]) >= slots.shape[0] - NX
    turn = jnp.where(last & (x >= 2), -1, 1)
    slot_question = (z + slots[:, 0] * turn) % NZ
    slot_owner = slots[:, 1] * NZ + (z + slots[:, 2] * turn) % NZ
    base = per_device * jnp.where(turn < 0, 1, slots[:, 3])
    column = lax.dynamic_index_in_dim(owners.reshape(NX, NZ, -1), x, 0, keepdims=False)
    number = jnp.arange(column.shape[1], dtype=jnp.int32) // TOPP + 1
    hit = (slot_question[:, None, None] == jnp.arange(NZ)[None, :, None]) & (
        slot_owner[:, None, None] == column[None, :, :]
    )
    tags = jnp.sum(jnp.where(hit, number[None, None, :], 0), axis=(1, 2)) - 1
    tags = jnp.where(tags < 0, -1, tags + base)

    split = NX * stay
    itself = in_vmem(
        self_kernel,
        "itself",
        jax.ShapeDtypeStruct((per_device, HD + PACK, ROWS), jnp.bfloat16),
        q_own,
        own,
        scratch=[
            pltpu.VMEM((per_device, HD + PACK, ROWS), jnp.float32),
            pltpu.VMEM((per_device, 1, ROWS), jnp.float32),
        ],
    )
    near = attention(
        near_kernel,
        "near",
        tags[: 3 * NX],
        here,
        [q_own, q_up, q_down],
        [],
        3,
        3 * NX,
        10,
    )
    near, q_up2, q_down2 = lax.optimization_barrier((near, q_up2, q_down2))
    own_part, near_up, near_down = near
    home_up = along_z(near_up, 1)
    home_down = along_z(near_down, -1)
    far = attention(
        far_kernel,
        "far",
        tags[3 * NX : split],
        here,
        [q_up2, q_down2],
        [],
        2,
        2 * NX,
        6,
    )
    far, most, rest = lax.optimization_barrier((far, most, rest))
    most = lax.all_gather(most, "x", axis=1, tiled=True)
    far_up, far_down = attention(
        move_kernel,
        "move",
        tags[split:],
        moved,
        [q_up2, q_down2],
        far,
        2,
        3 * NX,
        400000,
    )
    far_up = along_z(far_up, 2)
    far_down = along_z(far_down, -2)
    context = in_vmem(
        last_kernel,
        "last",
        jax.ShapeDtypeStruct(queries.shape, jnp.bfloat16),
        itself,
        own_part,
        home_up,
        home_down,
        far_up,
        far_down,
    )
    core = lax.axis_index("core")
    theirs = project(context, most, rest, 1 - core, x, "theirs")
    theirs = lax.ppermute(theirs, "core", [(0, 1), (1, 0)])
    ours = project(context, most, rest, core, x, "ours")
    chip = (ours.astype(jnp.float32) + theirs.astype(jnp.float32)).astype(jnp.bfloat16)
    chips = lax.all_to_all(chip, "y", split_axis=0, concat_axis=0, tiled=True)
    return jnp.sum(chips.astype(jnp.float32), axis=0).astype(jnp.bfloat16)


def solution(mesh):
    grid = Mesh(mesh.devices.reshape(NX, NZ, NY, NC), ("x", "z", "y", "core"))
    on_pass, on_head = ("x", "z"), ("y", "core")
    in_specs = (
        P(on_pass, on_head),
        P(on_pass, on_head, None),
        P(on_pass, None, on_head, None),
        P(on_head, on_pass),
        P(),
        P(),
        P(),
    )
    out_specs = P(on_pass, on_head)
    return jax.shard_map(body, mesh=grid, in_specs=in_specs, out_specs=out_specs, check_vma=False)
```

```python
import functools
import math

import jax
import jax.numpy as jnp
from jax import lax
from jax.experimental import pallas as pl
from jax.experimental.pallas import tpu as pltpu
from jax.sharding import Mesh, PartitionSpec as P

HD = 128
GROUP = 8
LQ = 128
PLEN = 512
TOPP = 8
NX, NZ, NY, NC = 4, 8, 4, 2
ROWS = GROUP * LQ
SCALE = math.log2(math.e) / math.sqrt(HD)
NEG = -1e30
WIDTH = 1024
PACK = 16
VMEM_LIMIT = 50 << 20

STAY = (0, 1, -1, 2, -2)
MOVE = (3, -3, 4)


def request_tables(lists, passage_slot, question_slot, per_device, pass_dev):
    slot_count = question_slot.shape[0]
    slot_ids = jnp.arange(slot_count, dtype=jnp.int32)
    holder = (question_slot[None, :] == slot_ids[:, None]).astype(jnp.int32)
    chosen = jnp.sum(holder[:, :, None] * lists[None, :, :], axis=1)
    catalog = jnp.arange(passage_slot.shape[0], dtype=jnp.int32)
    picked = (chosen[:, :, None] == catalog[None, None, :]).astype(jnp.int32)
    cache_rows = jnp.sum(picked * passage_slot[None, None, :], axis=2)
    cache_rows = cache_rows.reshape(slot_count // per_device, per_device * TOPP)
    return cache_rows // pass_dev, cache_rows % pass_dev


def staged(sources, places, buffer, read_sems, write_sems):
    reads, writes = [], []
    for n, (source, place) in enumerate(zip(sources, places)):
        reads.append(pltpu.make_async_copy(source, buffer.at[n], read_sems.at[n]))
        writes.append(pltpu.make_async_copy(buffer.at[n], place, write_sems.at[n]))
    for read in reads:
        read.start()
    for read, write in zip(reads, writes):
        read.wait()
        write.start()
    for write in writes:
        write.wait()


def row_copies(rows_ref, cache_ref, *refs):
    outs, scratch = refs[:-3], refs[-3:]
    places = [out_ref.at[i] for out_ref in outs for i in range(out_ref.shape[0])]
    staged([cache_ref.at[rows_ref[n]] for n in range(len(places))], places, *scratch)


def assemble_copies(up3, down3, up4, down4, out_ref, *scratch):
    sources = [ref.at[i] for ref in (up3, down3, up4, down4) for i in range(ref.shape[0])]
    places = [out_ref.at[i, k] for k in range(3) for i in range(NX)]
    staged(sources, places, *scratch)


def assemble(parts):
    anywhere = pl.BlockSpec(memory_space=pl.ANY)
    shape, dtype = parts[0].shape[1:], parts[0].dtype
    return pl.pallas_call(
        assemble_copies,
        out_shape=jax.ShapeDtypeStruct((NX, 3) + shape, dtype),
        in_specs=[anywhere] * len(parts),
        out_specs=anywhere,
        scratch_shapes=[
            pltpu.VMEM((3 * NX,) + shape, dtype),
            pltpu.SemaphoreType.DMA((3 * NX,)),
            pltpu.SemaphoreType.DMA((3 * NX,)),
        ],
        compiler_params=pltpu.CompilerParams(vmem_limit_bytes=VMEM_LIMIT),
        name="assemble",
    )(*parts)


def take_rows(cache, rows, counts):
    anywhere = pl.BlockSpec(memory_space=pl.ANY)
    total = sum(counts)
    return pl.pallas_call(
        row_copies,
        out_shape=tuple(jax.ShapeDtypeStruct((n,) + cache.shape[1:], cache.dtype) for n in counts),
        in_specs=[pl.BlockSpec(memory_space=pltpu.SMEM), anywhere],
        out_specs=(anywhere,) * len(counts),
        scratch_shapes=[
            pltpu.VMEM((total,) + cache.shape[1:], cache.dtype),
            pltpu.SemaphoreType.DMA((total,)),
            pltpu.SemaphoreType.DMA((total,)),
        ],
        compiler_params=pltpu.CompilerParams(vmem_limit_bytes=VMEM_LIMIT),
        name="take_rows",
    )(rows, cache)


def absorb(keys, values_t, query_ref, group, cols, acc, top, causal=False):
    scores = lax.dot_general(
        keys,
        query_ref[group, cols, :],
        (((1,), (1,)), ((), ())),
        preferred_element_type=jnp.float32,
    )
    if causal:
        key = lax.broadcasted_iota(jnp.int32, scores.shape, 0)
        token = lax.broadcasted_iota(jnp.int32, scores.shape, 1)
        scores = jnp.where(key <= token, scores, NEG)
    old = top[group, :, cols]
    new = jnp.maximum(old, jnp.max(scores, axis=0, keepdims=True))
    weights = jnp.exp2((scores - new) * SCALE)
    keep = jnp.exp2((old - new) * SCALE)
    top[group, :, cols] = new
    acc[group, :, cols] = acc[group, :, cols] * keep + jnp.dot(
        values_t, weights.astype(jnp.bfloat16), preferred_element_type=jnp.float32
    )


def start(acc, top):
    acc[...] = jnp.zeros_like(acc)
    top[...] = jnp.full_like(top, NEG)


def with_ones(values):
    ones = jnp.ones((PACK, values.shape[0]), values.dtype)
    return jnp.concatenate([values.T, ones], axis=0)


def fetches(items_ref, picks, buffer, sems):
    return [
        pltpu.make_async_copy(items_ref.at[i, k], buffer.at[n], sems.at[n])
        for n, (i, k) in enumerate(picks)
    ]


def absorb_all(tag_ref, copies, buffer, query_ref, acc, top):
    for copy in copies:
        copy.wait()

    def step(i, carry):
        tag = tag_ref[i]

        @pl.when(tag >= 0)
        def _():
            keys = buffer[i, :, 0:HD]
            values_t = with_ones(buffer[i, :, HD : 2 * HD])
            for part in range(ROWS // WIDTH):
                cols = pl.ds(part * WIDTH, WIDTH)
                absorb(keys, values_t, query_ref, tag, cols, acc, top)

        return carry

    lax.fori_loop(0, len(copies), step, 0)


def pack(level):
    parts = []
    for _ in range(3):
        part = level.astype(jnp.bfloat16).astype(jnp.float32)
        parts.append(part)
        level = level - part
    parts.append(jnp.zeros((PACK - 3, level.shape[1]), jnp.float32))
    return jnp.concatenate(parts, axis=0).astype(jnp.bfloat16)


def store(out_ref, j, mixed, level):
    out_ref[j, 0:HD, :] = mixed.astype(jnp.bfloat16)
    out_ref[j, HD : HD + PACK, :] = pack(level)


def load(ref, j):
    parts = ref[j, HD : HD + PACK, :].astype(jnp.float32)
    level = parts[0:1] + parts[1:2] + parts[2:3]
    return ref[j, 0:HD, :].astype(jnp.float32), level


def state_of(group, acc, top):
    sums = jnp.maximum(acc[group, HD : HD + 1, :], 1e-30)
    return acc[group, 0:HD, :] / sums, top[group] * SCALE + jnp.log2(sums)


def merge(pairs):
    level = pairs[0][1]
    for _, other in pairs[1:]:
        level = jnp.maximum(level, other)
    shares = [jnp.exp2(l - level) for _, l in pairs]
    whole = functools.reduce(jnp.add, shares)
    mixed = functools.reduce(jnp.add, [o * s for (o, _), s in zip(pairs, shares)])
    return mixed / whole, level + jnp.log2(whole)


def queries_of(refs, query, sems):
    n = refs[0].shape[0]
    copies = [
        pltpu.make_async_copy(ref, query.at[pl.ds(k * n, n)], sems.at[k])
        for k, ref in enumerate(refs)
    ]
    for copy in copies:
        copy.start()
    return copies


def self_kernel(q_own, own, out_ref, *state):
    start(*state)
    n = q_own.shape[0]
    for j in range(n):
        rows = slice(j * LQ, (j + 1) * LQ)
        keys = own[rows, 0:HD]
        values_t = with_ones(own[rows, HD : 2 * HD])

        def head(part, carry, j=j, keys=keys, values_t=values_t):
            cols = pl.ds(pl.multiple_of(part * LQ, LQ), LQ)
            absorb(keys, values_t, q_own, j, cols, *state, causal=True)
            return carry

        lax.fori_loop(0, GROUP, head, 0)
        store(out_ref, j, *state_of(j, *state))


def near_kernel(tags, here, q0, q1, q2, o0, o1, o2, buffer, sems, query, query_sems, *state):
    arriving = queries_of((q0, q1, q2), query, query_sems)
    copies = fetches(here, [(i, k) for k in range(3) for i in range(NX)], buffer, sems)
    for copy in copies:
        copy.start()
    start(*state)
    for copy in arriving:
        copy.wait()
    absorb_all(tags, copies, buffer, query, *state)
    n = o0.shape[0]
    for k, out_ref in enumerate((o0, o1, o2)):
        for j in range(n):
            store(out_ref, j, *state_of(k * n + j, *state))


def far_kernel(tags, here, q0, q1, o_up, o_down, buffer, sems, query, query_sems, *state):
    arriving = queries_of((q0, q1), query, query_sems)
    copies = fetches(here, [(i, k) for k in (3, 4) for i in range(NX)], buffer, sems)
    for copy in copies:
        copy.start()
    start(*state)
    for copy in arriving:
        copy.wait()
    absorb_all(tags, copies, buffer, query, *state)
    n = o_up.shape[0]
    for j in range(n):
        store(o_up, j, *state_of(j, *state))
        store(o_down, j, *state_of(n + j, *state))


def move_kernel(
    tags,
    moved,
    q0,
    q1,
    so_far_up,
    so_far_down,
    o_up,
    o_down,
    buffer,
    sems,
    query,
    query_sems,
    *state,
):
    arriving = queries_of((q0, q1), query, query_sems)
    copies = fetches(moved, [(i, k) for k in range(3) for i in range(NX)], buffer, sems)
    for copy in copies:
        copy.start()
    start(*state)
    for copy in arriving:
        copy.wait()
    absorb_all(tags, copies, buffer, query, *state)
    n = o_up.shape[0]
    for j in range(n):
        store(o_up, j, *merge([state_of(j, *state), load(so_far_up, j)]))
        store(o_down, j, *merge([state_of(n + j, *state), load(so_far_down, j)]))


def attention(kernel, name, tags, items, queries, arrays, groups, slots, work):
    vmem, anywhere = pl.BlockSpec(memory_space=pltpu.VMEM), pl.BlockSpec(memory_space=pl.ANY)
    n = queries[0].shape[0]
    return pl.pallas_call(
        kernel,
        out_shape=(jax.ShapeDtypeStruct((n, HD + PACK, ROWS), jnp.bfloat16),) * groups,
        in_specs=[pl.BlockSpec(memory_space=pltpu.SMEM), anywhere]
        + [anywhere] * len(queries)
        + [vmem] * len(arrays),
        out_specs=(vmem,) * groups,
        scratch_shapes=[
            pltpu.VMEM((slots, PLEN, 2 * HD), jnp.bfloat16),
            pltpu.SemaphoreType.DMA((slots,)),
            pltpu.VMEM((groups * n, ROWS, HD), jnp.bfloat16),
            pltpu.SemaphoreType.DMA((groups,)),
            pltpu.VMEM((groups * n, HD + PACK, ROWS), jnp.float32),
            pltpu.VMEM((groups * n, 1, ROWS), jnp.float32),
        ],
        compiler_params=pltpu.CompilerParams(vmem_limit_bytes=VMEM_LIMIT),
        cost_estimate=pl.CostEstimate(
            flops=work * ROWS * PLEN,
            bytes_accessed=work * PLEN,
            transcendentals=0,
        ),
        name=name,
    )(tags, items, *queries, *arrays)


def last_kernel(*refs):
    parts, out_ref = refs[:-1], refs[-1]
    for j in range(parts[0].shape[0]):
        mixed, _ = merge([load(part, j) for part in parts])
        for head in range(GROUP):
            cols = slice(head * LQ, (head + 1) * LQ)
            out_ref[j * LQ : (j + 1) * LQ, head * HD : (head + 1) * HD] = mixed[:, cols].T.astype(
                jnp.bfloat16
            )


def project_kernel(place, context_ref, most_ref, rest_ref, out_ref):
    cut = most_ref.shape[0]
    products = jnp.dot(
        context_ref[:, :cut], most_ref[...], preferred_element_type=jnp.float32
    ) + jnp.dot(context_ref[:, cut:], rest_ref[0], preferred_element_type=jnp.float32)
    out_ref[0] = products.astype(jnp.bfloat16)


def project(context, most, rest, core, x, name):
    width = most.shape[1] // (NY * NC)
    return pl.pallas_call(
        project_kernel,
        out_shape=jax.ShapeDtypeStruct((NY, context.shape[0], width), jnp.bfloat16),
        grid_spec=pltpu.PrefetchScalarGridSpec(
            num_scalar_prefetch=1,
            grid=(NY,),
            in_specs=[
                pl.BlockSpec(context.shape, lambda i, place: (0, 0)),
                pl.BlockSpec((most.shape[0], width), lambda i, place: (0, NC * i + place[0])),
                pl.BlockSpec(
                    (1, rest.shape[1], width),
                    lambda i, place: (lax.rem(i + NX - place[1], NX), 0, place[0]),
                ),
            ],
            out_specs=pl.BlockSpec((1, context.shape[0], width), lambda i, place: (i, 0, 0)),
        ),
        compiler_params=pltpu.CompilerParams(vmem_limit_bytes=VMEM_LIMIT),
        cost_estimate=pl.CostEstimate(
            flops=2 * context.shape[0] * context.shape[1] * width * NY,
            bytes_accessed=context.shape[1] * width * NY * 2,
            transcendentals=0,
        ),
        name=name,
    )(jnp.stack([core, x]), context, most, rest)


def in_vmem(kernel, name, out, *arrays, scratch=()):
    vmem = pl.BlockSpec(memory_space=pltpu.VMEM)
    return pl.pallas_call(
        kernel,
        out_shape=out,
        in_specs=[vmem] * len(arrays),
        out_specs=jax.tree.map(lambda _: vmem, out),
        scratch_shapes=scratch,
        compiler_params=pltpu.CompilerParams(vmem_limit_bytes=VMEM_LIMIT),
        name=name,
    )(*arrays)


def along_z(array, shift):
    return lax.ppermute(array, "z", [(i, (i + shift) % NZ) for i in range(NZ)])


def along_x(array, shift):
    return lax.ppermute(array, "x", [(i, (i + shift) % NX) for i in range(NX)])


def over_x(items):
    return lax.all_to_all(items, "x", split_axis=0, concat_axis=0, tiled=True)


def body(queries, own_kv, passage_cache, out_weight, lists, passage_slot, question_slot):
    x, z = lax.axis_index("x"), lax.axis_index("z")
    per_device = queries.shape[0] // LQ
    pass_dev = passage_cache.shape[0]
    cache = passage_cache.reshape(pass_dev, PLEN, 2 * HD)
    own = own_kv.reshape(per_device * LQ, 2 * HD)

    q_own = queries.reshape(per_device, LQ, GROUP, HD).transpose(0, 2, 1, 3)
    q_own = q_own.reshape(per_device, ROWS, HD)
    owners, local_rows = request_tables(lists, passage_slot, question_slot, per_device, pass_dev)
    mine = jnp.sum(jnp.where(owners == x * NZ + z, local_rows, 0), axis=1).reshape(NX, NZ)
    target_z = (z + jnp.array(STAY + MOVE, jnp.int32)) % NZ
    rows = jnp.sum(
        jnp.where(target_z[None, :, None] == jnp.arange(NZ)[None, None, :], mine[:, None, :], 0),
        axis=2,
    )
    stay = len(STAY)
    moving = take_rows(cache, rows[:, stay:].T.reshape(-1), (4, 4, 2, 2))
    moving, staying = lax.optimization_barrier((moving, rows[:, :stay].reshape(-1)))
    (here,) = take_rows(cache, staying, (NX * stay,))
    q_up = along_z(q_own, -1)
    q_down = along_z(q_own, 1)
    cut = out_weight.shape[0] * 7 // 8
    most = lax.all_gather(out_weight[:cut], "z", axis=1, tiled=True)
    rest = out_weight[cut:]
    rest = jnp.stack([rest] + [along_x(rest, -distance) for distance in range(1, NX)])
    here, q_up, q_down, rest = lax.optimization_barrier((here, q_up, q_down, rest))
    rest = lax.all_gather(rest, "z", axis=2, tiled=True)
    here = over_x(here.reshape(NX, stay, PLEN, 2 * HD))
    up3, down3, up4, down4 = moving
    up3 = along_z(up3, 1)
    down3 = along_z(down3, -1)
    up4 = along_z(up4, 2)
    down4 = along_z(down4, -2)
    up3, down3, up4, down4, q_up, q_down = lax.optimization_barrier(
        (up3, down3, up4, down4, q_up, q_down)
    )
    q_up2 = along_z(q_up, -1)
    q_down2 = along_z(q_down, 1)
    moved = assemble((up3, down3, up4, down4))
    moved, here = lax.optimization_barrier((moved, here))
    moved = over_x(moved)

    slots = [(d, i, 0, k) for k, d in enumerate(STAY[:3]) for i in range(NX)]
    slots += [(d, i, 0, k) for k, d in enumerate(STAY[3:]) for i in range(NX)]
    slots += [(2, i, -1, 0) for i in range(NX)]
    slots += [(-2, i, 1, 1) for i in range(NX)]
    slots += [(2, i, -2, 0) for i in range(NX)]
    slots = jnp.array(slots, jnp.int32)
    last = jnp.arange(slots.shape[0]) >= slots.shape[0] - NX
    turn = jnp.where(last & (x >= 2), -1, 1)
    slot_question = (z + slots[:, 0] * turn) % NZ
    slot_owner = slots[:, 1] * NZ + (z + slots[:, 2] * turn) % NZ
    base = per_device * jnp.where(turn < 0, 1, slots[:, 3])
    column = lax.dynamic_index_in_dim(owners.reshape(NX, NZ, -1), x, 0, keepdims=False)
    number = jnp.arange(column.shape[1], dtype=jnp.int32) // TOPP + 1
    hit = (slot_question[:, None, None] == jnp.arange(NZ)[None, :, None]) & (
        slot_owner[:, None, None] == column[None, :, :]
    )
    tags = jnp.sum(jnp.where(hit, number[None, None, :], 0), axis=(1, 2)) - 1
    tags = jnp.where(tags < 0, -1, tags + base)

    split = NX * stay
    itself = in_vmem(
        self_kernel,
        "itself",
        jax.ShapeDtypeStruct((per_device, HD + PACK, ROWS), jnp.bfloat16),
        q_own,
        own,
        scratch=[
            pltpu.VMEM((per_device, HD + PACK, ROWS), jnp.float32),
            pltpu.VMEM((per_device, 1, ROWS), jnp.float32),
        ],
    )
    near = attention(
        near_kernel,
        "near",
        tags[: 3 * NX],
        here,
        [q_own, q_up, q_down],
        [],
        3,
        3 * NX,
        10,
    )
    near, most, rest = lax.optimization_barrier((near, most, rest))
    near, q_up2, q_down2 = lax.optimization_barrier((near, q_up2, q_down2))
    most = lax.all_gather(most, "x", axis=1, tiled=True)
    own_part, near_up, near_down = near
    home_up = along_z(near_up, 1)
    home_down = along_z(near_down, -1)
    far = attention(
        far_kernel,
        "far",
        tags[3 * NX : split],
        here,
        [q_up2, q_down2],
        [],
        2,
        2 * NX,
        6,
    )
    far_up, far_down = attention(
        move_kernel,
        "move",
        tags[split:],
        moved,
        [q_up2, q_down2],
        far,
        2,
        3 * NX,
        400000,
    )
    far_up = along_z(far_up, 2)
    far_down = along_z(far_down, -2)
    context = in_vmem(
        last_kernel,
        "last",
        jax.ShapeDtypeStruct(queries.shape, jnp.bfloat16),
        itself,
        own_part,
        home_up,
        home_down,
        far_up,
        far_down,
    )
    core = lax.axis_index("core")
    theirs = project(context, most, rest, 1 - core, x, "theirs")
    theirs = lax.ppermute(theirs, "core", [(0, 1), (1, 0)])
    ours = project(context, most, rest, core, x, "ours")
    chip = (ours.astype(jnp.float32) + theirs.astype(jnp.float32)).astype(jnp.bfloat16)
    chips = lax.all_to_all(chip, "y", split_axis=0, concat_axis=0, tiled=True)
    return jnp.sum(chips.astype(jnp.float32), axis=0).astype(jnp.bfloat16)


def solution(mesh):
    grid = Mesh(mesh.devices.reshape(NX, NZ, NY, NC), ("x", "z", "y", "core"))
    on_pass, on_head = ("x", "z"), ("y", "core")
    in_specs = (
        P(on_pass, on_head),
        P(on_pass, on_head, None),
        P(on_pass, None, on_head, None),
        P(on_head, on_pass),
        P(),
        P(),
        P(),
    )
    out_specs = P(on_pass, on_head)
    return jax.shard_map(body, mesh=grid, in_specs=in_specs, out_specs=out_specs, check_vma=False)
```
